32 devices in a mesh: parts: 2 (over x), wall: 16 (over z, y, core).
Axes of the slice: x: 2, y: 2, z: 4, core: 2. Of those that a mesh axis runs over, the one named last changes fastest.
Arguments:
- displacement: float32 [3, 524288], P(None, ('parts', 'wall')), parts along dimension 1, may hold values from -6 to 6
- velocity: float32 [3, 524288], P(None, ('parts', 'wall')), parts along dimension 1, may hold values from -6 to 6
- send_list: int32 [32, 16, 64], P(('parts', 'wall')), parts along dimension 0, may hold values from 0 to 16383, as said below
- arrive_list: int32 [32, 16, 64], P(('parts', 'wall')), parts along dimension 0, may hold values from 0 to 16383, as said below
- recv_count: int32 [32, 16], P(('parts', 'wall')), parts along dimension 0, may hold values from 0 to 64, as said below
- horizon_blocks: int32 [4096, 27], P(('parts', 'wall')), parts along dimension 0, may hold values from 0 to 2047, as said below
- bond_intact: int32 [4096, 27, 128], P(('parts', 'wall')), parts along dimension 0, may hold values 0 or 1
- modulus: float32 [524288], P(('parts', 'wall')), parts along dimension 0, may hold values from 0.5 to 2
- bond_weight: bfloat16 [27, 128, 128], replicated, may hold values from -0.109375 to 0.109375
Outputs:
- new_displacement: float32 [3, 524288], P(None, ('parts', 'wall')), parts along dimension 1
- new_velocity: float32 [3, 524288], P(None, ('parts', 'wall')), parts along dimension 1
The draws below stay inside these ranges and needn't reach their ends.
There are 2 independent parts, one for each index of `parts`. The reference program is written for one: setup_inputs(seed, part) draws one part's arguments, and reference() takes and returns one part's arrays. A program takes and returns all parts, laid end to end along the dimension named above; an argument that names none is the same for every part. Nothing has to cross between parts.
Inputs may be any that keep to these rules, and one draw needn't show every extreme that they name: For c < recv_count[d, s], send_list[s, d, c] is the local index on owner s of a node handed to owner d; the nodes that s hands away are distinct, and every owner hands away as many nodes as it receives. Other slots hold 0. For c < recv_count[d, s], arrive_list[d, s, c] is the local index on owner d where the c-th node from s lands; over all s and c these are exactly the local indices that d hands away, each once. Other slots hold 0. recv_count[d, s] is 0 for s = d and at least 1 otherwise; at most 64 nodes go from one owner to one other owner, and that many do on some pair in every draw. `horizon_blocks`: block b lies in layer b // 64; every block listed for b lies in the same layer, the layer before or the layer after.
All inputs are finite; a program needn't handle non-finite values. No bound on the sum of `bond_intact` on one device may be relied on, other than what follows from the above.
Results may differ from the reference program's by a relative error of at most 0.0011.
Values may be sent and summed in bfloat16 or wider, within the bound.
A program may use at most 64 MiB of HBM per device.

```python
import math
import jax
import jax.numpy as jnp
from jax import lax

BLK = 128
NNZ = 27
SUBSTEPS = 2
LAYER = 64
CAP = 64
NB_DEV = 128
NODES_DEV = 16384
NBLK = 2048
NODES = 262144
NLAYERS = 32
N_WALL = 16


def migration_plan(key):
    base_key = jax.random.fold_in(key, 7)
    key_order, key_count, key_vacate = jax.random.split(base_key, 3)
    ordering = jax.random.permutation(key_order, N_WALL).astype(jnp.int32)
    amounts = jax.random.randint(key_count, (N_WALL,), 1, CAP + 1, dtype=jnp.int32)
    amounts = amounts.at[0].set(0).at[1].set(CAP)
    starts = jnp.cumsum(amounts) - amounts
    vacate_keys = jax.random.split(key_vacate, N_WALL)

    def vacate_one(single):
        return jax.random.permutation(single, NODES_DEV)
    vacated = jax.vmap(vacate_one)(vacate_keys).astype(jnp.int32)
    offsets = (ordering[None, :] - ordering[:, None]) % N_WALL
    slot_ids = jnp.arange(CAP, dtype=jnp.int32)
    live_slot = slot_ids[None, None, :] < amounts[offsets][:, :, None]
    spot_ids = jnp.minimum(starts[offsets][:, :, None] + slot_ids[None, None, :], NODES_DEV - 1)
    owners = jnp.arange(N_WALL, dtype=jnp.int32)[:, None, None]
    sent_ids = jnp.where(live_slot, vacated[owners, spot_ids], 0).astype(jnp.int32)
    spot_turned = jnp.transpose(spot_ids, (1, 0, 2))
    live_turned = jnp.transpose(live_slot, (1, 0, 2))
    arrived = jnp.where(live_turned, vacated[owners, spot_turned], 0).astype(jnp.int32)
    received = amounts[jnp.transpose(offsets)].astype(jnp.int32)
    return (sent_ids, arrived, received)


def draw_send_list(key, part):
    return migration_plan(key)[0]


def draw_arrive_list(key, part):
    return migration_plan(key)[1]


def draw_recv_count(key, part):
    return migration_plan(key)[2]


def draw_horizon_blocks(key, part):
    key_layer, key_place = jax.random.split(jax.random.fold_in(key, 11))
    layer_ids = jnp.arange(NBLK, dtype=jnp.int32) // LAYER
    layer_step = jax.random.randint(key_layer, (NBLK, NNZ), -1, 2, dtype=jnp.int32)
    target_layer = jnp.clip(layer_ids[:, None] + layer_step, 0, NLAYERS - 1)
    position_in = jax.random.randint(key_place, (NBLK, NNZ), 0, LAYER, dtype=jnp.int32)
    return (target_layer * LAYER + position_in).astype(jnp.int32)


def set_ends(result, own_key, smallest, high):
    place = [jax.random.randint(jax.random.fold_in(own_key, axis), (), 0, length) for axis, length in enumerate(result.shape)]
    widest = result.shape.index(max(result.shape))
    next_to = place[:widest] + [(place[widest] + 1) % result.shape[widest]] + place[widest + 1:]
    return result.at[tuple(place)].set(smallest).at[tuple(next_to)].set(high)


def block_levels(key, shape, cuts, low, top_value):
    def one(dim, parts):
        draws = jax.random.uniform(jax.random.fold_in(jax.random.fold_in(key, 6), dim), (parts,), jnp.float32, low / len(cuts), top_value / len(cuts))
        return jnp.repeat(jnp.exp(draws), shape[dim] // parts).reshape((-1,) + (1,) * (len(shape) - dim - 1))

    gain = one(*cuts[0])
    for cut in cuts[1:]:
        gain = gain * one(*cut)
    return gain


def gaussian(key, extent, scale, most, pieces=(), held_as=jnp.bfloat16):
    gain = block_levels(key, extent, pieces, -0.22, 0.18) if pieces else 1.0
    entries = jax.random.normal(key, extent, jnp.float32) * scale * gain
    return jnp.minimum(jnp.maximum(entries, -most), most).astype(held_as)


def setup_inputs(seed: int = 0, part: int = 0) -> dict:
    seeds = jax.random.split(jax.random.key(seed), 10)
    own_keys = jax.random.split(jax.random.fold_in(seeds[9], part), 10)
    return {
        "displacement": gaussian(own_keys[0], (3, NODES), 1.0, 6.0, ((1, 16),), jnp.float32),
        "velocity": gaussian(own_keys[1], (3, NODES), 1.0, 6.0, ((1, 16),), jnp.float32),
        "send_list": draw_send_list(jax.random.fold_in(jax.random.fold_in(seeds[9], part), 71), part),
        "arrive_list": draw_arrive_list(jax.random.fold_in(jax.random.fold_in(seeds[9], part), 71), part),
        "recv_count": draw_recv_count(jax.random.fold_in(jax.random.fold_in(seeds[9], part), 71), part),
        "horizon_blocks": draw_horizon_blocks(jax.random.fold_in(jax.random.fold_in(seeds[9], part), 71), part),
        "bond_intact": set_ends((jax.random.randint(own_keys[6], (NBLK, NNZ, BLK), 0, 10) < 9).astype(jnp.int32), jax.random.fold_in(own_keys[6], 1), 0, 1),
        "modulus": jnp.clip(jnp.exp(math.log(2.0) - 1.3862944 * jax.random.uniform(own_keys[7], (NODES,), jnp.float32) ** block_levels(own_keys[7], (NODES,), ((0, 16),), -0.2, 0.2)), 0.5, 2.0),
        "bond_weight": gaussian(seeds[8], (NNZ, BLK, BLK), (NNZ * BLK) ** -0.5, 0.109375),
    }


TIME_STEP = 0.25


def migrate_nodes(stacked, send_list, arrive_list, recv_count):
    owner_ids = jnp.arange(N_WALL).astype(jnp.int32)
    source_ids = owner_ids[None, :, None] * NODES_DEV + jnp.transpose(send_list, (1, 0, 2)).astype(jnp.int32)
    live_slot = jnp.arange(CAP).astype(jnp.int32)[None, None, :] < recv_count[:, :, None]
    target_ids = jnp.where(live_slot, owner_ids[:, None, None] * NODES_DEV + arrive_list, NODES).astype(jnp.int32)
    moved = stacked[:, source_ids.reshape(-1)]
    return stacked.at[:, target_ids.reshape(-1)].set(moved, mode="drop")


def contract_blocks(source, horizon_blocks, intact_float, kernel_float):
    row_count = source.shape[0]

    def one_group(bundle):
        columns, intact = bundle
        picked = jnp.take(source, columns, axis=1).astype(jnp.float32)
        products = jnp.einsum("rbji,jki->rbjk", picked, kernel_float)
        return jnp.sum(products * intact[None], axis=2)

    grouped = lax.map(one_group, (horizon_blocks.reshape(N_WALL, NB_DEV, NNZ), intact_float.reshape(N_WALL, NB_DEV, NNZ, BLK)))
    return jnp.transpose(grouped, (1, 0, 2, 3)).reshape(row_count, NODES)


def force_of(position, modulus, stiffness, horizon_blocks, intact_float, kernel_float):
    rounded = lax.optimization_barrier(position.astype(jnp.bfloat16))
    widened = rounded.astype(jnp.float32)
    summed = contract_blocks(rounded.reshape(3, NBLK, BLK), horizon_blocks, intact_float, kernel_float)
    stretch = modulus * (summed - stiffness * widened)
    dilatation = jnp.mean(stretch, axis=0)
    soften = 1.0 / (1.0 + dilatation * dilatation)
    soft_low = lax.optimization_barrier(soften.astype(jnp.bfloat16))
    weighted = (soft_low.astype(jnp.float32) * widened).astype(jnp.bfloat16)
    packed = jnp.concatenate([weighted, soft_low[None]], axis=0)
    paired = contract_blocks(packed.reshape(4, NBLK, BLK), horizon_blocks, intact_float, kernel_float)
    return 0.5 * (modulus * (paired[:3] - widened * paired[3]) + soften * stretch)


def reference(displacement, velocity, send_list, arrive_list, recv_count, horizon_blocks, bond_intact, modulus, bond_weight):
    stacked = jnp.concatenate([displacement, velocity], axis=0)
    migrated = migrate_nodes(stacked, send_list, arrive_list, recv_count)
    position = migrated[:3]
    speed = migrated[3:]
    intact_float = bond_intact.astype(jnp.float32)
    kernel_float = bond_weight.astype(jnp.float32)
    row_totals = jnp.sum(kernel_float, axis=2)
    stiffness = jnp.sum(intact_float * row_totals[None], axis=1).reshape(NODES)
    acceleration = force_of(position, modulus, stiffness, horizon_blocks, intact_float, kernel_float)
    for substep in range(SUBSTEPS):
        position = position + TIME_STEP * speed + (0.5 * TIME_STEP * TIME_STEP) * acceleration
        following = force_of(position, modulus, stiffness, horizon_blocks, intact_float, kernel_float)
        speed = speed + (0.5 * TIME_STEP) * (acceleration + following)
        acceleration = following
    return position, speed
```

```python
import functools
import math

import jax
import jax.numpy as jnp
from jax import lax
from jax.experimental import pallas as pl
from jax.experimental.pallas import tpu as pltpu
from jax.sharding import PartitionSpec as P

SUBSTEPS = 2
LAYER = 64
PEER_BATCH = 16
TIME_STEP = 0.25
VMEM_LIMIT = 66977792
MESH = pl.DeviceIdType.MESH
F32 = jnp.float32
BF16 = jnp.bfloat16


def force_kernel(
    blocks,
    width,
    nnz,
    peers,
    send_hbm,
    arrive_hbm,
    count_hbm,
    hor_hbm,
    bonds_hbm,
    mod_hbm,
    weight_hbm,
    pos_hbm,
    vel_hbm,
    pos_out,
    vel_out,
    send_ref,
    arrive_ref,
    count_ref,
    hor_ref,
    mod_ref,
    weight_ref,
    pos_raw,
    vel_raw,
    pos_in,
    vel_in,
    out_buf,
    in_buf,
    spread_ref,
    landed_ref,
    raw_ref,
    intact_ref,
    wt_ref,
    onehot_ref,
    ext_ref,
    picked_ref,
    stiff_ref,
    acc_ref,
    stretch_ref,
    soften_ref,
    send_sem,
    recv_sem,
    node_send_sem,
    node_recv_sem,
    fetch_sem,
    pos_ref,
    vel_ref,
):
    me = lax.axis_index("wall")
    count = lax.axis_size("wall")
    reach = 3 * LAYER
    slots = 2 * (SUBSTEPS + 1)
    has_left = me > 0
    has_right = me < count - 1
    left = lax.rem(me + count - 1, count)
    right = lax.rem(me + 1, count)

    nodes = blocks * width
    capacity = send_ref.shape[1]
    shift = width.bit_length() - 1
    batch = math.gcd(PEER_BATCH, peers)
    lane_count = batch * capacity

    pairs = [(send_hbm.at[0], send_ref)]
    pairs += [(pos_hbm, pos_raw), (vel_hbm, vel_raw)]
    early = len(pairs)
    pairs += [(hor_hbm, hor_ref), (weight_hbm, weight_ref), (bonds_hbm, raw_ref)]
    pairs += [(arrive_hbm.at[0], arrive_ref), (count_hbm, count_ref), (mod_hbm, mod_ref)]
    fetches = [pltpu.make_async_copy(pair[0], pair[1], fetch_sem.at[i]) for i, pair in enumerate(pairs)]
    for fetch in fetches:
        fetch.start()

    barrier = pltpu.get_barrier_semaphore()

    def greet(step, carry):
        pl.semaphore_signal(
            barrier, inc=1, device_id={"wall": lax.rem(me + step, count)}, device_id_type=MESH
        )
        return carry

    lax.fori_loop(1, peers, greet, 0)

    def split(value):
        high = value.astype(BF16)
        low = (value - high.astype(F32)).astype(BF16)
        return high, low

    for fetch in fetches[:early]:
        fetch.wait()
    for row in range(3):
        pos_in[row] = pos_raw[:, row, :]
        vel_in[row] = vel_raw[:, row, :]
    state = [pos_in, pos_in, pos_in, vel_in, vel_in, vel_in]

    def gather_batch(step, carry):
        rows = send_ref[pl.ds(step * batch, batch), :]
        index = jnp.concatenate([rows[i : i + 1, :] for i in range(batch)], axis=1)
        picked_rows = []
        tile = 256 if lane_count % 256 == 0 else lane_count
        splits = [jnp.concatenate(split(state[row][row % 3]), axis=1) for row in range(6)]
        for start in range(0, lane_count, tile):
            part = index[:, start : start + tile]
            of_node = lax.broadcasted_iota(jnp.int32, (width, tile), 0) == (part & (width - 1))
            of_block = lax.broadcasted_iota(jnp.int32, (blocks, tile), 0) == (part >> shift)
            column = jnp.where(of_node, 1.0, 0.0).astype(BF16)
            column = jnp.concatenate([column, column], axis=0)
            values = []
            for row in range(6):
                found = jnp.dot(splits[row], column, preferred_element_type=F32)
                values.append(jnp.sum(jnp.where(of_block, found, 0.0), axis=0, keepdims=True))
            picked_rows.append(jnp.concatenate(values, axis=0))
        picked = jnp.concatenate(picked_rows, axis=1)
        for i in range(batch):
            out_buf[step * batch + i, 0:6, 0:capacity] = picked[:, i * capacity : (i + 1) * capacity]
        return carry

    lax.fori_loop(0, peers // batch, gather_batch, 0)
    in_buf[me, :, :] = jnp.zeros(in_buf.shape[1:], F32)
    pl.semaphore_wait(barrier, peers - 1)

    def node_copy(step):
        peer = lax.rem(me + step, count)
        return pltpu.make_async_remote_copy(
            src_ref=out_buf.at[peer],
            dst_ref=in_buf.at[me],
            send_sem=node_send_sem.at[peer],
            recv_sem=node_recv_sem.at[me],
            device_id={"wall": peer},
            device_id_type=MESH,
        )

    def node_arrival(step):
        peer = lax.rem(me + step, count)
        return pltpu.make_async_remote_copy(
            src_ref=out_buf.at[peer],
            dst_ref=in_buf.at[peer],
            send_sem=node_send_sem.at[peer],
            recv_sem=node_recv_sem.at[peer],
            device_id={"wall": peer},
            device_id_type=MESH,
        )

    def start_nodes(step, carry):
        node_copy(step).start()
        return carry

    lax.fori_loop(1, peers, start_nodes, 0)

    lanes = lax.broadcasted_iota(jnp.int32, (LAYER, reach), 1)
    fetches[early].wait()
    padding = jnp.zeros((-nnz % 8, blocks), jnp.int32)
    horizon = jnp.transpose(jnp.concatenate([hor_ref[...], padding], axis=0))
    for half in range(2):
        local = horizon[half * LAYER : (half + 1) * LAYER] - (me * blocks - LAYER + half * LAYER)
        for j in range(nnz):
            hit = local[:, j : j + 1] == lanes
            onehot_ref[half, pl.ds(j * LAYER, LAYER), :] = jnp.where(hit, 1.0, 0.0).astype(BF16)

    for fetch in fetches[early + 1 :]:
        fetch.wait()
    stiff = jnp.zeros((blocks, width), F32)
    ones = jnp.ones((16, width), BF16)
    for j in range(nnz):
        weight = jnp.transpose(weight_ref[j])
        wt_ref[j] = weight
        totals = jnp.dot(ones, weight, preferred_element_type=F32)[0:1, :]
        intact = raw_ref[j].astype(F32)
        intact_ref[j] = intact
        stiff = stiff + intact * totals
    stiff_ref[...] = stiff

    def halo_copy(slot, half, rows):
        wide = rows * width
        if half == 0:
            source = ext_ref.at[slot, pl.ds(LAYER, LAYER), pl.ds(0, wide)]
            target = ext_ref.at[slot, pl.ds(3 * LAYER, LAYER), pl.ds(0, wide)]
            device = left
        else:
            source = ext_ref.at[slot, pl.ds(2 * LAYER, LAYER), pl.ds(0, wide)]
            target = ext_ref.at[slot, pl.ds(0, LAYER), pl.ds(0, wide)]
            device = right
        return pltpu.make_async_remote_copy(
            src_ref=source,
            dst_ref=target,
            send_sem=send_sem.at[slot, half],
            recv_sem=recv_sem.at[slot, 1 - half],
            device_id={"wall": device},
            device_id_type=MESH,
        )

    def exists(half):
        return has_left if half == 0 else has_right

    def send(slot, half, rows):
        @pl.when(exists(half))
        def _():
            halo_copy(slot, half, rows).start()

    def wait_halo(slot, half, rows):
        @pl.when(exists(half))
        def _():
            halo_copy(slot, 1 - half, rows).wait_recv()

    def own(half):
        return pl.ds(half * LAYER, LAYER)

    def put(slot, half, row, value):
        ext_ref[slot, pl.ds(LAYER + half * LAYER, LAYER), pl.ds(row * width, width)] = value

    def get(slot, half, row):
        return ext_ref[slot, pl.ds(LAYER + half * LAYER, LAYER), pl.ds(row * width, width)].astype(F32)

    @pl.when(jnp.logical_not(has_left))
    def _():
        for slot in range(slots):
            ext_ref[slot, pl.ds(0, LAYER), :] = jnp.zeros((LAYER, 4 * width), BF16)

    @pl.when(jnp.logical_not(has_right))
    def _():
        for slot in range(slots):
            ext_ref[slot, pl.ds(3 * LAYER, LAYER), :] = jnp.zeros((LAYER, 4 * width), BF16)

    def finish_nodes(step, carry):
        node_arrival(step).wait()
        return carry

    lax.fori_loop(1, peers, finish_nodes, 0)

    landed_ref[...] = jnp.zeros(landed_ref.shape, F32)

    def scatter_batch(step, carry):
        rows = arrive_ref[pl.ds(step * batch, batch), :]
        slot_ids = lax.broadcasted_iota(jnp.int32, (1, capacity), 1)
        index = jnp.concatenate(
            [
                jnp.where(slot_ids < count_ref[0, step * batch + i], rows[i : i + 1, :], nodes)
                for i in range(batch)
            ],
            axis=1,
        )
        values = jnp.concatenate(
            [in_buf[step * batch + i][0:6, 0:capacity] for i in range(batch)], axis=1
        )
        high, low = split(values)
        parts = [high.astype(F32), low.astype(F32)]
        of_node = lax.broadcasted_iota(jnp.int32, (width, lane_count), 0) == (index & (width - 1))
        of_block = lax.broadcasted_iota(jnp.int32, (blocks, lane_count), 0) == (index >> shift)
        column = jnp.where(of_node, 1.0, 0.0).astype(BF16)
        for row in range(6):
            for k in range(2):
                spread_ref[pl.ds((2 * row + k) * blocks, blocks), :] = jnp.where(
                    of_block, parts[k][row : row + 1, :], 0.0
                ).astype(BF16)
        spread_ref[pl.ds(12 * blocks, blocks), :] = jnp.where(of_block, 1.0, 0.0).astype(BF16)
        landed_ref[...] = landed_ref[...] + lax.dot_general(
            spread_ref[...], column, (((1,), (1,)), ((), ())), preferred_element_type=F32
        )
        return carry

    lax.fori_loop(0, peers // batch, scatter_batch, 0)

    for half in (0, 1):
        hit = landed_ref[pl.ds(12 * blocks + half * LAYER, LAYER), :] > 0.5
        for row in range(6):
            high = landed_ref[pl.ds(2 * row * blocks + half * LAYER, LAYER), :]
            low = landed_ref[pl.ds((2 * row + 1) * blocks + half * LAYER, LAYER), :]
            value = jnp.where(hit, high + low, state[row][row % 3, own(half), :])
            if row < 3:
                pos_ref[row, own(half), :] = value
                put(0, half, row, value.astype(BF16))
            else:
                vel_ref[row - 3, own(half), :] = value
        send(0, half, 3)

    group = 9 if nnz % 9 == 0 else nnz

    def contract(slot, rows, half):
        wide = rows * width
        source = ext_ref[slot, pl.ds(half * LAYER, reach), pl.ds(0, wide)]
        for start in range(0, nnz, group):
            part = pl.ds(start * LAYER, group * LAYER)
            picked_ref[part, pl.ds(0, wide)] = jnp.dot(
                onehot_ref[half, part, :], source, preferred_element_type=F32
            ).astype(BF16)
        sums = [jnp.zeros((LAYER, width), F32) for _ in range(rows)]
        for j in range(nnz):
            part = pl.ds(j * LAYER, LAYER)
            mask = intact_ref[j, own(half), :]
            stacked = jnp.concatenate(
                [picked_ref[part, pl.ds(row * width, width)] for row in range(rows)], axis=0
            )
            product = jnp.dot(stacked, wt_ref[j], preferred_element_type=F32)
            for row in range(rows):
                sums[row] = sums[row] + product[row * LAYER : (row + 1) * LAYER] * mask
        return sums

    def evaluation(t, carry):
        near, far = 2 * t, 2 * t + 1
        for half in (0, 1):
            wait_halo(near, half, 3)
            summed = contract(near, 3, half)
            scaling = mod_ref[own(half), :]
            stiffness = stiff_ref[own(half), :]
            rounded = [get(near, half, row) for row in range(3)]
            stretch = [scaling * (summed[row] - stiffness * rounded[row]) for row in range(3)]
            dilatation = (stretch[0] + stretch[1] + stretch[2]) / 3.0
            soften = 1.0 / (1.0 + dilatation * dilatation)
            soft_low = soften.astype(BF16)
            soft_wide = soft_low.astype(F32)
            for row in range(3):
                put(far, half, row, (soft_wide * rounded[row]).astype(BF16))
                stretch_ref[row, own(half), :] = stretch[row]
            put(far, half, 3, soft_low)
            soften_ref[own(half), :] = soften
            send(far, half, 4)
        for half in (1, 0):
            wait_halo(far, half, 4)
            paired = contract(far, 4, half)
            scaling = mod_ref[own(half), :]
            soften = soften_ref[own(half), :]
            for row in range(3):
                rounded = get(near, half, row)
                force = 0.5 * (
                    scaling * (paired[row] - rounded * paired[3]) + soften * stretch_ref[row, own(half), :]
                )

                @pl.when(t > 0)
                def _():
                    vel_ref[row, own(half), :] = vel_ref[row, own(half), :] + 0.5 * TIME_STEP * (
                        acc_ref[row, own(half), :] + force
                    )

                acc_ref[row, own(half), :] = force

            @pl.when(t < SUBSTEPS)
            def _():
                for row in range(3):
                    moved = (
                        pos_ref[row, own(half), :]
                        + TIME_STEP * vel_ref[row, own(half), :]
                        + 0.5 * TIME_STEP * TIME_STEP * acc_ref[row, own(half), :]
                    )
                    pos_ref[row, own(half), :] = moved
                    put(2 * t + 2, half, row, moved.astype(BF16))
                send(2 * t + 2, half, 3)

        return carry

    lax.fori_loop(0, SUBSTEPS + 1, evaluation, 0)

    for row in range(3):
        pos_out[:, row, :] = pos_ref[row]
        vel_out[:, row, :] = vel_ref[row]

    for half in range(2):
        @pl.when(exists(half))
        def _():
            for slot in range(slots):
                halo_copy(slot, half, 3 if slot % 2 == 0 else 4).wait_send()


def store_kernel(pos_in, vel_in, pos_out, vel_out, sems):
    copies = [
        pltpu.make_async_copy(pos_in, pos_out, sems.at[0]),
        pltpu.make_async_copy(vel_in, vel_out, sems.at[1]),
    ]
    for copy in copies:
        copy.start()
    for copy in copies:
        copy.wait()


def shards(
    displacement,
    velocity,
    send_list,
    arrive_list,
    recv_count,
    horizon_blocks,
    bond_intact,
    modulus,
    bond_weight,
):
    node_count = displacement.shape[1]
    blocks, nnz, width = bond_intact.shape
    peers, capacity = send_list.shape[1:]
    lane_count = math.gcd(PEER_BATCH, peers) * capacity
    slots = 2 * (SUBSTEPS + 1)
    vmem = pl.BlockSpec(memory_space=pltpu.VMEM)
    hbm = pl.BlockSpec(memory_space=pltpu.HBM)
    shape = jax.ShapeDtypeStruct((blocks, 3, width), F32)
    spare = VMEM_LIMIT - 2 * 4 * blocks * 4 * width
    final_position, final_speed = pl.pallas_call(
        functools.partial(force_kernel, blocks, width, nnz, peers),
        out_shape=(pltpu.VMEM(shape.shape, F32), pltpu.VMEM(shape.shape, F32)),
        in_specs=[hbm] * 9,
        out_specs=(vmem, vmem),
        scratch_shapes=[
            pltpu.VMEM((peers, capacity), jnp.int32),
            pltpu.VMEM((peers, capacity), jnp.int32),
            pltpu.SMEM((1, peers), jnp.int32),
            pltpu.VMEM((nnz, blocks), jnp.int32),
            pltpu.VMEM((blocks, width), F32),
            pltpu.VMEM((nnz, width, width), BF16),
            pltpu.VMEM((blocks, 3, width), F32),
            pltpu.VMEM((blocks, 3, width), F32),
            pltpu.VMEM((3, blocks, width), F32),
            pltpu.VMEM((3, blocks, width), F32),
            pltpu.VMEM((peers, 8, 128 * pl.cdiv(capacity, 128)), F32),
            pltpu.VMEM((peers, 8, 128 * pl.cdiv(capacity, 128)), F32),
            pltpu.VMEM((13 * blocks, lane_count), BF16),
            pltpu.VMEM((13 * blocks, width), F32),
            pltpu.VMEM((nnz, blocks, width), jnp.int32),
            pltpu.VMEM((nnz, blocks, width), F32),
            pltpu.VMEM((nnz, width, width), BF16),
            pltpu.VMEM((2, nnz * LAYER, 3 * LAYER), BF16),
            pltpu.VMEM((slots, 4 * LAYER, 4 * width), BF16),
            pltpu.VMEM((nnz * LAYER, 4 * width), BF16),
            pltpu.VMEM((blocks, width), F32),
            pltpu.VMEM((3, blocks, width), F32),
            pltpu.VMEM((3, blocks, width), F32),
            pltpu.VMEM((blocks, width), F32),
            pltpu.SemaphoreType.DMA((slots, 2)),
            pltpu.SemaphoreType.DMA((slots, 2)),
            pltpu.SemaphoreType.DMA((peers,)),
            pltpu.SemaphoreType.DMA((peers,)),
            pltpu.SemaphoreType.DMA((9,)),
            pltpu.VMEM((3, blocks, width), F32),
            pltpu.VMEM((3, blocks, width), F32),
        ],
        compiler_params=pltpu.CompilerParams(
            collective_id=0, has_side_effects=True, vmem_limit_bytes=spare
        ),
        name="forces",
    )(
        send_list,
        arrive_list,
        recv_count,
        jnp.transpose(horizon_blocks),
        jnp.transpose(bond_intact, (1, 0, 2)),
        modulus.reshape(blocks, width),
        bond_weight,
        jnp.transpose(displacement.reshape(3, blocks, width), (1, 0, 2)),
        jnp.transpose(velocity.reshape(3, blocks, width), (1, 0, 2)),
    )
    final_position, final_speed = pl.pallas_call(
        store_kernel,
        out_shape=(shape, shape),
        in_specs=[pl.BlockSpec(memory_space=pl.ANY)] * 2,
        out_specs=(hbm, hbm),
        scratch_shapes=[pltpu.SemaphoreType.DMA((2,))],
        compiler_params=pltpu.CompilerParams(vmem_limit_bytes=1048576),
        name="store",
    )(final_position, final_speed)
    return tuple(jnp.transpose(x, (1, 0, 2)).reshape(3, node_count) for x in (final_position, final_speed))


def solution(mesh):
    in_specs = (
        P(None, ("parts", "wall")),
        P(None, ("parts", "wall")),
        P(("parts", "wall"), None, None),
        P(("parts", "wall"), None, None),
        P(("parts", "wall"), None),
        P(("parts", "wall"), None),
        P(("parts", "wall"), None, None),
        P(("parts", "wall")),
        P(),
    )
    out_specs = (P(None, ("parts", "wall")), P(None, ("parts", "wall")))
    return jax.shard_map(shards, mesh=mesh, in_specs=in_specs, out_specs=out_specs, check_vma=False)
```

```python
import functools
import math

import jax
import jax.numpy as jnp
from jax import lax
from jax.experimental import pallas as pl
from jax.experimental.pallas import tpu as pltpu
from jax.sharding import PartitionSpec as P

SUBSTEPS = 2
LAYER = 64
PEER_BATCH = 16
TIME_STEP = 0.25
VMEM_LIMIT = 66977792
MESH = pl.DeviceIdType.MESH
F32 = jnp.float32
BF16 = jnp.bfloat16


def force_kernel(
    blocks,
    width,
    nnz,
    peers,
    send_hbm,
    arrive_hbm,
    count_hbm,
    hor_hbm,
    bonds_hbm,
    mod_hbm,
    weight_hbm,
    pos_hbm,
    vel_hbm,
    pos_out,
    vel_out,
    send_ref,
    arrive_ref,
    count_ref,
    hor_ref,
    mod_ref,
    weight_ref,
    pos_raw,
    vel_raw,
    pos_in,
    vel_in,
    out_buf,
    in_buf,
    index_ref,
    node_ref,
    block_ref,
    hit_ref,
    spread_ref,
    landed_ref,
    ghost_spread_ref,
    ghost_landed_ref,
    raw_ref,
    intact_ref,
    wt_ref,
    onehot_ref,
    ext_ref,
    picked_ref,
    stiff_ref,
    stretch_ref,
    soften_ref,
    pos_ref,
    vel_ref,
    send_sem,
    recv_sem,
    index_send_sem,
    index_recv_sem,
    node_send_sem,
    node_recv_sem,
    fetch_sem,
):
    me = lax.axis_index("wall")
    count = lax.axis_size("wall")
    reach = 3 * LAYER
    slots = 2 * (SUBSTEPS + 1)
    slow = lax.rem(me, 2)
    fast = 1 - slow

    nodes = blocks * width
    capacity = send_ref.shape[1]
    shift = width.bit_length() - 1
    batch = math.gcd(PEER_BATCH, peers)
    lane_count = batch * capacity

    pairs = [(send_hbm.at[0], send_ref)]
    pairs += [(pos_hbm, pos_raw), (vel_hbm, vel_raw)]
    early = len(pairs)
    pairs += [(arrive_hbm.at[0], arrive_ref), (count_hbm, count_ref)]
    listed = len(pairs)
    pairs += [(hor_hbm, hor_ref), (weight_hbm, weight_ref), (bonds_hbm, raw_ref), (mod_hbm, mod_ref)]
    fetches = [pltpu.make_async_copy(pair[0], pair[1], fetch_sem.at[i]) for i, pair in enumerate(pairs)]
    for fetch in fetches:
        fetch.start()

    barrier = pltpu.get_barrier_semaphore()

    def greet(step, carry):
        pl.semaphore_signal(
            barrier, inc=1, device_id={"wall": lax.rem(me + step, count)}, device_id_type=MESH
        )
        return carry

    lax.fori_loop(1, peers, greet, 0)

    def split(value):
        high = value.astype(BF16)
        low = (value - high.astype(F32)).astype(BF16)
        return high, low

    def neighbour(half):
        return lax.rem(me + count - 1 + 2 * half, count)

    def exists(half):
        there = me - 1 + 2 * half
        return jnp.logical_and(there >= 0, there < count)

    def own(half):
        return pl.ds(half * LAYER if isinstance(half, int) else pl.multiple_of(half * LAYER, LAYER), LAYER)

    def held(half):
        start = LAYER + half * LAYER
        return pl.ds(start if isinstance(half, int) else pl.multiple_of(start, LAYER), LAYER)

    def halo_copy(slot, half, part, lanes):
        start = 3 * LAYER * (1 - half)
        target = pl.ds(start if isinstance(half, int) else pl.multiple_of(start, LAYER), LAYER)
        return pltpu.make_async_remote_copy(
            src_ref=ext_ref.at[slot, held(half), lanes],
            dst_ref=ext_ref.at[slot, target, lanes],
            send_sem=send_sem.at[slot, half, part],
            recv_sem=recv_sem.at[slot, 1 - half, part],
            device_id={"wall": neighbour(half)},
            device_id_type=MESH,
        )

    def lanes_of(first, rows):
        return pl.ds(first * width, rows * width)

    def send(slot, half, part, lanes):
        @pl.when(exists(half))
        def _():
            halo_copy(slot, half, part, lanes).start()

    def wait_halo(slot, half, part, lanes):
        @pl.when(exists(half))
        def _():
            halo_copy(slot, 1 - half, part, lanes).wait_recv()

    def wait_sent(slot, half, part, lanes):
        @pl.when(exists(half))
        def _():
            halo_copy(slot, half, part, lanes).wait_send()

    def put(slot, half, column, value):
        ext_ref[slot, held(half), lanes_of(column, 1)] = value

    def get(slot, half, column):
        return ext_ref[slot, held(half), lanes_of(column, 1)].astype(F32)

    def index_copy(half):
        return pltpu.make_async_remote_copy(
            src_ref=index_ref.at[1],
            dst_ref=index_ref.at[2 - 2 * half],
            send_sem=index_send_sem.at[half],
            recv_sem=index_recv_sem.at[1 - half],
            device_id={"wall": neighbour(half)},
            device_id_type=MESH,
        )

    out_buf[...] = jnp.zeros(out_buf.shape, F32)
    for fetch in fetches[:early]:
        fetch.wait()
    for row in range(3):
        pos_in[row] = pos_raw[:, row, :]
        vel_in[row] = vel_raw[:, row, :]
    state = [pos_in, pos_in, pos_in, vel_in, vel_in, vel_in]

    def gather_batch(step, carry):
        rows = send_ref[pl.ds(step * batch, batch), :]
        index = jnp.concatenate([rows[i : i + 1, :] for i in range(batch)], axis=1)
        placed_rows = []
        speed_rows = []
        tile = 256 if lane_count % 256 == 0 else lane_count
        splits = [jnp.concatenate(split(state[row][row % 3]), axis=1) for row in range(6)]
        for start in range(0, lane_count, tile):
            part = index[:, start : start + tile]
            of_node = lax.broadcasted_iota(jnp.int32, (width, tile), 0) == (part & (width - 1))
            of_block = lax.broadcasted_iota(jnp.int32, (blocks, tile), 0) == (part >> shift)
            column = jnp.where(of_node, 1.0, 0.0).astype(BF16)
            column = jnp.concatenate([column, column], axis=0)
            values = []
            for row in range(6):
                found = jnp.dot(splits[row], column, preferred_element_type=F32)
                values.append(jnp.sum(jnp.where(of_block, found, 0.0), axis=0, keepdims=True))
            placed_rows.append(jnp.concatenate(values[:3] + values[:3], axis=0))
            speed_rows.append(jnp.concatenate(values[3:], axis=0))
        placed = jnp.concatenate(placed_rows, axis=1)
        speeds = jnp.concatenate(speed_rows, axis=1)
        for i in range(batch):
            peer = step * batch + i
            mine = slice(i * capacity, (i + 1) * capacity)
            out_buf[peer + 1, 0:3, 0:capacity] = placed[0:3, mine]
            out_buf[peer + 1, 0:3, capacity : 2 * capacity] = speeds[:, mine]
            out_buf[peer + 2, 3:6, 0:capacity] = placed[3:6, mine]
            out_buf[peer, 3:6, capacity : 2 * capacity] = placed[3:6, mine]
        return carry

    lax.fori_loop(0, peers // batch, gather_batch, 0)
    in_buf[me, 0:6, :] = out_buf[me + 1, 0:6, :]
    pl.semaphore_wait(barrier, peers - 1)

    def node_copy(step):
        peer = lax.rem(me + step, count)
        return pltpu.make_async_remote_copy(
            src_ref=out_buf.at[peer + 1, pl.ds(0, 6), :],
            dst_ref=in_buf.at[me, pl.ds(0, 6), :],
            send_sem=node_send_sem.at[peer],
            recv_sem=node_recv_sem.at[me],
            device_id={"wall": peer},
            device_id_type=MESH,
        )

    def node_arrival(step):
        peer = lax.rem(me + step, count)
        return pltpu.make_async_remote_copy(
            src_ref=out_buf.at[peer + 1, pl.ds(0, 6), :],
            dst_ref=in_buf.at[peer, pl.ds(0, 6), :],
            send_sem=node_send_sem.at[peer],
            recv_sem=node_recv_sem.at[peer],
            device_id={"wall": peer},
            device_id_type=MESH,
        )

    def start_nodes(step, carry):
        node_copy(step).start()
        return carry

    lax.fori_loop(1, peers, start_nodes, 0)

    for half in (0, 1):
        for row in range(3):
            put(0, half, row, pos_in[row, own(half), :].astype(BF16))
        send(0, half, 0, lanes_of(0, 3))

    for fetch in fetches[early:listed]:
        fetch.wait()

    def index_batch(step, carry):
        rows = arrive_ref[pl.ds(step * batch, batch), :]
        slot_ids = lax.broadcasted_iota(jnp.int32, (1, capacity), 1)
        index_ref[1, step] = jnp.concatenate(
            [
                jnp.where(slot_ids < count_ref[0, step * batch + i], rows[i : i + 1, :], nodes)
                for i in range(batch)
            ],
            axis=1,
        )
        return carry

    lax.fori_loop(0, peers // batch, index_batch, 0)
    for half in (0, 1):

        @pl.when(exists(half))
        def _():
            index_copy(half).start()

        @pl.when(jnp.logical_not(exists(half)))
        def _():
            index_ref[2 * half] = jnp.full(index_ref.shape[1:], nodes, jnp.int32)
            for slot in range(slots):
                ext_ref[slot, pl.ds(3 * LAYER * half, LAYER), :] = jnp.zeros((LAYER, 4 * width), BF16)

    lanes = lax.broadcasted_iota(jnp.int32, (LAYER, reach), 1)
    fetches[listed].wait()
    padding = jnp.zeros((-nnz % 8, blocks), jnp.int32)
    horizon = jnp.transpose(jnp.concatenate([hor_ref[...], padding], axis=0))
    for half in range(2):
        local = horizon[half * LAYER : (half + 1) * LAYER] - (me * blocks - LAYER + half * LAYER)
        for j in range(nnz):
            hit = local[:, j : j + 1] == lanes
            onehot_ref[half, pl.ds(j * LAYER, LAYER), :] = jnp.where(hit, 1.0, 0.0).astype(BF16)

    for fetch in fetches[listed + 1 :]:
        fetch.wait()
    stiff = jnp.zeros((blocks, width), F32)
    ones = jnp.ones((16, width), BF16)
    for j in range(nnz):
        weight = jnp.transpose(weight_ref[j])
        wt_ref[j] = weight
        totals = jnp.dot(ones, weight, preferred_element_type=F32)[0:1, :]
        intact = raw_ref[j].astype(F32)
        intact_ref[j] = intact
        stiff = stiff + intact * totals
    stiff_ref[...] = stiff

    for half in (0, 1):

        @pl.when(exists(half))
        def _():
            index_copy(1 - half).wait_recv()

    def mark_batch(step, carry):
        for which in range(3):
            index = index_ref[which, step]
            of_node = lax.broadcasted_iota(jnp.int32, (width, lane_count), 0) == (index & (width - 1))
            node_ref[which, step] = jnp.where(of_node, 1.0, 0.0).astype(BF16)
            depth = blocks if which == 1 else LAYER
            first = LAYER if which == 0 else 0
            of_block = lax.broadcasted_iota(jnp.int32, (depth, lane_count), 0) + first == (index >> shift)
            marks = jnp.where(of_block, 1.0, 0.0).astype(BF16)
            start = (blocks + LAYER, 0, blocks)[which]
            block_ref[step, pl.ds(start, depth), :] = marks
            hit_ref[pl.ds(start, depth), :] = hit_ref[pl.ds(start, depth), :] + lax.dot_general(
                marks, node_ref[which, step], (((1,), (1,)), ((), ())), preferred_element_type=F32
            )
        return carry

    hit_ref[...] = jnp.zeros(hit_ref.shape, F32)
    lax.fori_loop(0, peers // batch, mark_batch, 0)

    landed_ref[...] = jnp.zeros(landed_ref.shape, F32)
    ghost_landed_ref[...] = jnp.zeros(ghost_landed_ref.shape, F32)

    for half in (0, 1):
        wait_halo(0, half, 0, lanes_of(0, 3))
        wait_sent(0, half, 0, lanes_of(0, 3))

    def finish_nodes(step, carry):
        node_arrival(step).wait()
        return carry

    lax.fori_loop(1, peers, finish_nodes, 0)

    def scatter_batch(step, carry):
        bundles = [in_buf[step * batch + i, 0:6, :] for i in range(batch)]
        first = jnp.concatenate([bundle[:, 0:capacity] for bundle in bundles], axis=1)
        second = jnp.concatenate([bundle[:, capacity : 2 * capacity] for bundle in bundles], axis=1)
        marks = block_ref[step, pl.ds(0, blocks), :]
        for k, values in enumerate((first, second)):
            parts = split(values)
            for row in range(3):
                for low in range(2):
                    spread_ref[pl.ds((6 * k + 2 * row + low) * blocks, blocks), :] = (
                        marks * parts[low][row : row + 1, :]
                    )
                side = pl.ds(blocks + LAYER - k * LAYER, LAYER)
                ghost_spread_ref[k, pl.ds(row * LAYER, LAYER), :] = (
                    block_ref[step, side, :] * parts[0][3 + row : 4 + row, :]
                )
            ghost_landed_ref[k] = ghost_landed_ref[k] + lax.dot_general(
                ghost_spread_ref[k], node_ref[2 * k, step], (((1,), (1,)), ((), ())), preferred_element_type=F32
            )
        landed_ref[...] = landed_ref[...] + lax.dot_general(
            spread_ref[...], node_ref[1, step], (((1,), (1,)), ((), ())), preferred_element_type=F32
        )
        return carry

    lax.fori_loop(0, peers // batch, scatter_batch, 0)

    for k in (0, 1):
        hit = hit_ref[pl.ds(blocks + LAYER - k * LAYER, LAYER), :] > 0.5
        for row in range(3):
            where = (0, pl.ds(3 * LAYER * k, LAYER), lanes_of(row, 1))
            landed = ghost_landed_ref[k, pl.ds(row * LAYER, LAYER), :]
            ext_ref[where] = jnp.where(hit, landed, ext_ref[where].astype(F32)).astype(BF16)
    for half in (0, 1):
        hit = hit_ref[own(half), :] > 0.5
        for row in range(6):
            high = landed_ref[pl.ds(2 * row * blocks + half * LAYER, LAYER), :]
            low = landed_ref[pl.ds((2 * row + 1) * blocks + half * LAYER, LAYER), :]
            value = jnp.where(hit, high + low, state[row][row % 3, own(half), :])
            if row < 3:
                pos_ref[row, own(half), :] = value
                put(0, half, row, value.astype(BF16))
            else:
                vel_ref[row - 3, own(half), :] = value

    group = 9 if nnz % 9 == 0 else nnz

    def contract(slot, first, rows, half):
        wide = rows * width
        start = half * LAYER if isinstance(half, int) else pl.multiple_of(half * LAYER, LAYER)
        source = ext_ref[slot, pl.ds(start, reach), lanes_of(first, rows)]
        for begin in range(0, nnz, group):
            part = pl.ds(begin * LAYER, group * LAYER)
            picked_ref[part, lanes_of(first, rows)] = jnp.dot(
                onehot_ref[half, part, :], source, preferred_element_type=F32
            ).astype(BF16)
        sums = [jnp.zeros((LAYER, width), F32) for _ in range(rows)]
        for j in range(nnz):
            part = pl.ds(j * LAYER, LAYER)
            mask = intact_ref[j, own(half), :]
            stacked = jnp.concatenate(
                [picked_ref[part, lanes_of(first + row, 1)] for row in range(rows)], axis=0
            )
            product = jnp.dot(stacked, wt_ref[j], preferred_element_type=F32)
            for row in range(rows):
                sums[row] = sums[row] + product[row * LAYER : (row + 1) * LAYER] * mask
        return sums

    def near_parts(apart):
        return ((0, 1), (1, 2)) if apart else ((0, 3),)

    def far_parts(apart):
        return ((0, 2), (2, 2)) if apart else ((0, 4),)

    def stretching(t, half, apart, waits):
        near, far = 2 * t, 2 * t + 1
        summed = []
        for part, (first, rows) in enumerate(near_parts(apart)):
            if waits:
                wait_halo(near, half, part, lanes_of(first, rows))
            summed += contract(near, first, rows, half)
        scaling = mod_ref[own(half), :]
        stiffness = stiff_ref[own(half), :]
        rounded = [get(near, half, row) for row in range(3)]
        stretch = [scaling * (summed[row] - stiffness * rounded[row]) for row in range(3)]
        dilatation = (stretch[0] + stretch[1] + stretch[2]) / 3.0
        soften = 1.0 / (1.0 + dilatation * dilatation)
        soft_low = soften.astype(BF16)
        soft_wide = soft_low.astype(F32)
        put(far, half, 0, soft_low)
        for row in range(3):
            put(far, half, 1 + row, (soft_wide * rounded[row]).astype(BF16))
        for part, (first, rows) in enumerate(far_parts(apart)):
            send(far, half, part, lanes_of(first, rows))
        for row in range(3):
            stretch_ref[row, own(half), :] = stretch[row]
        soften_ref[own(half), :] = soften

    def pairing(t, half, apart, last):
        near, far = 2 * t, 2 * t + 1
        scaling = mod_ref[own(half), :]
        soften = soften_ref[own(half), :]
        kick = 0.5 * TIME_STEP if last else jnp.where(t == 0, 0.5 * TIME_STEP, TIME_STEP)
        paired = []
        for part, (first, rows) in enumerate(far_parts(apart)):
            wait_halo(far, half, part, lanes_of(first, rows))
            begin = max(len(paired) - 1, 0)
            paired += contract(far, first, rows, half)
            for row in range(begin, len(paired) - 1):
                rounded = get(near, half, row)
                force = 0.5 * (
                    scaling * (paired[1 + row] - rounded * paired[0]) + soften * stretch_ref[row, own(half), :]
                )
                speed = vel_ref[row, own(half), :] + kick * force
                if last:
                    vel_out[own(half), row, :] = speed
                else:
                    vel_ref[row, own(half), :] = speed
                    moved = pos_ref[row, own(half), :] + TIME_STEP * speed
                    pos_ref[row, own(half), :] = moved
                    put(near + 2, half, row, moved.astype(BF16))
            if not last:
                send(near + 2, half, part, lanes_of(*near_parts(apart)[part]))

    stretching(0, slow, True, False)
    stretching(0, fast, False, False)

    def substep(t, carry):
        pairing(t, fast, False, False)
        pairing(t, slow, True, False)
        stretching(t + 1, fast, False, True)
        stretching(t + 1, slow, True, True)
        return carry

    lax.fori_loop(0, SUBSTEPS, substep, 0)

    for row in range(3):
        pos_out[:, row, :] = pos_ref[row]
    pairing(SUBSTEPS, fast, False, True)
    pairing(SUBSTEPS, slow, True, True)

    for half in (0, 1):

        @pl.when(exists(half))
        def _():
            index_copy(half).wait_send()

    for slot in range(1, slots):
        for half, apart in ((fast, False), (slow, True)):
            parts = far_parts(apart) if slot % 2 else near_parts(apart)
            for part, (first, rows) in enumerate(parts):
                wait_sent(slot, half, part, lanes_of(first, rows))


def store_kernel(pos_in, vel_in, pos_out, vel_out, sems):
    copies = [
        pltpu.make_async_copy(pos_in, pos_out, sems.at[0]),
        pltpu.make_async_copy(vel_in, vel_out, sems.at[1]),
    ]
    for copy in copies:
        copy.start()
    for copy in copies:
        copy.wait()


def shards(
    displacement,
    velocity,
    send_list,
    arrive_list,
    recv_count,
    horizon_blocks,
    bond_intact,
    modulus,
    bond_weight,
):
    node_count = displacement.shape[1]
    blocks, nnz, width = bond_intact.shape
    peers, capacity = send_list.shape[1:]
    lane_count = math.gcd(PEER_BATCH, peers) * capacity
    batches = peers * capacity // lane_count
    bundle_width = 128 * pl.cdiv(2 * capacity, 128)
    slots = 2 * (SUBSTEPS + 1)
    vmem = pl.BlockSpec(memory_space=pltpu.VMEM)
    hbm = pl.BlockSpec(memory_space=pltpu.HBM)
    shape = jax.ShapeDtypeStruct((blocks, 3, width), F32)
    spare = VMEM_LIMIT - 2 * 4 * blocks * 4 * width
    final_position, final_speed = pl.pallas_call(
        functools.partial(force_kernel, blocks, width, nnz, peers),
        out_shape=(pltpu.VMEM(shape.shape, F32), pltpu.VMEM(shape.shape, F32)),
        in_specs=[hbm] * 9,
        out_specs=(vmem, vmem),
        scratch_shapes=[
            pltpu.VMEM((peers, capacity), jnp.int32),
            pltpu.VMEM((peers, capacity), jnp.int32),
            pltpu.SMEM((1, peers), jnp.int32),
            pltpu.VMEM((nnz, blocks), jnp.int32),
            pltpu.VMEM((blocks, width), F32),
            pltpu.VMEM((nnz, width, width), BF16),
            pltpu.VMEM((blocks, 3, width), F32),
            pltpu.VMEM((blocks, 3, width), F32),
            pltpu.VMEM((3, blocks, width), F32),
            pltpu.VMEM((3, blocks, width), F32),
            pltpu.VMEM((peers + 2, 8, bundle_width), F32),
            pltpu.VMEM((peers, 8, bundle_width), F32),
            pltpu.VMEM((3, batches, 1, lane_count), jnp.int32),
            pltpu.VMEM((3, batches, width, lane_count), BF16),
            pltpu.VMEM((batches, blocks + 2 * LAYER, lane_count), BF16),
            pltpu.VMEM((blocks + 2 * LAYER, width), F32),
            pltpu.VMEM((12 * blocks, lane_count), BF16),
            pltpu.VMEM((12 * blocks, width), F32),
            pltpu.VMEM((2, 3 * LAYER, lane_count), BF16),
            pltpu.VMEM((2, 3 * LAYER, width), F32),
            pltpu.VMEM((nnz, blocks, width), jnp.int32),
            pltpu.VMEM((nnz, blocks, width), F32),
            pltpu.VMEM((nnz, width, width), BF16),
            pltpu.VMEM((2, nnz * LAYER, 3 * LAYER), BF16),
            pltpu.VMEM((slots, 4 * LAYER, 4 * width), BF16),
            pltpu.VMEM((nnz * LAYER, 4 * width), BF16),
            pltpu.VMEM((blocks, width), F32),
            pltpu.VMEM((3, blocks, width), F32),
            pltpu.VMEM((blocks, width), F32),
            pltpu.VMEM((3, blocks, width), F32),
            pltpu.VMEM((3, blocks, width), F32),
            pltpu.SemaphoreType.DMA((slots, 2, 2)),
            pltpu.SemaphoreType.DMA((slots, 2, 2)),
            pltpu.SemaphoreType.DMA((2,)),
            pltpu.SemaphoreType.DMA((2,)),
            pltpu.SemaphoreType.DMA((peers,)),
            pltpu.SemaphoreType.DMA((peers,)),
            pltpu.SemaphoreType.DMA((9,)),
        ],
        compiler_params=pltpu.CompilerParams(
            collective_id=0, has_side_effects=True, vmem_limit_bytes=spare
        ),
        name="forces",
    )(
        send_list,
        arrive_list,
        recv_count,
        jnp.transpose(horizon_blocks),
        jnp.transpose(bond_intact, (1, 0, 2)),
        modulus.reshape(blocks, width),
        bond_weight,
        jnp.transpose(displacement.reshape(3, blocks, width), (1, 0, 2)),
        jnp.transpose(velocity.reshape(3, blocks, width), (1, 0, 2)),
    )
    final_position, final_speed = pl.pallas_call(
        store_kernel,
        out_shape=(shape, shape),
        in_specs=[pl.BlockSpec(memory_space=pl.ANY)] * 2,
        out_specs=(hbm, hbm),
        scratch_shapes=[pltpu.SemaphoreType.DMA((2,))],
        compiler_params=pltpu.CompilerParams(vmem_limit_bytes=1048576),
        name="store",
    )(final_position, final_speed)
    return tuple(jnp.transpose(x, (1, 0, 2)).reshape(3, node_count) for x in (final_position, final_speed))


def solution(mesh):
    in_specs = (
        P(None, ("parts", "wall")),
        P(None, ("parts", "wall")),
        P(("parts", "wall"), None, None),
        P(("parts", "wall"), None, None),
        P(("parts", "wall"), None),
        P(("parts", "wall"), None),
        P(("parts", "wall"), None, None),
        P(("parts", "wall")),
        P(),
    )
    out_specs = (P(None, ("parts", "wall")), P(None, ("parts", "wall")))
    return jax.shard_map(shards, mesh=mesh, in_specs=in_specs, out_specs=out_specs, check_vma=False)
```

```python
import functools
import math

import jax
import jax.numpy as jnp
from jax import lax
from jax.experimental import pallas as pl
from jax.experimental.pallas import tpu as pltpu
from jax.sharding import PartitionSpec as P

SUBSTEPS = 2
LAYER = 64
PEER_BATCH = 16
TIME_STEP = 0.25
VMEM_LIMIT = 66977792
MESH = pl.DeviceIdType.MESH
F32 = jnp.float32
BF16 = jnp.bfloat16


def force_kernel(
    blocks,
    width,
    nnz,
    peers,
    send_hbm,
    arrive_hbm,
    count_hbm,
    hor_hbm,
    bonds_hbm,
    mod_hbm,
    weight_hbm,
    pos_hbm,
    vel_hbm,
    pos_out,
    vel_out,
    send_ref,
    arrive_ref,
    count_ref,
    hor_ref,
    mod_ref,
    weight_ref,
    pos_raw,
    vel_raw,
    pos_in,
    vel_in,
    out_pos,
    in_pos,
    out_vel,
    in_vel,
    index_ref,
    node_ref,
    block_ref,
    hit_ref,
    spread_ref,
    landed_ref,
    ghost_spread_ref,
    ghost_landed_ref,
    raw_ref,
    intact_ref,
    wt_ref,
    onehot_ref,
    ext_ref,
    picked_ref,
    stiff_ref,
    stretch_ref,
    soften_ref,
    pos_ref,
    vel_ref,
    send_sem,
    recv_sem,
    index_send_sem,
    index_recv_sem,
    node_send_sem,
    node_recv_sem,
    fetch_sem,
):
    me = lax.axis_index("wall")
    count = lax.axis_size("wall")
    reach = 3 * LAYER
    slots = 2 * (SUBSTEPS + 1)
    slow = lax.rem(me, 2)
    fast = 1 - slow

    nodes = blocks * width
    capacity = send_ref.shape[1]
    shift = width.bit_length() - 1
    batch = math.gcd(PEER_BATCH, peers)
    batches = peers // batch
    lane_count = batch * capacity

    barrier = pltpu.get_barrier_semaphore()

    def greet(step, carry):
        pl.semaphore_signal(
            barrier, inc=1, device_id={"wall": lax.rem(me + step, count)}, device_id_type=MESH
        )
        return carry

    lax.fori_loop(1, peers, greet, 0)

    pairs = [(send_hbm.at[0], send_ref), (pos_hbm, pos_raw)]
    early = len(pairs)
    pairs += [(vel_hbm, vel_raw), (arrive_hbm.at[0], arrive_ref), (count_hbm, count_ref)]
    listed = len(pairs)
    pairs += [(hor_hbm, hor_ref), (weight_hbm, weight_ref), (bonds_hbm, raw_ref), (mod_hbm, mod_ref)]
    fetches = [pltpu.make_async_copy(pair[0], pair[1], fetch_sem.at[i]) for i, pair in enumerate(pairs)]
    for fetch in fetches:
        fetch.start()

    def split(value):
        high = value.astype(BF16)
        low = (value - high.astype(F32)).astype(BF16)
        return high, low

    def neighbour(half):
        return lax.rem(me + count - 1 + 2 * half, count)

    def exists(half):
        there = me - 1 + 2 * half
        return jnp.logical_and(there >= 0, there < count)

    def own(half):
        return pl.ds(half * LAYER if isinstance(half, int) else pl.multiple_of(half * LAYER, LAYER), LAYER)

    def held(half):
        start = LAYER + half * LAYER
        return pl.ds(start if isinstance(half, int) else pl.multiple_of(start, LAYER), LAYER)

    def halo_copy(slot, half, part, lanes):
        start = 3 * LAYER * (1 - half)
        target = pl.ds(start if isinstance(half, int) else pl.multiple_of(start, LAYER), LAYER)
        return pltpu.make_async_remote_copy(
            src_ref=ext_ref.at[slot, held(half), lanes],
            dst_ref=ext_ref.at[slot, target, lanes],
            send_sem=send_sem.at[slot, half, part],
            recv_sem=recv_sem.at[slot, 1 - half, part],
            device_id={"wall": neighbour(half)},
            device_id_type=MESH,
        )

    def lanes_of(first, rows):
        return pl.ds(first * width, rows * width)

    def send(slot, half, part, lanes):
        @pl.when(exists(half))
        def _():
            halo_copy(slot, half, part, lanes).start()

    def wait_halo(slot, half, part, lanes):
        @pl.when(exists(half))
        def _():
            halo_copy(slot, 1 - half, part, lanes).wait_recv()

    def wait_sent(slot, half, part, lanes):
        @pl.when(exists(half))
        def _():
            halo_copy(slot, half, part, lanes).wait_send()

    def put(slot, half, column, value):
        ext_ref[slot, held(half), lanes_of(column, 1)] = value

    def get(slot, half, column):
        return ext_ref[slot, held(half), lanes_of(column, 1)].astype(F32)

    def index_copy(half):
        return pltpu.make_async_remote_copy(
            src_ref=index_ref.at[1],
            dst_ref=index_ref.at[2 - 2 * half],
            send_sem=index_send_sem.at[half],
            recv_sem=index_recv_sem.at[1 - half],
            device_id={"wall": neighbour(half)},
            device_id_type=MESH,
        )

    def each_batch(body):
        def step(index, carry):
            body(index)
            return carry

        if batches == 1:
            body(0)
        else:
            lax.fori_loop(0, batches, step, 0)

    def pick(step, source):
        rows = send_ref[pl.ds(step * batch, batch), :]
        index = jnp.concatenate([rows[i : i + 1, :] for i in range(batch)], axis=1)
        picked_rows = []
        tile = 256 if lane_count % 256 == 0 else lane_count
        splits = [jnp.concatenate(split(source[row]), axis=1) for row in range(3)]
        for start in range(0, lane_count, tile):
            part = index[:, start : start + tile]
            of_node = lax.broadcasted_iota(jnp.int32, (width, tile), 0) == (part & (width - 1))
            of_block = lax.broadcasted_iota(jnp.int32, (blocks, tile), 0) == (part >> shift)
            column = jnp.where(of_node, 1.0, 0.0).astype(BF16)
            column = jnp.concatenate([column, column], axis=0)
            values = []
            for row in range(3):
                found = jnp.dot(splits[row], column, preferred_element_type=F32)
                values.append(jnp.sum(jnp.where(of_block, found, 0.0), axis=0, keepdims=True))
            picked_rows.append(values)
        return [jnp.concatenate([values[row] for values in picked_rows], axis=1) for row in range(3)]

    def gather_places(step):
        values = pick(step, pos_in)
        placed = jnp.concatenate(values + values, axis=0)
        for i in range(batch):
            peer = step * batch + i
            mine = slice(i * capacity, (i + 1) * capacity)
            out_pos[peer + 1, 0:3, 0:capacity] = placed[0:3, mine]
            out_pos[peer + 2, 0:3, capacity : 2 * capacity] = placed[0:3, mine]
            out_pos[peer, 3:6, 0:capacity] = placed[3:6, mine]

    def gather_speeds(step):
        speeds = jnp.concatenate(pick(step, vel_in), axis=0)
        for i in range(batch):
            out_vel[step * batch + i, 0:3, 0:capacity] = speeds[:, i * capacity : (i + 1) * capacity]

    def pos_copy(peer, there, many=1):
        return pltpu.make_async_remote_copy(
            src_ref=out_pos.at[pl.ds(peer, many), pl.ds(0, 6), :],
            dst_ref=in_pos.at[pl.ds(there, many), pl.ds(0, 6), :],
            send_sem=node_send_sem.at[0],
            recv_sem=node_recv_sem.at[0],
            device_id={"wall": neighbour(1)} if many > 1 else {"wall": peer - 1},
            device_id_type=MESH,
        )

    def vel_copy(peer, there, many=1):
        return pltpu.make_async_remote_copy(
            src_ref=out_vel.at[pl.ds(peer, many), pl.ds(0, 3), :],
            dst_ref=in_vel.at[pl.ds(there, many), pl.ds(0, 3), :],
            send_sem=node_send_sem.at[1],
            recv_sem=node_recv_sem.at[1],
            device_id={"wall": neighbour(1)} if many > 1 else {"wall": peer},
            device_id_type=MESH,
        )

    out_pos[...] = jnp.zeros(out_pos.shape, F32)
    for fetch in fetches[:early]:
        fetch.wait()
    for row in range(3):
        pos_in[row] = pos_raw[:, row, :]
    each_batch(gather_places)
    in_pos[me, 0:6, :] = out_pos[me + 1, 0:6, :]
    pl.semaphore_wait(barrier, peers - 1)

    def start_places(step, carry):
        pos_copy(lax.rem(me + step, count) + 1, me).start()
        return carry

    lax.fori_loop(1, peers, start_places, 0)

    for half in (0, 1):
        for row in range(3):
            put(0, half, row, pos_in[row, own(half), :].astype(BF16))
        send(0, half, 0, lanes_of(0, 3))

    for fetch in fetches[early:listed]:
        fetch.wait()
    out_vel[...] = jnp.zeros(out_vel.shape, F32)
    for row in range(3):
        vel_in[row] = vel_raw[:, row, :]

    def index_batch(step):
        rows = arrive_ref[pl.ds(step * batch, batch), :]
        slot_ids = lax.broadcasted_iota(jnp.int32, (1, capacity), 1)
        index_ref[1, step] = jnp.concatenate(
            [
                jnp.where(slot_ids < count_ref[0, step * batch + i], rows[i : i + 1, :], nodes)
                for i in range(batch)
            ],
            axis=1,
        )

    each_batch(index_batch)
    for half in (0, 1):

        @pl.when(exists(half))
        def _():
            index_copy(half).start()

        @pl.when(jnp.logical_not(exists(half)))
        def _():
            index_ref[2 * half] = jnp.full(index_ref.shape[1:], nodes, jnp.int32)
            for slot in range(slots):
                ext_ref[slot, pl.ds(3 * LAYER * half, LAYER), :] = jnp.zeros((LAYER, 4 * width), BF16)

    each_batch(gather_speeds)
    in_vel[me, 0:3, :] = out_vel[me, 0:3, :]

    def start_speeds(step, carry):
        vel_copy(lax.rem(me + step, count), me).start()
        return carry

    lax.fori_loop(1, peers, start_speeds, 0)

    lanes = lax.broadcasted_iota(jnp.int32, (LAYER, reach), 1)
    fetches[listed].wait()
    padding = jnp.zeros((-nnz % 8, blocks), jnp.int32)
    horizon = jnp.transpose(jnp.concatenate([hor_ref[...], padding], axis=0))
    for half in range(2):
        local = horizon[half * LAYER : (half + 1) * LAYER] - (me * blocks - LAYER + half * LAYER)
        for j in range(nnz):
            hit = local[:, j : j + 1] == lanes
            onehot_ref[half, pl.ds(j * LAYER, LAYER), :] = jnp.where(hit, 1.0, 0.0).astype(BF16)

    for fetch in fetches[listed + 1 :]:
        fetch.wait()
    stiff = jnp.zeros((blocks, width), F32)
    ones = jnp.ones((16, width), BF16)
    for j in range(nnz):
        weight = jnp.transpose(weight_ref[j])
        wt_ref[j] = weight
        totals = jnp.dot(ones, weight, preferred_element_type=F32)[0:1, :]
        intact = raw_ref[j].astype(F32)
        intact_ref[j] = intact
        stiff = stiff + intact * totals
    stiff_ref[...] = stiff

    for half in (0, 1):

        @pl.when(exists(half))
        def _():
            index_copy(1 - half).wait_recv()

    def gain(ref, value):
        ref[...] = value if batches == 1 else ref[...] + value

    def clear(refs):
        if batches > 1:
            for ref in refs:
                ref[...] = jnp.zeros(ref.shape, F32)

    def land(marks, which, step):
        return lax.dot_general(
            marks, node_ref[which, step], (((1,), (1,)), ((), ())), preferred_element_type=F32
        )

    def mark_batch(step):
        for which in range(3):
            index = index_ref[which, step]
            of_node = lax.broadcasted_iota(jnp.int32, (width, lane_count), 0) == (index & (width - 1))
            node_ref[which, step] = jnp.where(of_node, 1.0, 0.0).astype(BF16)
            depth = blocks if which == 1 else LAYER
            first = LAYER if which == 0 else 0
            of_block = lax.broadcasted_iota(jnp.int32, (depth, lane_count), 0) + first == (index >> shift)
            marks = jnp.where(of_block, 1.0, 0.0).astype(BF16)
            rows = pl.ds((blocks + LAYER, 0, blocks)[which], depth)
            block_ref[step, rows, :] = marks
            gain(hit_ref.at[rows], land(marks, which, step))

    clear([hit_ref])
    each_batch(mark_batch)
    clear([landed_ref, ghost_landed_ref])

    for half in (0, 1):
        wait_halo(0, half, 0, lanes_of(0, 3))
        wait_sent(0, half, 0, lanes_of(0, 3))

    def places(step):
        bundles = [in_pos[step * batch + i, 0:6, :] for i in range(batch)]
        first = jnp.concatenate([bundle[:, 0:capacity] for bundle in bundles], axis=1)
        left = jnp.concatenate([bundle[0:3, capacity : 2 * capacity] for bundle in bundles], axis=1)
        return first[0:3], left, first[3:6]

    def ghost_rows(half):
        return pl.ds(pl.multiple_of(blocks + LAYER - half * LAYER, LAYER), LAYER)

    def land_ghost(step, half, values):
        rounded = values.astype(BF16)
        for row in range(3):
            ghost_spread_ref[pl.ds(row * LAYER, LAYER), :] = (
                block_ref[step, ghost_rows(half), :] * rounded[row : row + 1, :]
            )
        gain(ghost_landed_ref.at[half], land(ghost_spread_ref[...], 2 * half, step))

    def keep_ghost(half):
        hit = hit_ref[ghost_rows(half), :] > 0.5
        rows = pl.ds(pl.multiple_of(3 * LAYER * half, LAYER), LAYER)
        for row in range(3):
            landed = ghost_landed_ref[half, pl.ds(row * LAYER, LAYER), :]
            held_now = ext_ref[0, rows, lanes_of(row, 1)].astype(F32)
            ext_ref[0, rows, lanes_of(row, 1)] = jnp.where(hit, landed, held_now).astype(BF16)

    def spread(step, section, rounded):
        marks = block_ref[step, pl.ds(0, blocks), :]
        for row in range(3):
            spread_ref[pl.ds((3 * section + row) * blocks, blocks), :] = marks * rounded[row : row + 1, :]

    def land_section(step, section, pieces):
        for first, rows in pieces:
            rows_of = pl.ds((3 * section + first) * blocks, rows * blocks)
            gain(landed_ref.at[rows_of], land(spread_ref[rows_of, :], 1, step))

    def land_first(step):
        mine, left, right = places(step)
        spread(step, 0, mine.astype(BF16))
        land_ghost(step, slow, jnp.where(slow == 0, left, right))
        land_section(step, 0, ((0, 2), (2, 1)))

    def land_fast(step):
        _, left, right = places(step)
        land_ghost(step, fast, jnp.where(fast == 0, left, right))

    def land_rest(step):
        mine, _, _ = places(step)
        speeds = jnp.concatenate(
            [in_vel[step * batch + i, 0:3, :][:, 0:capacity] for i in range(batch)], axis=1
        )
        spread(step, 1, split(mine)[1])
        for part, rounded in enumerate(split(speeds)):
            spread(step, 2 + part, rounded)
        for section in (1, 2, 3):
            land_section(step, section, ((0, 3),))

    pos_copy(0, 0, peers - 1).wait_recv()
    each_batch(land_first)
    keep_ghost(slow)
    for half in (0, 1):
        hit = hit_ref[own(half), :] > 0.5
        for row in range(3):
            landed = landed_ref[pl.ds(row * blocks + half * LAYER, LAYER), :]
            put(0, half, row, jnp.where(hit, landed, get(0, half, row)).astype(BF16))

    group = 9 if nnz % 9 == 0 else nnz

    def contract(slot, first, rows, half):
        wide = rows * width
        start = half * LAYER if isinstance(half, int) else pl.multiple_of(half * LAYER, LAYER)
        source = ext_ref[slot, pl.ds(start, reach), lanes_of(first, rows)]
        for begin in range(0, nnz, group):
            part = pl.ds(begin * LAYER, group * LAYER)
            picked_ref[part, lanes_of(first, rows)] = jnp.dot(
                onehot_ref[half, part, :], source, preferred_element_type=F32
            ).astype(BF16)
        sums = [jnp.zeros((LAYER, width), F32) for _ in range(rows)]
        for j in range(nnz):
            part = pl.ds(j * LAYER, LAYER)
            mask = intact_ref[j, own(half), :]
            stacked = jnp.concatenate(
                [picked_ref[part, lanes_of(first + row, 1)] for row in range(rows)], axis=0
            )
            product = jnp.dot(stacked, wt_ref[j], preferred_element_type=F32)
            for row in range(rows):
                sums[row] = sums[row] + product[row * LAYER : (row + 1) * LAYER] * mask
        return sums

    def near_parts(apart):
        return ((0, 1), (1, 2)) if apart else ((0, 3),)

    def far_parts(apart):
        return ((0, 2), (2, 2)) if apart else ((0, 4),)

    def stretching(t, half, apart, waits):
        near, far = 2 * t, 2 * t + 1
        summed = []
        for part, (first, rows) in enumerate(near_parts(apart)):
            if waits:
                wait_halo(near, half, part, lanes_of(first, rows))
            summed += contract(near, first, rows, half)
        scaling = mod_ref[own(half), :]
        stiffness = stiff_ref[own(half), :]
        rounded = [get(near, half, row) for row in range(3)]
        stretch = [scaling * (summed[row] - stiffness * rounded[row]) for row in range(3)]
        dilatation = (stretch[0] + stretch[1] + stretch[2]) / 3.0
        soften = 1.0 / (1.0 + dilatation * dilatation)
        soft_low = soften.astype(BF16)
        soft_wide = soft_low.astype(F32)
        put(far, half, 0, soft_low)
        for row in range(3):
            put(far, half, 1 + row, (soft_wide * rounded[row]).astype(BF16))
        for part, (first, rows) in enumerate(far_parts(apart)):
            send(far, half, part, lanes_of(first, rows))
        for row in range(3):
            stretch_ref[row, own(half), :] = stretch[row]
        soften_ref[own(half), :] = soften

    def pairing(t, half, apart, last):
        near, far = 2 * t, 2 * t + 1
        scaling = mod_ref[own(half), :]
        soften = soften_ref[own(half), :]
        kick = 0.5 * TIME_STEP if last else jnp.where(t == 0, 0.5 * TIME_STEP, TIME_STEP)
        paired = []
        for part, (first, rows) in enumerate(far_parts(apart)):
            wait_halo(far, half, part, lanes_of(first, rows))
            begin = max(len(paired) - 1, 0)
            paired += contract(far, first, rows, half)
            for row in range(begin, len(paired) - 1):
                rounded = get(near, half, row)
                force = 0.5 * (
                    scaling * (paired[1 + row] - rounded * paired[0]) + soften * stretch_ref[row, own(half), :]
                )
                speed = vel_ref[row, own(half), :] + kick * force
                if last:
                    vel_out[own(half), row, :] = speed
                else:
                    vel_ref[row, own(half), :] = speed
                    moved = pos_ref[row, own(half), :] + TIME_STEP * speed
                    pos_ref[row, own(half), :] = moved
                    put(near + 2, half, row, moved.astype(BF16))
            if not last:
                send(near + 2, half, part, lanes_of(*near_parts(apart)[part]))

    stretching(0, slow, True, False)
    each_batch(land_fast)
    keep_ghost(fast)
    stretching(0, fast, False, False)

    vel_copy(0, 0, peers - 1).wait_recv()
    each_batch(land_rest)
    for half in (0, 1):
        hit = hit_ref[own(half), :] > 0.5
        for row in range(3):
            parts = [
                landed_ref[pl.ds((3 * section + row) * blocks + half * LAYER, LAYER), :] for section in range(4)
            ]
            pos_ref[row, own(half), :] = jnp.where(hit, parts[0] + parts[1], pos_in[row, own(half), :])
            vel_ref[row, own(half), :] = jnp.where(hit, parts[2] + parts[3], vel_in[row, own(half), :])

    def substep(t, carry):
        pairing(t, fast, False, False)
        pairing(t, slow, True, False)
        stretching(t + 1, fast, False, True)
        stretching(t + 1, slow, True, True)
        return carry

    lax.fori_loop(0, SUBSTEPS, substep, 0)

    for row in range(3):
        pos_out[:, row, :] = pos_ref[row]
    pairing(SUBSTEPS, fast, False, True)
    pairing(SUBSTEPS, slow, True, True)

    pos_copy(0, 0, peers - 1).wait_send()
    vel_copy(0, 0, peers - 1).wait_send()
    for half in (0, 1):

        @pl.when(exists(half))
        def _():
            index_copy(half).wait_send()

    for slot in range(1, slots):
        for half, apart in ((fast, False), (slow, True)):
            parts = far_parts(apart) if slot % 2 else near_parts(apart)
            for part, (first, rows) in enumerate(parts):
                wait_sent(slot, half, part, lanes_of(first, rows))


def store_kernel(pos_in, vel_in, pos_out, vel_out, sems):
    copies = [
        pltpu.make_async_copy(pos_in, pos_out, sems.at[0]),
        pltpu.make_async_copy(vel_in, vel_out, sems.at[1]),
    ]
    for copy in copies:
        copy.start()
    for copy in copies:
        copy.wait()


def shards(
    displacement,
    velocity,
    send_list,
    arrive_list,
    recv_count,
    horizon_blocks,
    bond_intact,
    modulus,
    bond_weight,
):
    node_count = displacement.shape[1]
    blocks, nnz, width = bond_intact.shape
    peers, capacity = send_list.shape[1:]
    lane_count = math.gcd(PEER_BATCH, peers) * capacity
    batches = peers * capacity // lane_count
    bundle_width = 128 * pl.cdiv(2 * capacity, 128)
    slots = 2 * (SUBSTEPS + 1)
    vmem = pl.BlockSpec(memory_space=pltpu.VMEM)
    hbm = pl.BlockSpec(memory_space=pltpu.HBM)
    shape = jax.ShapeDtypeStruct((blocks, 3, width), F32)
    spare = VMEM_LIMIT - 2 * 4 * blocks * 4 * width
    final_position, final_speed = pl.pallas_call(
        functools.partial(force_kernel, blocks, width, nnz, peers),
        out_shape=(pltpu.VMEM(shape.shape, F32), pltpu.VMEM(shape.shape, F32)),
        in_specs=[hbm] * 9,
        out_specs=(vmem, vmem),
        scratch_shapes=[
            pltpu.VMEM((peers, capacity), jnp.int32),
            pltpu.VMEM((peers, capacity), jnp.int32),
            pltpu.SMEM((1, peers), jnp.int32),
            pltpu.VMEM((nnz, blocks), jnp.int32),
            pltpu.VMEM((blocks, width), F32),
            pltpu.VMEM((nnz, width, width), BF16),
            pltpu.VMEM((blocks, 3, width), F32),
            pltpu.VMEM((blocks, 3, width), F32),
            pltpu.VMEM((3, blocks, width), F32),
            pltpu.VMEM((3, blocks, width), F32),
            pltpu.VMEM((peers + 2, 8, bundle_width), F32),
            pltpu.VMEM((peers, 8, bundle_width), F32),
            pltpu.VMEM((peers, 8, bundle_width), F32),
            pltpu.VMEM((peers, 8, bundle_width), F32),
            pltpu.VMEM((3, batches, 1, lane_count), jnp.int32),
            pltpu.VMEM((3, batches, width, lane_count), BF16),
            pltpu.VMEM((batches, blocks + 2 * LAYER, lane_count), BF16),
            pltpu.VMEM((blocks + 2 * LAYER, width), F32),
            pltpu.VMEM((12 * blocks, lane_count), BF16),
            pltpu.VMEM((12 * blocks, width), F32),
            pltpu.VMEM((3 * LAYER, lane_count), BF16),
            pltpu.VMEM((2, 3 * LAYER, width), F32),
            pltpu.VMEM((nnz, blocks, width), jnp.int32),
            pltpu.VMEM((nnz, blocks, width), F32),
            pltpu.VMEM((nnz, width, width), BF16),
            pltpu.VMEM((2, nnz * LAYER, 3 * LAYER), BF16),
            pltpu.VMEM((slots, 4 * LAYER, 4 * width), BF16),
            pltpu.VMEM((nnz * LAYER, 4 * width), BF16),
            pltpu.VMEM((blocks, width), F32),
            pltpu.VMEM((3, blocks, width), F32),
            pltpu.VMEM((blocks, width), F32),
            pltpu.VMEM((3, blocks, width), F32),
            pltpu.VMEM((3, blocks, width), F32),
            pltpu.SemaphoreType.DMA((slots, 2, 2)),
            pltpu.SemaphoreType.DMA((slots, 2, 2)),
            pltpu.SemaphoreType.DMA((2,)),
            pltpu.SemaphoreType.DMA((2,)),
            pltpu.SemaphoreType.DMA((2,)),
            pltpu.SemaphoreType.DMA((2,)),
            pltpu.SemaphoreType.DMA((9,)),
        ],
        compiler_params=pltpu.CompilerParams(
            collective_id=0, has_side_effects=True, vmem_limit_bytes=spare
        ),
        name="forces",
    )(
        send_list,
        arrive_list,
        recv_count,
        jnp.transpose(horizon_blocks),
        jnp.transpose(bond_intact, (1, 0, 2)),
        modulus.reshape(blocks, width),
        bond_weight,
        jnp.transpose(displacement.reshape(3, blocks, width), (1, 0, 2)),
        jnp.transpose(velocity.reshape(3, blocks, width), (1, 0, 2)),
    )
    final_position, final_speed = pl.pallas_call(
        store_kernel,
        out_shape=(shape, shape),
        in_specs=[pl.BlockSpec(memory_space=pl.ANY)] * 2,
        out_specs=(hbm, hbm),
        scratch_shapes=[pltpu.SemaphoreType.DMA((2,))],
        compiler_params=pltpu.CompilerParams(vmem_limit_bytes=1048576),
        name="store",
    )(final_position, final_speed)
    return tuple(jnp.transpose(x, (1, 0, 2)).reshape(3, node_count) for x in (final_position, final_speed))


def solution(mesh):
    in_specs = (
        P(None, ("parts", "wall")),
        P(None, ("parts", "wall")),
        P(("parts", "wall"), None, None),
        P(("parts", "wall"), None, None),
        P(("parts", "wall"), None),
        P(("parts", "wall"), None),
        P(("parts", "wall"), None, None),
        P(("parts", "wall")),
        P(),
    )
    out_specs = (P(None, ("parts", "wall")), P(None, ("parts", "wall")))
    return jax.shard_map(shards, mesh=mesh, in_specs=in_specs, out_specs=out_specs, check_vma=False)
```

```python
import functools
import math

import jax
import jax.numpy as jnp
from jax import lax
from jax.experimental import pallas as pl
from jax.experimental.pallas import tpu as pltpu
from jax.sharding import PartitionSpec as P

SUBSTEPS = 2
LAYER = 64
PEER_BATCH = 16
TIME_STEP = 0.25
VMEM_LIMIT = 66977792
MESH = pl.DeviceIdType.MESH
F32 = jnp.float32
BF16 = jnp.bfloat16


def force_kernel(
    blocks,
    width,
    nnz,
    peers,
    send_hbm,
    arrive_hbm,
    count_hbm,
    hor_hbm,
    bonds_hbm,
    mod_hbm,
    weight_hbm,
    pos_hbm,
    vel_hbm,
    pos_out,
    vel_out,
    send_ref,
    arrive_ref,
    count_ref,
    hor_ref,
    mod_ref,
    weight_ref,
    pos_raw,
    vel_raw,
    pos_in,
    vel_in,
    out_pos,
    in_pos,
    out_vel,
    in_vel,
    leave_node_ref,
    leave_block_ref,
    index_ref,
    node_ref,
    block_ref,
    hit_ref,
    spread_ref,
    landed_ref,
    ghost_spread_ref,
    ghost_landed_ref,
    raw_ref,
    intact_ref,
    wt_ref,
    onehot_ref,
    ext_ref,
    picked_ref,
    stiff_ref,
    stretch_ref,
    soften_ref,
    pos_ref,
    vel_ref,
    send_sem,
    recv_sem,
    index_send_sem,
    index_recv_sem,
    node_send_sem,
    node_recv_sem,
    fetch_sem,
):
    me = lax.axis_index("wall")
    count = lax.axis_size("wall")
    reach = 3 * LAYER
    slots = 2 * (SUBSTEPS + 1)
    slow = lax.rem(me, 2)
    fast = 1 - slow

    nodes = blocks * width
    capacity = send_ref.shape[1]
    shift = width.bit_length() - 1
    batch = math.gcd(PEER_BATCH, peers)
    batches = peers // batch
    lane_count = batch * capacity

    barrier = pltpu.get_barrier_semaphore()

    def greet(step, carry):
        pl.semaphore_signal(
            barrier, inc=1, device_id={"wall": lax.rem(me + step, count)}, device_id_type=MESH
        )
        return carry

    lax.fori_loop(1, peers, greet, 0)

    pairs = {
        "send": (send_hbm.at[0], send_ref),
        "pos": (pos_hbm, pos_raw),
        "arrive": (arrive_hbm.at[0], arrive_ref),
        "count": (count_hbm, count_ref),
        "hor": (hor_hbm, hor_ref),
        "weight": (weight_hbm, weight_ref),
        "bonds": (bonds_hbm, raw_ref),
        "mod": (mod_hbm, mod_ref),
        "vel": (vel_hbm, vel_raw),
    }
    fetches = {
        name: pltpu.make_async_copy(pair[0], pair[1], fetch_sem.at[i])
        for i, (name, pair) in enumerate(pairs.items())
    }
    for name in ("send", "pos", "arrive", "count", "hor"):
        fetches[name].start()

    def split(value):
        high = value.astype(BF16)
        low = (value - high.astype(F32)).astype(BF16)
        return high, low

    def neighbour(half):
        return lax.rem(me + count - 1 + 2 * half, count)

    def exists(half):
        there = me - 1 + 2 * half
        return jnp.logical_and(there >= 0, there < count)

    def own(half):
        return pl.ds(half * LAYER if isinstance(half, int) else pl.multiple_of(half * LAYER, LAYER), LAYER)

    def held(half):
        start = LAYER + half * LAYER
        return pl.ds(start if isinstance(half, int) else pl.multiple_of(start, LAYER), LAYER)

    def halo_copy(slot, half, part, lanes):
        start = 3 * LAYER * (1 - half)
        target = pl.ds(start if isinstance(half, int) else pl.multiple_of(start, LAYER), LAYER)
        return pltpu.make_async_remote_copy(
            src_ref=ext_ref.at[slot, held(half), lanes],
            dst_ref=ext_ref.at[slot, target, lanes],
            send_sem=send_sem.at[slot, half, part],
            recv_sem=recv_sem.at[slot, 1 - half, part],
            device_id={"wall": neighbour(half)},
            device_id_type=MESH,
        )

    def lanes_of(first, rows):
        return pl.ds(first * width, rows * width)

    def send(slot, half, part, lanes):
        @pl.when(exists(half))
        def _():
            halo_copy(slot, half, part, lanes).start()

    def wait_halo(slot, half, part, lanes):
        @pl.when(exists(half))
        def _():
            halo_copy(slot, 1 - half, part, lanes).wait_recv()

    def wait_sent(slot, half, part, lanes):
        @pl.when(exists(half))
        def _():
            halo_copy(slot, half, part, lanes).wait_send()

    def put(slot, half, column, value):
        ext_ref[slot, held(half), lanes_of(column, 1)] = value

    def get(slot, half, column):
        return ext_ref[slot, held(half), lanes_of(column, 1)].astype(F32)

    def index_copy(half):
        return pltpu.make_async_remote_copy(
            src_ref=index_ref.at[1],
            dst_ref=index_ref.at[2 - 2 * half],
            send_sem=index_send_sem.at[half],
            recv_sem=index_recv_sem.at[1 - half],
            device_id={"wall": neighbour(half)},
            device_id_type=MESH,
        )

    def each_batch(body):
        def step(index, carry):
            body(index)
            return carry

        if batches == 1:
            body(0)
        else:
            lax.fori_loop(0, batches, step, 0)

    def apart(body):
        def once(step, carry):
            body()
            return carry

        lax.fori_loop(0, 1 + lax.div(me, count), once, 0)

    def mark_leaving(step):
        rows = send_ref[pl.ds(step * batch, batch), :]
        index = jnp.concatenate([rows[i : i + 1, :] for i in range(batch)], axis=1)
        of_node = lax.broadcasted_iota(jnp.int32, (width, lane_count), 0) == (index & (width - 1))
        of_block = lax.broadcasted_iota(jnp.int32, (blocks, lane_count), 0) == (index >> shift)
        column = jnp.where(of_node, 1.0, 0.0).astype(BF16)
        leave_node_ref[step, 0:width, :] = column
        leave_node_ref[step, width : 2 * width, :] = column
        leave_block_ref[step] = jnp.where(of_block, 1.0, 0.0)

    def pick(step, source):
        tile = 256 if lane_count % 256 == 0 else lane_count
        splits = [jnp.concatenate(split(source[row]), axis=1) for row in range(3)]
        picked_rows = []
        for start in range(0, lane_count, tile):
            of_block = leave_block_ref[step, :, start : start + tile]
            values = []
            for row in range(3):
                found = jnp.dot(
                    splits[row], leave_node_ref[step, :, start : start + tile], preferred_element_type=F32
                )
                values.append(jnp.sum(of_block * found, axis=0, keepdims=True))
            picked_rows.append(values)
        return [jnp.concatenate([values[row] for values in picked_rows], axis=1) for row in range(3)]

    def gather_places(step):
        values = pick(step, pos_in)
        placed = jnp.concatenate(values + values, axis=0)
        for i in range(batch):
            peer = step * batch + i
            mine = slice(i * capacity, (i + 1) * capacity)
            out_pos[peer + 1, 0:3, 0:capacity] = placed[0:3, mine]
            out_pos[peer + 2, 0:3, capacity : 2 * capacity] = placed[0:3, mine]
            out_pos[peer, 3:6, 0:capacity] = placed[3:6, mine]

    def gather_speeds(step):
        speeds = jnp.concatenate(pick(step, vel_in), axis=0)
        for i in range(batch):
            out_vel[step * batch + i, 0:3, 0:capacity] = speeds[:, i * capacity : (i + 1) * capacity]

    def pos_copy(peer, there, many=1):
        return pltpu.make_async_remote_copy(
            src_ref=out_pos.at[pl.ds(peer, many), pl.ds(0, 6), :],
            dst_ref=in_pos.at[pl.ds(there, many), pl.ds(0, 6), :],
            send_sem=node_send_sem.at[0],
            recv_sem=node_recv_sem.at[0],
            device_id={"wall": neighbour(1)} if many > 1 else {"wall": peer - 1},
            device_id_type=MESH,
        )

    def vel_copy(peer, there, many=1):
        return pltpu.make_async_remote_copy(
            src_ref=out_vel.at[pl.ds(peer, many), pl.ds(0, 3), :],
            dst_ref=in_vel.at[pl.ds(there, many), pl.ds(0, 3), :],
            send_sem=node_send_sem.at[1],
            recv_sem=node_recv_sem.at[1],
            device_id={"wall": neighbour(1)} if many > 1 else {"wall": peer},
            device_id_type=MESH,
        )

    out_pos[...] = jnp.zeros(out_pos.shape, F32)
    def index_batch(step):
        rows = arrive_ref[pl.ds(step * batch, batch), :]
        slot_ids = lax.broadcasted_iota(jnp.int32, (1, capacity), 1)
        index_ref[1, step] = jnp.concatenate(
            [
                jnp.where(slot_ids < count_ref[0, step * batch + i], rows[i : i + 1, :], nodes)
                for i in range(batch)
            ],
            axis=1,
        )

    fetches["send"].wait()
    each_batch(mark_leaving)
    for name in ("arrive", "count"):
        fetches[name].wait()
    each_batch(index_batch)
    fetches["pos"].wait()
    for name in ("weight", "bonds", "mod", "vel"):
        fetches[name].start()
    for row in range(3):
        pos_in[row] = pos_raw[:, row, :]
    each_batch(gather_places)
    in_pos[me, 0:6, :] = out_pos[me + 1, 0:6, :]
    pl.semaphore_wait(barrier, peers - 1)

    def start_places(step, carry):
        pos_copy(lax.rem(me + step, count) + 1, me).start()
        return carry

    lax.fori_loop(1, peers, start_places, 0)

    for half in (0, 1):

        @pl.when(exists(half))
        def _():
            index_copy(half).start()

        @pl.when(jnp.logical_not(exists(half)))
        def _():
            index_ref[2 * half] = jnp.full(index_ref.shape[1:], nodes, jnp.int32)
            for slot in range(slots):
                ext_ref[slot, pl.ds(3 * LAYER * half, LAYER), :] = jnp.zeros((LAYER, 4 * width), BF16)

    for half in (0, 1):
        for row in range(3):
            put(0, half, row, pos_in[row, own(half), :].astype(BF16))
        send(0, half, 0, lanes_of(0, 3))

    lanes = lax.broadcasted_iota(jnp.int32, (LAYER, reach), 1)
    fetches["hor"].wait()
    padding = jnp.zeros((-nnz % 8, blocks), jnp.int32)
    horizon = jnp.transpose(jnp.concatenate([hor_ref[...], padding], axis=0))
    for half in range(2):
        local = horizon[half * LAYER : (half + 1) * LAYER] - (me * blocks - LAYER + half * LAYER)
        for j in range(nnz):
            hit = local[:, j : j + 1] == lanes
            onehot_ref[half, pl.ds(j * LAYER, LAYER), :] = jnp.where(hit, 1.0, 0.0).astype(BF16)

    fetches["vel"].wait()
    out_vel[...] = jnp.zeros(out_vel.shape, F32)
    for row in range(3):
        vel_in[row] = vel_raw[:, row, :]

    each_batch(gather_speeds)
    in_vel[me, 0:3, :] = out_vel[me, 0:3, :]

    def start_speeds(step, carry):
        vel_copy(lax.rem(me + step, count), me).start()
        return carry

    lax.fori_loop(1, peers, start_speeds, 0)

    for name in ("weight", "bonds", "mod"):
        fetches[name].wait()
    stiff = jnp.zeros((blocks, width), F32)
    ones = jnp.ones((16, width), BF16)
    for j in range(nnz):
        weight = jnp.transpose(weight_ref[j])
        wt_ref[j] = weight
        totals = jnp.dot(ones, weight, preferred_element_type=F32)[0:1, :]
        intact = raw_ref[j].astype(F32)
        intact_ref[j] = intact
        stiff = stiff + intact * totals
    stiff_ref[...] = stiff

    for half in (0, 1):

        @pl.when(exists(half))
        def _():
            index_copy(1 - half).wait_recv()

    def gain(ref, value):
        ref[...] = value if batches == 1 else ref[...] + value

    def clear(refs):
        if batches > 1:
            for ref in refs:
                ref[...] = jnp.zeros(ref.shape, F32)

    def land(marks, which, step):
        return lax.dot_general(
            marks, node_ref[which, step], (((1,), (1,)), ((), ())), preferred_element_type=F32
        )

    def mark_batch(step):
        for which in range(3):
            index = index_ref[which, step]
            of_node = lax.broadcasted_iota(jnp.int32, (width, lane_count), 0) == (index & (width - 1))
            node_ref[which, step] = jnp.where(of_node, 1.0, 0.0).astype(BF16)
            depth = blocks if which == 1 else LAYER
            first = LAYER if which == 0 else 0
            of_block = lax.broadcasted_iota(jnp.int32, (depth, lane_count), 0) + first == (index >> shift)
            marks = jnp.where(of_block, 1.0, 0.0).astype(BF16)
            rows = pl.ds((blocks + LAYER, 0, blocks)[which], depth)
            block_ref[step, rows, :] = marks
            gain(hit_ref.at[rows], land(marks, which, step))

    clear([hit_ref])
    each_batch(mark_batch)
    clear([landed_ref, ghost_landed_ref])

    for half in (0, 1):
        wait_halo(0, half, 0, lanes_of(0, 3))
        wait_sent(0, half, 0, lanes_of(0, 3))

    def places(step):
        bundles = [in_pos[step * batch + i, 0:6, :] for i in range(batch)]
        first = jnp.concatenate([bundle[:, 0:capacity] for bundle in bundles], axis=1)
        left = jnp.concatenate([bundle[0:3, capacity : 2 * capacity] for bundle in bundles], axis=1)
        return first[0:3], left, first[3:6]

    def ghost_rows(half):
        return pl.ds(pl.multiple_of(blocks + LAYER - half * LAYER, LAYER), LAYER)

    def land_ghost(step, half, values):
        rounded = values.astype(BF16)
        for row in range(3):
            ghost_spread_ref[pl.ds(row * LAYER, LAYER), :] = (
                block_ref[step, ghost_rows(half), :] * rounded[row : row + 1, :]
            )
        gain(ghost_landed_ref.at[half], land(ghost_spread_ref[...], 2 * half, step))

    def keep_ghost(half):
        hit = hit_ref[ghost_rows(half), :] > 0.5
        rows = pl.ds(pl.multiple_of(3 * LAYER * half, LAYER), LAYER)
        for row in range(3):
            landed = ghost_landed_ref[half, pl.ds(row * LAYER, LAYER), :]
            held_now = ext_ref[0, rows, lanes_of(row, 1)].astype(F32)
            ext_ref[0, rows, lanes_of(row, 1)] = jnp.where(hit, landed, held_now).astype(BF16)

    def spread(step, section, rounded):
        marks = block_ref[step, pl.ds(0, blocks), :]
        for row in range(3):
            spread_ref[pl.ds((3 * section + row) * blocks, blocks), :] = marks * rounded[row : row + 1, :]

    def land_section(step, section, pieces):
        for first, rows in pieces:
            rows_of = pl.ds((3 * section + first) * blocks, rows * blocks)
            gain(landed_ref.at[rows_of], land(spread_ref[rows_of, :], 1, step))

    def land_first(step):
        mine, left, right = places(step)
        spread(step, 0, mine.astype(BF16))
        land_ghost(step, slow, jnp.where(slow == 0, left, right))
        land_section(step, 0, ((0, 2), (2, 1)))

    def land_fast(step):
        _, left, right = places(step)
        land_ghost(step, fast, jnp.where(fast == 0, left, right))

    def land_rest(step):
        mine, _, _ = places(step)
        speeds = jnp.concatenate(
            [in_vel[step * batch + i, 0:3, :][:, 0:capacity] for i in range(batch)], axis=1
        )
        spread(step, 1, split(mine)[1])
        for part, rounded in enumerate(split(speeds)):
            spread(step, 2 + part, rounded)
        for section in (1, 2, 3):
            land_section(step, section, ((0, 3),))

    pos_copy(0, 0, peers - 1).wait_recv()

    @apart
    def _():
        each_batch(land_first)
        keep_ghost(slow)
        for half in (0, 1):
            hit = hit_ref[own(half), :] > 0.5
            for row in range(3):
                landed = landed_ref[pl.ds(row * blocks + half * LAYER, LAYER), :]
                put(0, half, row, jnp.where(hit, landed, get(0, half, row)).astype(BF16))

    group = 9 if nnz % 9 == 0 else nnz

    def contract(slot, first, rows, half):
        wide = rows * width
        start = half * LAYER if isinstance(half, int) else pl.multiple_of(half * LAYER, LAYER)
        source = ext_ref[slot, pl.ds(start, reach), lanes_of(first, rows)]
        for begin in range(0, nnz, group):
            part = pl.ds(begin * LAYER, group * LAYER)
            picked_ref[part, lanes_of(first, rows)] = jnp.dot(
                onehot_ref[half, part, :], source, preferred_element_type=F32
            ).astype(BF16)
        sums = [jnp.zeros((LAYER, width), F32) for _ in range(rows)]
        for j in range(nnz):
            part = pl.ds(j * LAYER, LAYER)
            mask = intact_ref[j, own(half), :]
            stacked = jnp.concatenate(
                [picked_ref[part, lanes_of(first + row, 1)] for row in range(rows)], axis=0
            )
            product = jnp.dot(stacked, wt_ref[j], preferred_element_type=F32)
            for row in range(rows):
                sums[row] = sums[row] + product[row * LAYER : (row + 1) * LAYER] * mask
        return sums

    def near_parts(parted):
        return ((0, 1), (1, 2)) if parted else ((0, 3),)

    def far_parts(parted):
        return ((0, 2), (2, 2)) if parted else ((0, 4),)

    def stretching(t, half, parted, waits):
        near, far = 2 * t, 2 * t + 1
        summed = []
        for part, (first, rows) in enumerate(near_parts(parted and waits)):
            if waits:
                wait_halo(near, half, part, lanes_of(first, rows))
            summed += contract(near, first, rows, half)
        scaling = mod_ref[own(half), :]
        stiffness = stiff_ref[own(half), :]
        rounded = [get(near, half, row) for row in range(3)]
        stretch = [scaling * (summed[row] - stiffness * rounded[row]) for row in range(3)]
        dilatation = (stretch[0] + stretch[1] + stretch[2]) / 3.0
        soften = 1.0 / (1.0 + dilatation * dilatation)
        soft_low = soften.astype(BF16)
        soft_wide = soft_low.astype(F32)
        put(far, half, 0, soft_low)
        for row in range(3):
            put(far, half, 1 + row, (soft_wide * rounded[row]).astype(BF16))
        for part, (first, rows) in enumerate(far_parts(parted)):
            send(far, half, part, lanes_of(first, rows))
        for row in range(3):
            stretch_ref[row, own(half), :] = stretch[row]
        soften_ref[own(half), :] = soften

    def pairing(t, half, parted, last):
        near, far = 2 * t, 2 * t + 1
        scaling = mod_ref[own(half), :]
        soften = soften_ref[own(half), :]
        kick = 0.5 * TIME_STEP if last else jnp.where(t == 0, 0.5 * TIME_STEP, TIME_STEP)
        paired = []
        for part, (first, rows) in enumerate(far_parts(parted)):
            wait_halo(far, half, part, lanes_of(first, rows))
            begin = max(len(paired) - 1, 0)
            paired += contract(far, first, rows, half)
            for row in range(begin, len(paired) - 1):
                rounded = get(near, half, row)
                force = 0.5 * (
                    scaling * (paired[1 + row] - rounded * paired[0]) + soften * stretch_ref[row, own(half), :]
                )
                speed = vel_ref[row, own(half), :] + kick * force
                if last:
                    vel_out[own(half), row, :] = speed
                else:
                    vel_ref[row, own(half), :] = speed
                    moved = pos_ref[row, own(half), :] + TIME_STEP * speed
                    pos_ref[row, own(half), :] = moved
                    put(near + 2, half, row, moved.astype(BF16))
            if not last:
                send(near + 2, half, part, lanes_of(*near_parts(parted)[part]))

    stretching(0, slow, True, False)

    @apart
    def _():
        each_batch(land_fast)
        keep_ghost(fast)

    stretching(0, fast, False, False)

    vel_copy(0, 0, peers - 1).wait_recv()
    each_batch(land_rest)
    for half in (0, 1):
        hit = hit_ref[own(half), :] > 0.5
        for row in range(3):
            parts = [
                landed_ref[pl.ds((3 * section + row) * blocks + half * LAYER, LAYER), :] for section in range(4)
            ]
            pos_ref[row, own(half), :] = jnp.where(hit, parts[0] + parts[1], pos_in[row, own(half), :])
            vel_ref[row, own(half), :] = jnp.where(hit, parts[2] + parts[3], vel_in[row, own(half), :])

    def substep(t, carry):
        pairing(t, fast, False, False)
        pairing(t, slow, True, False)
        stretching(t + 1, fast, False, True)
        stretching(t + 1, slow, True, True)
        return carry

    lax.fori_loop(0, SUBSTEPS, substep, 0)

    for row in range(3):
        pos_out[:, row, :] = pos_ref[row]
    pairing(SUBSTEPS, fast, False, True)
    pairing(SUBSTEPS, slow, True, True)

    pos_copy(0, 0, peers - 1).wait_send()
    vel_copy(0, 0, peers - 1).wait_send()
    for half in (0, 1):

        @pl.when(exists(half))
        def _():
            index_copy(half).wait_send()

    for slot in range(1, slots):
        for half, parted in ((fast, False), (slow, True)):
            parts = far_parts(parted) if slot % 2 else near_parts(parted)
            for part, (first, rows) in enumerate(parts):
                wait_sent(slot, half, part, lanes_of(first, rows))


def store_kernel(pos_in, vel_in, pos_out, vel_out, sems):
    copies = [
        pltpu.make_async_copy(pos_in, pos_out, sems.at[0]),
        pltpu.make_async_copy(vel_in, vel_out, sems.at[1]),
    ]
    for copy in copies:
        copy.start()
    for copy in copies:
        copy.wait()


def shards(
    displacement,
    velocity,
    send_list,
    arrive_list,
    recv_count,
    horizon_blocks,
    bond_intact,
    modulus,
    bond_weight,
):
    node_count = displacement.shape[1]
    blocks, nnz, width = bond_intact.shape
    peers, capacity = send_list.shape[1:]
    lane_count = math.gcd(PEER_BATCH, peers) * capacity
    batches = peers * capacity // lane_count
    bundle_width = 128 * pl.cdiv(2 * capacity, 128)
    slots = 2 * (SUBSTEPS + 1)
    vmem = pl.BlockSpec(memory_space=pltpu.VMEM)
    hbm = pl.BlockSpec(memory_space=pltpu.HBM)
    shape = jax.ShapeDtypeStruct((blocks, 3, width), F32)
    spare = VMEM_LIMIT - 2 * 4 * blocks * 4 * width
    final_position, final_speed = pl.pallas_call(
        functools.partial(force_kernel, blocks, width, nnz, peers),
        out_shape=(pltpu.VMEM(shape.shape, F32), pltpu.VMEM(shape.shape, F32)),
        in_specs=[hbm] * 9,
        out_specs=(vmem, vmem),
        scratch_shapes=[
            pltpu.VMEM((peers, capacity), jnp.int32),
            pltpu.VMEM((peers, capacity), jnp.int32),
            pltpu.SMEM((1, peers), jnp.int32),
            pltpu.VMEM((nnz, blocks), jnp.int32),
            pltpu.VMEM((blocks, width), F32),
            pltpu.VMEM((nnz, width, width), BF16),
            pltpu.VMEM((blocks, 3, width), F32),
            pltpu.VMEM((blocks, 3, width), F32),
            pltpu.VMEM((3, blocks, width), F32),
            pltpu.VMEM((3, blocks, width), F32),
            pltpu.VMEM((peers + 2, 8, bundle_width), F32),
            pltpu.VMEM((peers, 8, bundle_width), F32),
            pltpu.VMEM((peers, 8, bundle_width), F32),
            pltpu.VMEM((peers, 8, bundle_width), F32),
            pltpu.VMEM((batches, 2 * width, lane_count), BF16),
            pltpu.VMEM((batches, blocks, lane_count), F32),
            pltpu.VMEM((3, batches, 1, lane_count), jnp.int32),
            pltpu.VMEM((3, batches, width, lane_count), BF16),
            pltpu.VMEM((batches, blocks + 2 * LAYER, lane_count), BF16),
            pltpu.VMEM((blocks + 2 * LAYER, width), F32),
            pltpu.VMEM((12 * blocks, lane_count), BF16),
            pltpu.VMEM((12 * blocks, width), F32),
            pltpu.VMEM((3 * LAYER, lane_count), BF16),
            pltpu.VMEM((2, 3 * LAYER, width), F32),
            pltpu.VMEM((nnz, blocks, width), jnp.int32),
            pltpu.VMEM((nnz, blocks, width), F32),
            pltpu.VMEM((nnz, width, width), BF16),
            pltpu.VMEM((2, nnz * LAYER, 3 * LAYER), BF16),
            pltpu.VMEM((slots, 4 * LAYER, 4 * width), BF16),
            pltpu.VMEM((nnz * LAYER, 4 * width), BF16),
            pltpu.VMEM((blocks, width), F32),
            pltpu.VMEM((3, blocks, width), F32),
            pltpu.VMEM((blocks, width), F32),
            pltpu.VMEM((3, blocks, width), F32),
            pltpu.VMEM((3, blocks, width), F32),
            pltpu.SemaphoreType.DMA((slots, 2, 2)),
            pltpu.SemaphoreType.DMA((slots, 2, 2)),
            pltpu.SemaphoreType.DMA((2,)),
            pltpu.SemaphoreType.DMA((2,)),
            pltpu.SemaphoreType.DMA((2,)),
            pltpu.SemaphoreType.DMA((2,)),
            pltpu.SemaphoreType.DMA((9,)),
        ],
        compiler_params=pltpu.CompilerParams(
            collective_id=0, has_side_effects=True, vmem_limit_bytes=spare
        ),
        name="forces",
    )(
        send_list,
        arrive_list,
        recv_count,
        jnp.transpose(horizon_blocks),
        jnp.transpose(bond_intact, (1, 0, 2)),
        modulus.reshape(blocks, width),
        bond_weight,
        jnp.transpose(displacement.reshape(3, blocks, width), (1, 0, 2)),
        jnp.transpose(velocity.reshape(3, blocks, width), (1, 0, 2)),
    )
    final_position, final_speed = pl.pallas_call(
        store_kernel,
        out_shape=(shape, shape),
        in_specs=[pl.BlockSpec(memory_space=pl.ANY)] * 2,
        out_specs=(hbm, hbm),
        scratch_shapes=[pltpu.SemaphoreType.DMA((2,))],
        compiler_params=pltpu.CompilerParams(vmem_limit_bytes=1048576),
        name="store",
    )(final_position, final_speed)
    return tuple(jnp.transpose(x, (1, 0, 2)).reshape(3, node_count) for x in (final_position, final_speed))


def solution(mesh):
    in_specs = (
        P(None, ("parts", "wall")),
        P(None, ("parts", "wall")),
        P(("parts", "wall"), None, None),
        P(("parts", "wall"), None, None),
        P(("parts", "wall"), None),
        P(("parts", "wall"), None),
        P(("parts", "wall"), None, None),
        P(("parts", "wall")),
        P(),
    )
    out_specs = (P(None, ("parts", "wall")), P(None, ("parts", "wall")))
    return jax.shard_map(shards, mesh=mesh, in_specs=in_specs, out_specs=out_specs, check_vma=False)
```

```python
import functools
import math

import jax
import jax.numpy as jnp
from jax import lax
from jax.experimental import pallas as pl
from jax.experimental.pallas import tpu as pltpu
from jax.sharding import PartitionSpec as P

SUBSTEPS = 2
LAYER = 64
PEER_BATCH = 16
TIME_STEP = 0.25
VMEM_LIMIT = 66977792
MESH = pl.DeviceIdType.MESH
F32 = jnp.float32
BF16 = jnp.bfloat16


def force_kernel(
    blocks,
    width,
    nnz,
    peers,
    send_hbm,
    arrive_hbm,
    count_hbm,
    hor_hbm,
    bonds_hbm,
    mod_hbm,
    weight_hbm,
    pos_hbm,
    vel_hbm,
    pos_out,
    vel_out,
    send_ref,
    arrive_ref,
    count_ref,
    hor_ref,
    mod_ref,
    weight_ref,
    pos_raw,
    vel_raw,
    pos_in,
    vel_in,
    out_pos,
    in_pos,
    out_vel,
    in_vel,
    leave_node_ref,
    leave_block_ref,
    index_ref,
    node_ref,
    block_ref,
    hit_ref,
    spread_ref,
    landed_ref,
    ghost_spread_ref,
    ghost_landed_ref,
    raw_ref,
    intact_ref,
    wt_ref,
    onehot_ref,
    ext_ref,
    picked_ref,
    stiff_ref,
    stretch_ref,
    soften_ref,
    pos_ref,
    vel_ref,
    send_sem,
    recv_sem,
    index_send_sem,
    index_recv_sem,
    node_send_sem,
    node_recv_sem,
    fetch_sem,
):
    me = lax.axis_index("wall")
    count = lax.axis_size("wall")
    reach = 3 * LAYER
    slots = 2 * (SUBSTEPS + 1)
    slow = lax.rem(me, 2)
    fast = 1 - slow

    nodes = blocks * width
    capacity = send_ref.shape[1]
    shift = width.bit_length() - 1
    batch = math.gcd(PEER_BATCH, peers)
    batches = peers // batch
    lane_count = batch * capacity

    barrier = pltpu.get_barrier_semaphore()

    def greet(step, carry):
        pl.semaphore_signal(
            barrier, inc=1, device_id={"wall": lax.rem(me + step, count)}, device_id_type=MESH
        )
        return carry

    lax.fori_loop(1, peers, greet, 0)

    pairs = {
        "send": (send_hbm.at[0], send_ref),
        "pos": (pos_hbm, pos_raw),
        "arrive": (arrive_hbm.at[0], arrive_ref),
        "count": (count_hbm, count_ref),
        "hor": (hor_hbm, hor_ref),
        "weight": (weight_hbm, weight_ref),
        "bonds": (bonds_hbm, raw_ref),
        "mod": (mod_hbm, mod_ref),
        "vel": (vel_hbm, vel_raw),
    }
    fetches = {
        name: pltpu.make_async_copy(pair[0], pair[1], fetch_sem.at[i])
        for i, (name, pair) in enumerate(pairs.items())
    }
    for name in ("send", "pos", "arrive", "count", "hor"):
        fetches[name].start()

    def split(value):
        high = value.astype(BF16)
        low = (value - high.astype(F32)).astype(BF16)
        return high, low

    def neighbour(half):
        return lax.rem(me + count - 1 + 2 * half, count)

    def exists(half):
        there = me - 1 + 2 * half
        return jnp.logical_and(there >= 0, there < count)

    def own(half):
        return pl.ds(half * LAYER if isinstance(half, int) else pl.multiple_of(half * LAYER, LAYER), LAYER)

    def held(half):
        start = LAYER + half * LAYER
        return pl.ds(start if isinstance(half, int) else pl.multiple_of(start, LAYER), LAYER)

    def halo_copy(slot, half, part, lanes):
        start = 3 * LAYER * (1 - half)
        target = pl.ds(start if isinstance(half, int) else pl.multiple_of(start, LAYER), LAYER)
        return pltpu.make_async_remote_copy(
            src_ref=ext_ref.at[slot, held(half), lanes],
            dst_ref=ext_ref.at[slot, target, lanes],
            send_sem=send_sem.at[slot, half, part],
            recv_sem=recv_sem.at[slot, 1 - half, part],
            device_id={"wall": neighbour(half)},
            device_id_type=MESH,
        )

    def lanes_of(first, rows):
        return pl.ds(first * width, rows * width)

    def send(slot, half, part, lanes):
        @pl.when(exists(half))
        def _():
            halo_copy(slot, half, part, lanes).start()

    def wait_halo(slot, half, part, lanes):
        @pl.when(exists(half))
        def _():
            halo_copy(slot, 1 - half, part, lanes).wait_recv()

    def wait_sent(slot, half, part, lanes):
        @pl.when(exists(half))
        def _():
            halo_copy(slot, half, part, lanes).wait_send()

    def put(slot, half, column, value):
        ext_ref[slot, held(half), lanes_of(column, 1)] = value

    def get(slot, half, column):
        return ext_ref[slot, held(half), lanes_of(column, 1)].astype(F32)

    def index_copy(half):
        return pltpu.make_async_remote_copy(
            src_ref=index_ref.at[1],
            dst_ref=index_ref.at[2 - 2 * half],
            send_sem=index_send_sem.at[half],
            recv_sem=index_recv_sem.at[1 - half],
            device_id={"wall": neighbour(half)},
            device_id_type=MESH,
        )

    def each_batch(body):
        def step(index, carry):
            body(index)
            return carry

        if batches == 1:
            body(0)
        else:
            lax.fori_loop(0, batches, step, 0)

    def apart(body):
        def once(step, carry):
            body()
            return carry

        lax.fori_loop(0, 1 + lax.div(me, count), once, 0)

    def mark_leaving(step):
        rows = send_ref[pl.ds(step * batch, batch), :]
        index = jnp.concatenate([rows[i : i + 1, :] for i in range(batch)], axis=1)
        of_node = lax.broadcasted_iota(jnp.int32, (width, lane_count), 0) == (index & (width - 1))
        of_block = lax.broadcasted_iota(jnp.int32, (blocks, lane_count), 0) == (index >> shift)
        column = jnp.where(of_node, 1.0, 0.0).astype(BF16)
        leave_node_ref[step, 0:width, :] = column
        leave_node_ref[step, width : 2 * width, :] = column
        leave_block_ref[step] = jnp.where(of_block, 1.0, 0.0)

    def pick(step, source):
        tile = 256 if lane_count % 256 == 0 else lane_count
        splits = [jnp.concatenate(split(source[row]), axis=1) for row in range(3)]
        picked_rows = []
        for start in range(0, lane_count, tile):
            of_block = leave_block_ref[step, :, start : start + tile]
            values = []
            for row in range(3):
                found = jnp.dot(
                    splits[row], leave_node_ref[step, :, start : start + tile], preferred_element_type=F32
                )
                values.append(jnp.sum(of_block * found, axis=0, keepdims=True))
            picked_rows.append(values)
        return [jnp.concatenate([values[row] for values in picked_rows], axis=1) for row in range(3)]

    def gather_places(step):
        values = pick(step, pos_in)
        placed = jnp.concatenate(values + values, axis=0)
        for i in range(batch):
            peer = step * batch + i
            mine = slice(i * capacity, (i + 1) * capacity)
            out_pos[peer + 1, 0:3, 0:capacity] = placed[0:3, mine]
            out_pos[peer + 2, 0:3, capacity : 2 * capacity] = placed[0:3, mine]
            out_pos[peer, 3:6, 0:capacity] = placed[3:6, mine]

    def gather_speeds(step):
        speeds = jnp.concatenate(pick(step, vel_in), axis=0)
        for i in range(batch):
            out_vel[step * batch + i, 0:3, 0:capacity] = speeds[:, i * capacity : (i + 1) * capacity]

    def pos_copy(peer, there, many=1):
        return pltpu.make_async_remote_copy(
            src_ref=out_pos.at[pl.ds(peer, many), pl.ds(0, 6), :],
            dst_ref=in_pos.at[pl.ds(there, many), pl.ds(0, 6), :],
            send_sem=node_send_sem.at[0],
            recv_sem=node_recv_sem.at[0],
            device_id={"wall": neighbour(1)} if many > 1 else {"wall": peer - 1},
            device_id_type=MESH,
        )

    def vel_copy(peer, there, many=1):
        return pltpu.make_async_remote_copy(
            src_ref=out_vel.at[pl.ds(peer, many), pl.ds(0, 3), :],
            dst_ref=in_vel.at[pl.ds(there, many), pl.ds(0, 3), :],
            send_sem=node_send_sem.at[1],
            recv_sem=node_recv_sem.at[1],
            device_id={"wall": neighbour(1)} if many > 1 else {"wall": peer},
            device_id_type=MESH,
        )

    out_pos[...] = jnp.zeros(out_pos.shape, F32)
    def index_batch(step):
        rows = arrive_ref[pl.ds(step * batch, batch), :]
        slot_ids = lax.broadcasted_iota(jnp.int32, (1, capacity), 1)
        index_ref[1, step] = jnp.concatenate(
            [
                jnp.where(slot_ids < count_ref[0, step * batch + i], rows[i : i + 1, :], nodes)
                for i in range(batch)
            ],
            axis=1,
        )

    fetches["send"].wait()
    each_batch(mark_leaving)
    for name in ("arrive", "count"):
        fetches[name].wait()
    each_batch(index_batch)
    fetches["pos"].wait()
    for name in ("weight", "bonds", "mod", "vel"):
        fetches[name].start()
    for row in range(3):
        pos_in[row] = pos_raw[:, row, :]
    each_batch(gather_places)
    in_pos[me, 0:6, :] = out_pos[me + 1, 0:6, :]
    pl.semaphore_wait(barrier, peers - 1)

    def start_places(step, carry):
        pos_copy(lax.rem(me + step, count) + 1, me).start()
        return carry

    lax.fori_loop(1, peers, start_places, 0)

    for half in (0, 1):

        @pl.when(exists(half))
        def _():
            index_copy(half).start()

        @pl.when(jnp.logical_not(exists(half)))
        def _():
            index_ref[2 * half] = jnp.full(index_ref.shape[1:], nodes, jnp.int32)
            for slot in range(slots):
                ext_ref[slot, pl.ds(3 * LAYER * half, LAYER), :] = jnp.zeros((LAYER, 4 * width), BF16)

    for half in (0, 1):
        for row in range(3):
            put(0, half, row, pos_in[row, own(half), :].astype(BF16))
        send(0, half, 0, lanes_of(0, 3))

    lanes = lax.broadcasted_iota(jnp.int32, (LAYER, reach), 1)
    fetches["hor"].wait()
    padding = jnp.zeros((-nnz % 8, blocks), jnp.int32)
    horizon = jnp.transpose(jnp.concatenate([hor_ref[...], padding], axis=0))
    for half in range(2):
        local = horizon[half * LAYER : (half + 1) * LAYER] - (me * blocks - LAYER + half * LAYER)
        for j in range(nnz):
            hit = local[:, j : j + 1] == lanes
            onehot_ref[half, pl.ds(j * LAYER, LAYER), :] = jnp.where(hit, 1.0, 0.0).astype(BF16)

    fetches["vel"].wait()
    out_vel[...] = jnp.zeros(out_vel.shape, F32)
    for row in range(3):
        vel_in[row] = vel_raw[:, row, :]

    each_batch(gather_speeds)
    in_vel[me, 0:3, :] = out_vel[me, 0:3, :]

    def start_speeds(step, carry):
        vel_copy(lax.rem(me + step, count), me).start()
        return carry

    lax.fori_loop(1, peers, start_speeds, 0)

    for name in ("weight", "bonds", "mod"):
        fetches[name].wait()
    stiff = jnp.zeros((blocks, width), F32)
    ones = jnp.ones((16, width), BF16)
    for j in range(nnz):
        weight = jnp.transpose(weight_ref[j])
        wt_ref[j] = weight
        totals = jnp.dot(ones, weight, preferred_element_type=F32)[0:1, :]
        intact = raw_ref[j].astype(F32)
        intact_ref[j] = intact
        stiff = stiff + intact * totals
    stiff_ref[...] = stiff

    for half in (0, 1):

        @pl.when(exists(half))
        def _():
            index_copy(1 - half).wait_recv()

    def gain(ref, value):
        ref[...] = value if batches == 1 else ref[...] + value

    def clear(refs):
        if batches > 1:
            for ref in refs:
                ref[...] = jnp.zeros(ref.shape, F32)

    def columns_of(which):
        if isinstance(which, int):
            return pl.ds((0, 2 * width, width)[which], 2 * width if which == 1 else width)
        return pl.ds(pl.multiple_of(lax.div(which, 2) * width, width), width)

    def land(marks, columns, step):
        return lax.dot_general(
            marks, node_ref[step, columns, :], (((1,), (1,)), ((), ())), preferred_element_type=F32
        )

    def mark_batch(step):
        for which in range(3):
            index = index_ref[which, step]
            inside = index & (width - 1)
            block = index >> shift
            if which == 1:
                inside = inside + jnp.where(block >= LAYER, width, 0)
                block = jnp.where(block < 2 * LAYER, block & (LAYER - 1), 2 * LAYER)
            first = LAYER if which == 0 else 0
            columns = columns_of(which)
            of_node = lax.broadcasted_iota(jnp.int32, (columns.size, lane_count), 0) == inside
            node_ref[step, columns, :] = jnp.where(of_node, 1.0, 0.0).astype(BF16)
            of_block = lax.broadcasted_iota(jnp.int32, (LAYER, lane_count), 0) + first == block
            marks = jnp.where(of_block, 1.0, 0.0).astype(BF16)
            rows = pl.ds(which * LAYER, LAYER)
            block_ref[step, rows, :] = marks
            gain(hit_ref.at[:, columns], land(marks, columns, step))

    clear([hit_ref])
    each_batch(mark_batch)
    clear([landed_ref, ghost_landed_ref])

    for half in (0, 1):
        wait_halo(0, half, 0, lanes_of(0, 3))
        wait_sent(0, half, 0, lanes_of(0, 3))

    def places(step):
        bundles = [in_pos[step * batch + i, 0:6, :] for i in range(batch)]
        first = jnp.concatenate([bundle[:, 0:capacity] for bundle in bundles], axis=1)
        left = jnp.concatenate([bundle[0:3, capacity : 2 * capacity] for bundle in bundles], axis=1)
        return first[0:3], left, first[3:6]

    def ghost_rows(half):
        return pl.ds(pl.multiple_of(2 * half * LAYER, LAYER), LAYER)

    def land_ghost(step, half, values):
        rounded = values.astype(BF16)
        for row in range(3):
            ghost_spread_ref[pl.ds(row * LAYER, LAYER), :] = (
                block_ref[step, ghost_rows(half), :] * rounded[row : row + 1, :]
            )
        gain(ghost_landed_ref.at[half], land(ghost_spread_ref[...], columns_of(2 * half), step))

    def keep_ghost(half):
        hit = hit_ref[:, columns_of(2 * half)] > 0.5
        rows = pl.ds(pl.multiple_of(3 * LAYER * half, LAYER), LAYER)
        for row in range(3):
            landed = ghost_landed_ref[half, pl.ds(row * LAYER, LAYER), :]
            held_now = ext_ref[0, rows, lanes_of(row, 1)].astype(F32)
            ext_ref[0, rows, lanes_of(row, 1)] = jnp.where(hit, landed, held_now).astype(BF16)

    def spread(step, section, rounded):
        marks = block_ref[step, pl.ds(LAYER, LAYER), :]
        for row in range(3):
            spread_ref[pl.ds((3 * section + row) * LAYER, LAYER), :] = marks * rounded[row : row + 1, :]

    def land_section(step, section, pieces):
        for first, rows in pieces:
            rows_of = pl.ds((3 * section + first) * LAYER, rows * LAYER)
            gain(landed_ref.at[rows_of], land(spread_ref[rows_of, :], columns_of(1), step))

    def own_columns(half):
        return pl.ds(half * width, width)

    def own_hit(half):
        return hit_ref[:, pl.ds((2 + half) * width, width)] > 0.5

    def land_first(step):
        mine, left, right = places(step)
        spread(step, 0, mine.astype(BF16))
        land_ghost(step, slow, jnp.where(slow == 0, left, right))
        land_section(step, 0, ((0, 3),))

    def land_fast(step):
        _, left, right = places(step)
        land_ghost(step, fast, jnp.where(fast == 0, left, right))

    def land_rest(step):
        mine, _, _ = places(step)
        speeds = jnp.concatenate(
            [in_vel[step * batch + i, 0:3, :][:, 0:capacity] for i in range(batch)], axis=1
        )
        spread(step, 1, split(mine)[1])
        for part, rounded in enumerate(split(speeds)):
            spread(step, 2 + part, rounded)
        for section in (1, 2, 3):
            land_section(step, section, ((0, 3),))

    pos_copy(0, 0, peers - 1).wait_recv()

    @apart
    def _():
        each_batch(land_first)
        keep_ghost(slow)
        for half in (0, 1):
            hit = own_hit(half)
            for row in range(3):
                landed = landed_ref[pl.ds(row * LAYER, LAYER), own_columns(half)]
                put(0, half, row, jnp.where(hit, landed, get(0, half, row)).astype(BF16))

    group = 9 if nnz % 9 == 0 else nnz

    def contract(slot, first, rows, half):
        wide = rows * width
        start = half * LAYER if isinstance(half, int) else pl.multiple_of(half * LAYER, LAYER)
        source = ext_ref[slot, pl.ds(start, reach), lanes_of(first, rows)]
        for begin in range(0, nnz, group):
            part = pl.ds(begin * LAYER, group * LAYER)
            picked_ref[part, lanes_of(first, rows)] = jnp.dot(
                onehot_ref[half, part, :], source, preferred_element_type=F32
            ).astype(BF16)
        sums = [jnp.zeros((LAYER, width), F32) for _ in range(rows)]
        for j in range(nnz):
            part = pl.ds(j * LAYER, LAYER)
            mask = intact_ref[j, own(half), :]
            stacked = jnp.concatenate(
                [picked_ref[part, lanes_of(first + row, 1)] for row in range(rows)], axis=0
            )
            product = jnp.dot(stacked, wt_ref[j], preferred_element_type=F32)
            for row in range(rows):
                sums[row] = sums[row] + product[row * LAYER : (row + 1) * LAYER] * mask
        return sums

    def near_parts(parted):
        return ((0, 1), (1, 2)) if parted else ((0, 3),)

    def far_parts(parted):
        return ((0, 2), (2, 2)) if parted else ((0, 4),)

    def stretching(t, half, parted, waits):
        near, far = 2 * t, 2 * t + 1
        summed = []
        for part, (first, rows) in enumerate(near_parts(parted and waits)):
            if waits:
                wait_halo(near, half, part, lanes_of(first, rows))
            summed += contract(near, first, rows, half)
        scaling = mod_ref[own(half), :]
        stiffness = stiff_ref[own(half), :]
        rounded = [get(near, half, row) for row in range(3)]
        stretch = [scaling * (summed[row] - stiffness * rounded[row]) for row in range(3)]
        dilatation = (stretch[0] + stretch[1] + stretch[2]) / 3.0
        soften = 1.0 / (1.0 + dilatation * dilatation)
        soft_low = soften.astype(BF16)
        soft_wide = soft_low.astype(F32)
        put(far, half, 0, soft_low)
        for row in range(3):
            put(far, half, 1 + row, (soft_wide * rounded[row]).astype(BF16))
        for part, (first, rows) in enumerate(far_parts(parted)):
            send(far, half, part, lanes_of(first, rows))
        for row in range(3):
            stretch_ref[row, own(half), :] = stretch[row]
        soften_ref[own(half), :] = soften

    def pairing(t, half, parted, last):
        near, far = 2 * t, 2 * t + 1
        scaling = mod_ref[own(half), :]
        soften = soften_ref[own(half), :]
        kick = 0.5 * TIME_STEP if last else jnp.where(t == 0, 0.5 * TIME_STEP, TIME_STEP)
        paired = []
        for part, (first, rows) in enumerate(far_parts(parted)):
            wait_halo(far, half, part, lanes_of(first, rows))
            begin = max(len(paired) - 1, 0)
            paired += contract(far, first, rows, half)
            for row in range(begin, len(paired) - 1):
                rounded = get(near, half, row)
                force = 0.5 * (
                    scaling * (paired[1 + row] - rounded * paired[0]) + soften * stretch_ref[row, own(half), :]
                )
                speed = vel_ref[row, own(half), :] + kick * force
                if last:
                    vel_out[own(half), row, :] = speed
                else:
                    vel_ref[row, own(half), :] = speed
                    moved = pos_ref[row, own(half), :] + TIME_STEP * speed
                    pos_ref[row, own(half), :] = moved
                    put(near + 2, half, row, moved.astype(BF16))
            if not last:
                send(near + 2, half, part, lanes_of(*near_parts(parted)[part]))

    stretching(0, slow, True, False)

    @apart
    def _():
        each_batch(land_fast)
        keep_ghost(fast)

    stretching(0, fast, False, False)

    vel_copy(0, 0, peers - 1).wait_recv()
    each_batch(land_rest)
    for half in (0, 1):
        hit = own_hit(half)
        for row in range(3):
            parts = [
                landed_ref[pl.ds((3 * section + row) * LAYER, LAYER), own_columns(half)] for section in range(4)
            ]
            pos_ref[row, own(half), :] = jnp.where(hit, parts[0] + parts[1], pos_in[row, own(half), :])
            vel_ref[row, own(half), :] = jnp.where(hit, parts[2] + parts[3], vel_in[row, own(half), :])

    def substep(t, carry):
        pairing(t, fast, False, False)
        pairing(t, slow, True, False)
        stretching(t + 1, fast, False, True)
        stretching(t + 1, slow, True, True)
        return carry

    lax.fori_loop(0, SUBSTEPS, substep, 0)

    for row in range(3):
        pos_out[:, row, :] = pos_ref[row]
    pairing(SUBSTEPS, fast, False, True)
    pairing(SUBSTEPS, slow, True, True)

    pos_copy(0, 0, peers - 1).wait_send()
    vel_copy(0, 0, peers - 1).wait_send()
    for half in (0, 1):

        @pl.when(exists(half))
        def _():
            index_copy(half).wait_send()

    for slot in range(1, slots):
        for half, parted in ((fast, False), (slow, True)):
            parts = far_parts(parted) if slot % 2 else near_parts(parted)
            for part, (first, rows) in enumerate(parts):
                wait_sent(slot, half, part, lanes_of(first, rows))


def store_kernel(pos_in, vel_in, pos_out, vel_out, sems):
    copies = [
        pltpu.make_async_copy(pos_in, pos_out, sems.at[0]),
        pltpu.make_async_copy(vel_in, vel_out, sems.at[1]),
    ]
    for copy in copies:
        copy.start()
    for copy in copies:
        copy.wait()


def shards(
    displacement,
    velocity,
    send_list,
    arrive_list,
    recv_count,
    horizon_blocks,
    bond_intact,
    modulus,
    bond_weight,
):
    node_count = displacement.shape[1]
    blocks, nnz, width = bond_intact.shape
    peers, capacity = send_list.shape[1:]
    lane_count = math.gcd(PEER_BATCH, peers) * capacity
    batches = peers * capacity // lane_count
    bundle_width = 128 * pl.cdiv(2 * capacity, 128)
    slots = 2 * (SUBSTEPS + 1)
    vmem = pl.BlockSpec(memory_space=pltpu.VMEM)
    hbm = pl.BlockSpec(memory_space=pltpu.HBM)
    shape = jax.ShapeDtypeStruct((blocks, 3, width), F32)
    spare = VMEM_LIMIT - 2 * 4 * blocks * 4 * width
    final_position, final_speed = pl.pallas_call(
        functools.partial(force_kernel, blocks, width, nnz, peers),
        out_shape=(pltpu.VMEM(shape.shape, F32), pltpu.VMEM(shape.shape, F32)),
        in_specs=[hbm] * 9,
        out_specs=(vmem, vmem),
        scratch_shapes=[
            pltpu.VMEM((peers, capacity), jnp.int32),
            pltpu.VMEM((peers, capacity), jnp.int32),
            pltpu.SMEM((1, peers), jnp.int32),
            pltpu.VMEM((nnz, blocks), jnp.int32),
            pltpu.VMEM((blocks, width), F32),
            pltpu.VMEM((nnz, width, width), BF16),
            pltpu.VMEM((blocks, 3, width), F32),
            pltpu.VMEM((blocks, 3, width), F32),
            pltpu.VMEM((3, blocks, width), F32),
            pltpu.VMEM((3, blocks, width), F32),
            pltpu.VMEM((peers + 2, 8, bundle_width), F32),
            pltpu.VMEM((peers, 8, bundle_width), F32),
            pltpu.VMEM((peers, 8, bundle_width), F32),
            pltpu.VMEM((peers, 8, bundle_width), F32),
            pltpu.VMEM((batches, 2 * width, lane_count), BF16),
            pltpu.VMEM((batches, blocks, lane_count), F32),
            pltpu.VMEM((3, batches, 1, lane_count), jnp.int32),
            pltpu.VMEM((batches, 4 * width, lane_count), BF16),
            pltpu.VMEM((batches, 3 * LAYER, lane_count), BF16),
            pltpu.VMEM((LAYER, 4 * width), F32),
            pltpu.VMEM((12 * LAYER, lane_count), BF16),
            pltpu.VMEM((12 * LAYER, 2 * width), F32),
            pltpu.VMEM((3 * LAYER, lane_count), BF16),
            pltpu.VMEM((2, 3 * LAYER, width), F32),
            pltpu.VMEM((nnz, blocks, width), jnp.int32),
            pltpu.VMEM((nnz, blocks, width), F32),
            pltpu.VMEM((nnz, width, width), BF16),
            pltpu.VMEM((2, nnz * LAYER, 3 * LAYER), BF16),
            pltpu.VMEM((slots, 4 * LAYER, 4 * width), BF16),
            pltpu.VMEM((nnz * LAYER, 4 * width), BF16),
            pltpu.VMEM((blocks, width), F32),
            pltpu.VMEM((3, blocks, width), F32),
            pltpu.VMEM((blocks, width), F32),
            pltpu.VMEM((3, blocks, width), F32),
            pltpu.VMEM((3, blocks, width), F32),
            pltpu.SemaphoreType.DMA((slots, 2, 2)),
            pltpu.SemaphoreType.DMA((slots, 2, 2)),
            pltpu.SemaphoreType.DMA((2,)),
            pltpu.SemaphoreType.DMA((2,)),
            pltpu.SemaphoreType.DMA((2,)),
            pltpu.SemaphoreType.DMA((2,)),
            pltpu.SemaphoreType.DMA((9,)),
        ],
        compiler_params=pltpu.CompilerParams(
            collective_id=0, has_side_effects=True, vmem_limit_bytes=spare
        ),
        name="forces",
    )(
        send_list,
        arrive_list,
        recv_count,
        jnp.transpose(horizon_blocks),
        jnp.transpose(bond_intact, (1, 0, 2)),
        modulus.reshape(blocks, width),
        bond_weight,
        jnp.transpose(displacement.reshape(3, blocks, width), (1, 0, 2)),
        jnp.transpose(velocity.reshape(3, blocks, width), (1, 0, 2)),
    )
    final_position, final_speed = pl.pallas_call(
        store_kernel,
        out_shape=(shape, shape),
        in_specs=[pl.BlockSpec(memory_space=pl.ANY)] * 2,
        out_specs=(hbm, hbm),
        scratch_shapes=[pltpu.SemaphoreType.DMA((2,))],
        compiler_params=pltpu.CompilerParams(vmem_limit_bytes=1048576),
        name="store",
    )(final_position, final_speed)
    return tuple(jnp.transpose(x, (1, 0, 2)).reshape(3, node_count) for x in (final_position, final_speed))


def solution(mesh):
    in_specs = (
        P(None, ("parts", "wall")),
        P(None, ("parts", "wall")),
        P(("parts", "wall"), None, None),
        P(("parts", "wall"), None, None),
        P(("parts", "wall"), None),
        P(("parts", "wall"), None),
        P(("parts", "wall"), None, None),
        P(("parts", "wall")),
        P(),
    )
    out_specs = (P(None, ("parts", "wall")), P(None, ("parts", "wall")))
    return jax.shard_map(shards, mesh=mesh, in_specs=in_specs, out_specs=out_specs, check_vma=False)
```

```python
import functools
import math

import jax
import jax.numpy as jnp
from jax import lax
from jax.experimental import pallas as pl
from jax.experimental.pallas import tpu as pltpu
from jax.sharding import PartitionSpec as P

SUBSTEPS = 2
LAYER = 64
PEER_BATCH = 16
TIME_STEP = 0.25
VMEM_LIMIT = 66977792
MESH = pl.DeviceIdType.MESH
F32 = jnp.float32
BF16 = jnp.bfloat16


def force_kernel(
    blocks,
    width,
    nnz,
    peers,
    send_hbm,
    arrive_hbm,
    count_hbm,
    hor_hbm,
    bonds_hbm,
    mod_hbm,
    weight_hbm,
    pos_hbm,
    vel_hbm,
    pos_out,
    vel_out,
    send_ref,
    arrive_ref,
    count_ref,
    hor_ref,
    mod_ref,
    weight_ref,
    pos_raw,
    vel_raw,
    pos_in,
    vel_in,
    out_pos,
    in_pos,
    out_vel,
    in_vel,
    leave_node_ref,
    leave_block_ref,
    index_ref,
    node_ref,
    block_ref,
    hit_ref,
    spread_ref,
    landed_ref,
    ghost_spread_ref,
    ghost_landed_ref,
    raw_ref,
    intact_ref,
    wt_ref,
    onehot_ref,
    ext_ref,
    picked_ref,
    stiff_ref,
    stretch_ref,
    soften_ref,
    pos_ref,
    vel_ref,
    send_sem,
    recv_sem,
    index_send_sem,
    index_recv_sem,
    node_send_sem,
    node_recv_sem,
    fetch_sem,
):
    me = lax.axis_index("wall")
    count = lax.axis_size("wall")
    reach = 3 * LAYER
    slots = 2 * (SUBSTEPS + 1)
    slow = lax.rem(me, 2)
    fast = 1 - slow

    nodes = blocks * width
    capacity = send_ref.shape[1]
    shift = width.bit_length() - 1
    batch = math.gcd(PEER_BATCH, peers)
    batches = peers // batch
    lane_count = batch * capacity

    barrier = pltpu.get_barrier_semaphore()

    def greet(step, carry):
        pl.semaphore_signal(
            barrier, inc=1, device_id={"wall": lax.rem(me + step, count)}, device_id_type=MESH
        )
        return carry

    lax.fori_loop(1, peers, greet, 0)

    pairs = {
        "send": (send_hbm.at[0], send_ref),
        "pos": (pos_hbm, pos_raw),
        "arrive": (arrive_hbm.at[0], arrive_ref),
        "count": (count_hbm, count_ref),
        "hor": (hor_hbm, hor_ref),
        "weight": (weight_hbm, weight_ref),
        "bonds": (bonds_hbm, raw_ref),
        "mod": (mod_hbm, mod_ref),
        "vel": (vel_hbm, vel_raw),
    }
    fetches = {
        name: pltpu.make_async_copy(pair[0], pair[1], fetch_sem.at[i])
        for i, (name, pair) in enumerate(pairs.items())
    }
    for name in ("send", "pos", "arrive", "count", "hor"):
        fetches[name].start()

    def split(value):
        high = value.astype(BF16)
        low = (value - high.astype(F32)).astype(BF16)
        return high, low

    def neighbour(half):
        return lax.rem(me + count - 1 + 2 * half, count)

    def exists(half):
        there = me - 1 + 2 * half
        return jnp.logical_and(there >= 0, there < count)

    def own(half):
        return pl.ds(half * LAYER if isinstance(half, int) else pl.multiple_of(half * LAYER, LAYER), LAYER)

    def held(half):
        start = LAYER + half * LAYER
        return pl.ds(start if isinstance(half, int) else pl.multiple_of(start, LAYER), LAYER)

    def halo_copy(slot, half, part, lanes):
        start = 3 * LAYER * (1 - half)
        target = pl.ds(start if isinstance(half, int) else pl.multiple_of(start, LAYER), LAYER)
        return pltpu.make_async_remote_copy(
            src_ref=ext_ref.at[slot, held(half), lanes],
            dst_ref=ext_ref.at[slot, target, lanes],
            send_sem=send_sem.at[slot, half, part],
            recv_sem=recv_sem.at[slot, 1 - half, part],
            device_id={"wall": neighbour(half)},
            device_id_type=MESH,
        )

    def lanes_of(first, rows):
        return pl.ds(first * width, rows * width)

    def send(slot, half, part, lanes):
        @pl.when(exists(half))
        def _():
            halo_copy(slot, half, part, lanes).start()

    def wait_halo(slot, half, part, lanes):
        @pl.when(exists(half))
        def _():
            halo_copy(slot, 1 - half, part, lanes).wait_recv()

    def wait_sent(slot, half, part, lanes):
        @pl.when(exists(half))
        def _():
            halo_copy(slot, half, part, lanes).wait_send()

    def put(slot, half, column, value):
        ext_ref[slot, held(half), lanes_of(column, 1)] = value

    def get(slot, half, column):
        return ext_ref[slot, held(half), lanes_of(column, 1)].astype(F32)

    def index_copy(half):
        return pltpu.make_async_remote_copy(
            src_ref=index_ref.at[1],
            dst_ref=index_ref.at[2 - 2 * half],
            send_sem=index_send_sem.at[half],
            recv_sem=index_recv_sem.at[1 - half],
            device_id={"wall": neighbour(half)},
            device_id_type=MESH,
        )

    def each_batch(body):
        def step(index, carry):
            body(index)
            return carry

        if batches == 1:
            body(0)
        else:
            lax.fori_loop(0, batches, step, 0)

    def apart(body):
        def once(step, carry):
            body()
            return carry

        lax.fori_loop(0, 1 + lax.div(me, count), once, 0)

    def mark_leaving(step):
        rows = send_ref[pl.ds(step * batch, batch), :]
        index = jnp.concatenate([rows[i : i + 1, :] for i in range(batch)], axis=1)
        of_node = lax.broadcasted_iota(jnp.int32, (width, lane_count), 0) == (index & (width - 1))
        of_block = lax.broadcasted_iota(jnp.int32, (blocks, lane_count), 0) == (index >> shift)
        column = jnp.where(of_node, 1.0, 0.0).astype(BF16)
        leave_node_ref[step, 0:width, :] = column
        leave_node_ref[step, width : 2 * width, :] = column
        leave_block_ref[step] = jnp.where(of_block, 1.0, 0.0)

    def pick(step, source):
        tile = 256 if lane_count % 256 == 0 else lane_count
        splits = [jnp.concatenate(split(source[row]), axis=1) for row in range(3)]
        picked_rows = []
        for start in range(0, lane_count, tile):
            of_block = leave_block_ref[step, :, start : start + tile]
            values = []
            for row in range(3):
                found = jnp.dot(
                    splits[row], leave_node_ref[step, :, start : start + tile], preferred_element_type=F32
                )
                values.append(jnp.sum(of_block * found, axis=0, keepdims=True))
            picked_rows.append(values)
        return [jnp.concatenate([values[row] for values in picked_rows], axis=1) for row in range(3)]

    def gather_places(step):
        values = pick(step, pos_in)
        placed = jnp.concatenate(values + values, axis=0)
        for i in range(batch):
            peer = step * batch + i
            mine = slice(i * capacity, (i + 1) * capacity)
            out_pos[peer + 1, 0:3, 0:capacity] = placed[0:3, mine]
            out_pos[peer + 2, 0:3, capacity : 2 * capacity] = placed[0:3, mine]
            out_pos[peer, 3:6, 0:capacity] = placed[3:6, mine]

    def gather_speeds(step):
        speeds = jnp.concatenate(pick(step, vel_in), axis=0)
        for i in range(batch):
            out_vel[step * batch + i, 0:3, 0:capacity] = speeds[:, i * capacity : (i + 1) * capacity]

    def pos_copy(peer, there, many=1):
        return pltpu.make_async_remote_copy(
            src_ref=out_pos.at[pl.ds(peer, many), pl.ds(0, 6), :],
            dst_ref=in_pos.at[pl.ds(there, many), pl.ds(0, 6), :],
            send_sem=node_send_sem.at[0],
            recv_sem=node_recv_sem.at[0],
            device_id={"wall": neighbour(1)} if many > 1 else {"wall": peer - 1},
            device_id_type=MESH,
        )

    def vel_copy(peer, there, many=1):
        return pltpu.make_async_remote_copy(
            src_ref=out_vel.at[pl.ds(peer, many), pl.ds(0, 3), :],
            dst_ref=in_vel.at[pl.ds(there, many), pl.ds(0, 3), :],
            send_sem=node_send_sem.at[1],
            recv_sem=node_recv_sem.at[1],
            device_id={"wall": neighbour(1)} if many > 1 else {"wall": peer},
            device_id_type=MESH,
        )

    out_pos[...] = jnp.zeros(out_pos.shape, F32)
    def index_batch(step):
        rows = arrive_ref[pl.ds(step * batch, batch), :]
        slot_ids = lax.broadcasted_iota(jnp.int32, (1, capacity), 1)
        index_ref[1, step] = jnp.concatenate(
            [
                jnp.where(slot_ids < count_ref[0, step * batch + i], rows[i : i + 1, :], nodes)
                for i in range(batch)
            ],
            axis=1,
        )

    fetches["send"].wait()
    each_batch(mark_leaving)
    for name in ("arrive", "count"):
        fetches[name].wait()
    each_batch(index_batch)
    fetches["pos"].wait()
    for name in ("weight", "bonds", "mod", "vel"):
        fetches[name].start()
    for row in range(3):
        pos_in[row] = pos_raw[:, row, :]
    each_batch(gather_places)
    in_pos[me, 0:6, :] = out_pos[me + 1, 0:6, :]
    pl.semaphore_wait(barrier, peers - 1)

    def start_places(step, carry):
        pos_copy(lax.rem(me + step, count) + 1, me).start()
        return carry

    lax.fori_loop(1, peers, start_places, 0)

    for half in (0, 1):

        @pl.when(exists(half))
        def _():
            index_copy(half).start()

        @pl.when(jnp.logical_not(exists(half)))
        def _():
            index_ref[2 * half] = jnp.full(index_ref.shape[1:], nodes, jnp.int32)
            for slot in range(slots):
                ext_ref[slot, pl.ds(3 * LAYER * half, LAYER), :] = jnp.zeros((LAYER, 4 * width), BF16)

    for half in (0, 1):
        for row in range(3):
            put(0, half, row, pos_in[row, own(half), :].astype(BF16))
        send(0, half, 0, lanes_of(0, 3))

    lanes = lax.broadcasted_iota(jnp.int32, (LAYER, reach), 1)
    fetches["hor"].wait()
    padding = jnp.zeros((-nnz % 8, blocks), jnp.int32)
    horizon = jnp.transpose(jnp.concatenate([hor_ref[...], padding], axis=0))
    for half in range(2):
        local = horizon[half * LAYER : (half + 1) * LAYER] - (me * blocks - LAYER + half * LAYER)
        for j in range(nnz):
            hit = local[:, j : j + 1] == lanes
            onehot_ref[half, pl.ds(j * LAYER, LAYER), :] = jnp.where(hit, 1.0, 0.0).astype(BF16)

    fetches["vel"].wait()
    out_vel[...] = jnp.zeros(out_vel.shape, F32)
    for row in range(3):
        vel_in[row] = vel_raw[:, row, :]

    each_batch(gather_speeds)
    in_vel[me, 0:3, :] = out_vel[me, 0:3, :]

    def start_speeds(step, carry):
        vel_copy(lax.rem(me + step, count), me).start()
        return carry

    lax.fori_loop(1, peers, start_speeds, 0)

    for name in ("weight", "bonds", "mod"):
        fetches[name].wait()
    stiff = jnp.zeros((blocks, width), F32)
    ones = jnp.ones((16, width), BF16)
    for j in range(nnz):
        weight = jnp.transpose(weight_ref[j])
        wt_ref[j] = weight
        totals = jnp.dot(ones, weight, preferred_element_type=F32)[0:1, :]
        intact = raw_ref[j].astype(F32)
        intact_ref[j] = intact
        stiff = stiff + intact * totals
    stiff_ref[...] = stiff

    def gain(ref, value):
        ref[...] = value if batches == 1 else ref[...] + value

    def clear(refs):
        if batches > 1:
            for ref in refs:
                ref[...] = jnp.zeros(ref.shape, F32)

    def columns_of(which):
        if isinstance(which, int):
            return pl.ds((0, 2 * width, width)[which], 2 * width if which == 1 else width)
        return pl.ds(pl.multiple_of(lax.div(which, 2) * width, width), width)

    def land(marks, columns, step):
        return lax.dot_general(
            marks, node_ref[step, columns, :], (((1,), (1,)), ((), ())), preferred_element_type=F32
        )

    def mark_batch(step, which_ones):
        for which in which_ones:
            index = index_ref[which, step]
            inside = index & (width - 1)
            block = index >> shift
            if which == 1:
                inside = inside + jnp.where(block >= LAYER, width, 0)
                block = jnp.where(block < 2 * LAYER, block & (LAYER - 1), 2 * LAYER)
            first = LAYER if which == 0 else 0
            columns = columns_of(which)
            of_node = lax.broadcasted_iota(jnp.int32, (columns.size, lane_count), 0) == inside
            node_ref[step, columns, :] = jnp.where(of_node, 1.0, 0.0).astype(BF16)
            of_block = lax.broadcasted_iota(jnp.int32, (LAYER, lane_count), 0) + first == block
            marks = jnp.where(of_block, 1.0, 0.0).astype(BF16)
            rows = pl.ds(which * LAYER, LAYER)
            block_ref[step, rows, :] = marks
            gain(hit_ref.at[:, columns], land(marks, columns, step))

    clear([hit_ref, landed_ref, ghost_landed_ref])
    each_batch(lambda step: mark_batch(step, (1,)))
    for half in (0, 1):

        @pl.when(exists(half))
        def _():
            index_copy(1 - half).wait_recv()

    each_batch(lambda step: mark_batch(step, (0, 2)))

    for half in (0, 1):
        wait_halo(0, half, 0, lanes_of(0, 3))
        wait_sent(0, half, 0, lanes_of(0, 3))

    def places(step):
        bundles = [in_pos[step * batch + i, 0:6, :] for i in range(batch)]
        first = jnp.concatenate([bundle[:, 0:capacity] for bundle in bundles], axis=1)
        left = jnp.concatenate([bundle[0:3, capacity : 2 * capacity] for bundle in bundles], axis=1)
        return first[0:3], left, first[3:6]

    def ghost_rows(half):
        return pl.ds(pl.multiple_of(2 * half * LAYER, LAYER), LAYER)

    def land_ghost(step, half, values):
        rounded = values.astype(BF16)
        for row in range(3):
            ghost_spread_ref[pl.ds(row * LAYER, LAYER), :] = (
                block_ref[step, ghost_rows(half), :] * rounded[row : row + 1, :]
            )
        gain(ghost_landed_ref.at[half], land(ghost_spread_ref[...], columns_of(2 * half), step))

    def keep_ghost(half):
        hit = hit_ref[:, columns_of(2 * half)] > 0.5
        rows = pl.ds(pl.multiple_of(3 * LAYER * half, LAYER), LAYER)
        for row in range(3):
            landed = ghost_landed_ref[half, pl.ds(row * LAYER, LAYER), :]
            held_now = ext_ref[0, rows, lanes_of(row, 1)].astype(F32)
            ext_ref[0, rows, lanes_of(row, 1)] = jnp.where(hit, landed, held_now).astype(BF16)

    def spread(step, section, rounded):
        marks = block_ref[step, pl.ds(LAYER, LAYER), :]
        for row in range(3):
            spread_ref[pl.ds((3 * section + row) * LAYER, LAYER), :] = marks * rounded[row : row + 1, :]

    def land_section(step, section, pieces):
        for first, rows in pieces:
            rows_of = pl.ds((3 * section + first) * LAYER, rows * LAYER)
            gain(landed_ref.at[rows_of], land(spread_ref[rows_of, :], columns_of(1), step))

    def own_columns(half):
        return pl.ds(half * width, width)

    def own_hit(half):
        return hit_ref[:, pl.ds((2 + half) * width, width)] > 0.5

    def land_first(step):
        mine, left, right = places(step)
        spread(step, 0, mine.astype(BF16))
        land_ghost(step, slow, jnp.where(slow == 0, left, right))
        land_section(step, 0, ((0, 3),))

    def land_fast(step):
        _, left, right = places(step)
        land_ghost(step, fast, jnp.where(fast == 0, left, right))

    def land_rest(step):
        mine, _, _ = places(step)
        speeds = jnp.concatenate(
            [in_vel[step * batch + i, 0:3, :][:, 0:capacity] for i in range(batch)], axis=1
        )
        spread(step, 1, split(mine)[1])
        for part, rounded in enumerate(split(speeds)):
            spread(step, 2 + part, rounded)
        for section in (1, 2, 3):
            land_section(step, section, ((0, 3),))

    pos_copy(0, 0, peers - 1).wait_recv()

    @apart
    def _():
        each_batch(land_first)
        keep_ghost(slow)
        for half in (0, 1):
            hit = own_hit(half)
            for row in range(3):
                landed = landed_ref[pl.ds(row * LAYER, LAYER), own_columns(half)]
                put(0, half, row, jnp.where(hit, landed, get(0, half, row)).astype(BF16))

    group = 9 if nnz % 9 == 0 else nnz

    def contract(slot, first, rows, half):
        wide = rows * width
        start = half * LAYER if isinstance(half, int) else pl.multiple_of(half * LAYER, LAYER)
        source = ext_ref[slot, pl.ds(start, reach), lanes_of(first, rows)]
        for begin in range(0, nnz, group):
            part = pl.ds(begin * LAYER, group * LAYER)
            picked_ref[part, lanes_of(first, rows)] = jnp.dot(
                onehot_ref[half, part, :], source, preferred_element_type=F32
            ).astype(BF16)
        sums = [jnp.zeros((LAYER, width), F32) for _ in range(rows)]
        for j in range(nnz):
            part = pl.ds(j * LAYER, LAYER)
            mask = intact_ref[j, own(half), :]
            stacked = jnp.concatenate(
                [picked_ref[part, lanes_of(first + row, 1)] for row in range(rows)], axis=0
            )
            product = jnp.dot(stacked, wt_ref[j], preferred_element_type=F32)
            for row in range(rows):
                sums[row] = sums[row] + product[row * LAYER : (row + 1) * LAYER] * mask
        return sums

    def near_parts(parted):
        return ((0, 1), (1, 2)) if parted else ((0, 3),)

    def far_parts(parted):
        return ((0, 2), (2, 2)) if parted else ((0, 4),)

    def stretching(t, half, parted, waits):
        near, far = 2 * t, 2 * t + 1
        summed = []
        for part, (first, rows) in enumerate(near_parts(parted and waits)):
            if waits:
                wait_halo(near, half, part, lanes_of(first, rows))
            summed += contract(near, first, rows, half)
        scaling = mod_ref[own(half), :]
        stiffness = stiff_ref[own(half), :]
        rounded = [get(near, half, row) for row in range(3)]
        stretch = [scaling * (summed[row] - stiffness * rounded[row]) for row in range(3)]
        dilatation = (stretch[0] + stretch[1] + stretch[2]) / 3.0
        soften = 1.0 / (1.0 + dilatation * dilatation)
        soft_low = soften.astype(BF16)
        soft_wide = soft_low.astype(F32)
        put(far, half, 0, soft_low)
        for row in range(3):
            put(far, half, 1 + row, (soft_wide * rounded[row]).astype(BF16))
        send(far, half, 0, lanes_of(0, 1))
        for row in range(3):
            stretch_ref[row, own(half), :] = stretch[row]
        soften_ref[own(half), :] = soften

    def pairing(t, half, parted, last):
        near, far = 2 * t, 2 * t + 1
        scaling = mod_ref[own(half), :]
        soften = soften_ref[own(half), :]
        kick = 0.5 * TIME_STEP if last else jnp.where(t == 0, 0.5 * TIME_STEP, TIME_STEP)
        wait_halo(far, half, 0, lanes_of(0, 1))
        ghost = pl.ds(pl.multiple_of(3 * LAYER * half, LAYER), LAYER)
        soft_wide = ext_ref[far, ghost, lanes_of(0, 1)].astype(F32)
        for row in range(3):
            rounded = ext_ref[near, ghost, lanes_of(row, 1)].astype(F32)
            ext_ref[far, ghost, lanes_of(1 + row, 1)] = (soft_wide * rounded).astype(BF16)
        paired = []
        for part, (first, rows) in enumerate(far_parts(parted)):
            begin = max(len(paired) - 1, 0)
            paired += contract(far, first, rows, half)
            for row in range(begin, len(paired) - 1):
                rounded = get(near, half, row)
                force = 0.5 * (
                    scaling * (paired[1 + row] - rounded * paired[0]) + soften * stretch_ref[row, own(half), :]
                )
                speed = vel_ref[row, own(half), :] + kick * force
                if last:
                    vel_out[own(half), row, :] = speed
                else:
                    vel_ref[row, own(half), :] = speed
                    moved = pos_ref[row, own(half), :] + TIME_STEP * speed
                    pos_ref[row, own(half), :] = moved
                    put(near + 2, half, row, moved.astype(BF16))
            if not last:
                send(near + 2, half, part, lanes_of(*near_parts(parted)[part]))

    stretching(0, slow, True, False)

    @apart
    def _():
        each_batch(land_fast)
        keep_ghost(fast)

    stretching(0, fast, False, False)

    vel_copy(0, 0, peers - 1).wait_recv()
    each_batch(land_rest)
    for half in (0, 1):
        hit = own_hit(half)
        for row in range(3):
            parts = [
                landed_ref[pl.ds((3 * section + row) * LAYER, LAYER), own_columns(half)] for section in range(4)
            ]
            pos_ref[row, own(half), :] = jnp.where(hit, parts[0] + parts[1], pos_in[row, own(half), :])
            vel_ref[row, own(half), :] = jnp.where(hit, parts[2] + parts[3], vel_in[row, own(half), :])

    def substep(t, carry):
        pairing(t, fast, False, False)
        pairing(t, slow, True, False)
        stretching(t + 1, fast, False, True)
        stretching(t + 1, slow, True, True)
        return carry

    lax.fori_loop(0, SUBSTEPS, substep, 0)

    for row in range(3):
        pos_out[:, row, :] = pos_ref[row]
    pairing(SUBSTEPS, fast, False, True)
    pairing(SUBSTEPS, slow, False, True)

    pos_copy(0, 0, peers - 1).wait_send()
    vel_copy(0, 0, peers - 1).wait_send()
    for half in (0, 1):

        @pl.when(exists(half))
        def _():
            index_copy(half).wait_send()

    for slot in range(1, slots):
        for half, parted in ((fast, False), (slow, True)):
            parts = ((0, 1),) if slot % 2 else near_parts(parted)
            for part, (first, rows) in enumerate(parts):
                wait_sent(slot, half, part, lanes_of(first, rows))


def store_kernel(pos_in, vel_in, pos_out, vel_out, sems):
    copies = [
        pltpu.make_async_copy(pos_in, pos_out, sems.at[0]),
        pltpu.make_async_copy(vel_in, vel_out, sems.at[1]),
    ]
    for copy in copies:
        copy.start()
    for copy in copies:
        copy.wait()


def shards(
    displacement,
    velocity,
    send_list,
    arrive_list,
    recv_count,
    horizon_blocks,
    bond_intact,
    modulus,
    bond_weight,
):
    node_count = displacement.shape[1]
    blocks, nnz, width = bond_intact.shape
    peers, capacity = send_list.shape[1:]
    lane_count = math.gcd(PEER_BATCH, peers) * capacity
    batches = peers * capacity // lane_count
    bundle_width = 128 * pl.cdiv(2 * capacity, 128)
    slots = 2 * (SUBSTEPS + 1)
    vmem = pl.BlockSpec(memory_space=pltpu.VMEM)
    hbm = pl.BlockSpec(memory_space=pltpu.HBM)
    shape = jax.ShapeDtypeStruct((blocks, 3, width), F32)
    spare = VMEM_LIMIT - 2 * 4 * blocks * 4 * width
    final_position, final_speed = pl.pallas_call(
        functools.partial(force_kernel, blocks, width, nnz, peers),
        out_shape=(pltpu.VMEM(shape.shape, F32), pltpu.VMEM(shape.shape, F32)),
        in_specs=[hbm] * 9,
        out_specs=(vmem, vmem),
        scratch_shapes=[
            pltpu.VMEM((peers, capacity), jnp.int32),
            pltpu.VMEM((peers, capacity), jnp.int32),
            pltpu.SMEM((1, peers), jnp.int32),
            pltpu.VMEM((nnz, blocks), jnp.int32),
            pltpu.VMEM((blocks, width), F32),
            pltpu.VMEM((nnz, width, width), BF16),
            pltpu.VMEM((blocks, 3, width), F32),
            pltpu.VMEM((blocks, 3, width), F32),
            pltpu.VMEM((3, blocks, width), F32),
            pltpu.VMEM((3, blocks, width), F32),
            pltpu.VMEM((peers + 2, 8, bundle_width), F32),
            pltpu.VMEM((peers, 8, bundle_width), F32),
            pltpu.VMEM((peers, 8, bundle_width), F32),
            pltpu.VMEM((peers, 8, bundle_width), F32),
            pltpu.VMEM((batches, 2 * width, lane_count), BF16),
            pltpu.VMEM((batches, blocks, lane_count), F32),
            pltpu.VMEM((3, batches, 1, lane_count), jnp.int32),
            pltpu.VMEM((batches, 4 * width, lane_count), BF16),
            pltpu.VMEM((batches, 3 * LAYER, lane_count), BF16),
            pltpu.VMEM((LAYER, 4 * width), F32),
            pltpu.VMEM((12 * LAYER, lane_count), BF16),
            pltpu.VMEM((12 * LAYER, 2 * width), F32),
            pltpu.VMEM((3 * LAYER, lane_count), BF16),
            pltpu.VMEM((2, 3 * LAYER, width), F32),
            pltpu.VMEM((nnz, blocks, width), jnp.int32),
            pltpu.VMEM((nnz, blocks, width), F32),
            pltpu.VMEM((nnz, width, width), BF16),
            pltpu.VMEM((2, nnz * LAYER, 3 * LAYER), BF16),
            pltpu.VMEM((slots, 4 * LAYER, 4 * width), BF16),
            pltpu.VMEM((nnz * LAYER, 4 * width), BF16),
            pltpu.VMEM((blocks, width), F32),
            pltpu.VMEM((3, blocks, width), F32),
            pltpu.VMEM((blocks, width), F32),
            pltpu.VMEM((3, blocks, width), F32),
            pltpu.VMEM((3, blocks, width), F32),
            pltpu.SemaphoreType.DMA((slots, 2, 2)),
            pltpu.SemaphoreType.DMA((slots, 2, 2)),
            pltpu.SemaphoreType.DMA((2,)),
            pltpu.SemaphoreType.DMA((2,)),
            pltpu.SemaphoreType.DMA((2,)),
            pltpu.SemaphoreType.DMA((2,)),
            pltpu.SemaphoreType.DMA((9,)),
        ],
        compiler_params=pltpu.CompilerParams(
            collective_id=0, has_side_effects=True, vmem_limit_bytes=spare
        ),
        name="forces",
    )(
        send_list,
        arrive_list,
        recv_count,
        jnp.transpose(horizon_blocks),
        jnp.transpose(bond_intact, (1, 0, 2)),
        modulus.reshape(blocks, width),
        bond_weight,
        jnp.transpose(displacement.reshape(3, blocks, width), (1, 0, 2)),
        jnp.transpose(velocity.reshape(3, blocks, width), (1, 0, 2)),
    )
    final_position, final_speed = pl.pallas_call(
        store_kernel,
        out_shape=(shape, shape),
        in_specs=[pl.BlockSpec(memory_space=pl.ANY)] * 2,
        out_specs=(hbm, hbm),
        scratch_shapes=[pltpu.SemaphoreType.DMA((2,))],
        compiler_params=pltpu.CompilerParams(vmem_limit_bytes=1048576),
        name="store",
    )(final_position, final_speed)
    return tuple(jnp.transpose(x, (1, 0, 2)).reshape(3, node_count) for x in (final_position, final_speed))


def solution(mesh):
    in_specs = (
        P(None, ("parts", "wall")),
        P(None, ("parts", "wall")),
        P(("parts", "wall"), None, None),
        P(("parts", "wall"), None, None),
        P(("parts", "wall"), None),
        P(("parts", "wall"), None),
        P(("parts", "wall"), None, None),
        P(("parts", "wall")),
        P(),
    )
    out_specs = (P(None, ("parts", "wall")), P(None, ("parts", "wall")))
    return jax.shard_map(shards, mesh=mesh, in_specs=in_specs, out_specs=out_specs, check_vma=False)
```

```python
import functools
import math

import jax
import jax.numpy as jnp
from jax import lax
from jax.experimental import pallas as pl
from jax.experimental.pallas import tpu as pltpu
from jax.sharding import PartitionSpec as P

SUBSTEPS = 2
LAYER = 64
PEER_BATCH = 16
TIME_STEP = 0.25
VMEM_LIMIT = 66977792
MESH = pl.DeviceIdType.MESH
F32 = jnp.float32
BF16 = jnp.bfloat16


def force_kernel(
    blocks,
    width,
    nnz,
    peers,
    send_hbm,
    arrive_hbm,
    count_hbm,
    hor_hbm,
    bonds_hbm,
    mod_hbm,
    weight_hbm,
    pos_hbm,
    vel_hbm,
    pos_out,
    vel_out,
    send_ref,
    arrive_ref,
    count_ref,
    hor_ref,
    mod_ref,
    weight_ref,
    pos_raw,
    vel_raw,
    pos_in,
    vel_in,
    out_pos,
    in_pos,
    out_vel,
    in_vel,
    leave_node_ref,
    leave_block_ref,
    index_ref,
    node_ref,
    block_ref,
    hit_ref,
    spread_ref,
    landed_ref,
    ghost_spread_ref,
    ghost_landed_ref,
    raw_ref,
    intact_ref,
    wt_ref,
    onehot_ref,
    ext_ref,
    picked_ref,
    soft_picked_ref,
    stiff_ref,
    stretch_ref,
    soften_ref,
    pos_ref,
    vel_ref,
    send_sem,
    recv_sem,
    index_send_sem,
    index_recv_sem,
    node_send_sem,
    node_recv_sem,
    fetch_sem,
):
    me = lax.axis_index("wall")
    count = lax.axis_size("wall")
    reach = 3 * LAYER
    slots = 2 * (SUBSTEPS + 1)
    slow = lax.rem(me, 2)
    fast = 1 - slow

    nodes = blocks * width
    capacity = send_ref.shape[1]
    shift = width.bit_length() - 1
    batch = math.gcd(PEER_BATCH, peers)
    batches = peers // batch
    lane_count = batch * capacity

    barrier = pltpu.get_barrier_semaphore()

    def greet(step, carry):
        pl.semaphore_signal(
            barrier, inc=1, device_id={"wall": lax.rem(me + step, count)}, device_id_type=MESH
        )
        return carry

    lax.fori_loop(1, peers, greet, 0)

    pairs = {
        "send": (send_hbm.at[0], send_ref),
        "pos": (pos_hbm, pos_raw),
        "arrive": (arrive_hbm.at[0], arrive_ref),
        "count": (count_hbm, count_ref),
        "hor": (hor_hbm, hor_ref),
        "weight": (weight_hbm, weight_ref),
        "bonds": (bonds_hbm, raw_ref),
        "mod": (mod_hbm, mod_ref),
        "vel": (vel_hbm, vel_raw),
    }
    fetches = {
        name: pltpu.make_async_copy(pair[0], pair[1], fetch_sem.at[i])
        for i, (name, pair) in enumerate(pairs.items())
    }
    for name in ("send", "pos", "arrive", "count", "hor"):
        fetches[name].start()

    def split(value):
        high = value.astype(BF16)
        low = (value - high.astype(F32)).astype(BF16)
        return high, low

    def neighbour(half):
        return lax.rem(me + count - 1 + 2 * half, count)

    def exists(half):
        there = me - 1 + 2 * half
        return jnp.logical_and(there >= 0, there < count)

    def own(half):
        return pl.ds(half * LAYER if isinstance(half, int) else pl.multiple_of(half * LAYER, LAYER), LAYER)

    def held(half):
        start = LAYER + half * LAYER
        return pl.ds(start if isinstance(half, int) else pl.multiple_of(start, LAYER), LAYER)

    def halo_copy(slot, half, part, lanes):
        start = 3 * LAYER * (1 - half)
        target = pl.ds(start if isinstance(half, int) else pl.multiple_of(start, LAYER), LAYER)
        return pltpu.make_async_remote_copy(
            src_ref=ext_ref.at[slot, held(half), lanes],
            dst_ref=ext_ref.at[slot, target, lanes],
            send_sem=send_sem.at[slot, half, part],
            recv_sem=recv_sem.at[slot, 1 - half, part],
            device_id={"wall": neighbour(half)},
            device_id_type=MESH,
        )

    def lanes_of(first, rows):
        return pl.ds(first * width, rows * width)

    def send(slot, half, part, lanes):
        @pl.when(exists(half))
        def _():
            halo_copy(slot, half, part, lanes).start()

    def wait_halo(slot, half, part, lanes):
        @pl.when(exists(half))
        def _():
            halo_copy(slot, 1 - half, part, lanes).wait_recv()

    def wait_sent(slot, half, part, lanes):
        @pl.when(exists(half))
        def _():
            halo_copy(slot, half, part, lanes).wait_send()

    def put(slot, half, column, value):
        ext_ref[slot, held(half), lanes_of(column, 1)] = value

    def get(slot, half, column):
        return ext_ref[slot, held(half), lanes_of(column, 1)].astype(F32)

    def index_copy(half):
        return pltpu.make_async_remote_copy(
            src_ref=index_ref.at[1],
            dst_ref=index_ref.at[2 - 2 * half],
            send_sem=index_send_sem.at[half],
            recv_sem=index_recv_sem.at[1 - half],
            device_id={"wall": neighbour(half)},
            device_id_type=MESH,
        )

    def each_batch(body):
        def step(index, carry):
            body(index)
            return carry

        if batches == 1:
            body(0)
        else:
            lax.fori_loop(0, batches, step, 0)

    def apart(body):
        def once(step, carry):
            body()
            return carry

        lax.fori_loop(0, 1 + lax.div(me, count), once, 0)

    def mark_leaving(step):
        rows = send_ref[pl.ds(step * batch, batch), :]
        index = jnp.concatenate([rows[i : i + 1, :] for i in range(batch)], axis=1)
        of_node = lax.broadcasted_iota(jnp.int32, (width, lane_count), 0) == (index & (width - 1))
        of_block = lax.broadcasted_iota(jnp.int32, (blocks, lane_count), 0) == (index >> shift)
        column = jnp.where(of_node, 1.0, 0.0).astype(BF16)
        leave_node_ref[step, 0:width, :] = column
        leave_node_ref[step, width : 2 * width, :] = column
        leave_block_ref[step] = jnp.where(of_block, 1.0, 0.0)

    def pick(step, source):
        tile = 256 if lane_count % 256 == 0 else lane_count
        splits = [jnp.concatenate(split(source[row]), axis=1) for row in range(3)]
        picked_rows = []
        for start in range(0, lane_count, tile):
            of_block = leave_block_ref[step, :, start : start + tile]
            values = []
            for row in range(3):
                found = jnp.dot(
                    splits[row], leave_node_ref[step, :, start : start + tile], preferred_element_type=F32
                )
                values.append(jnp.sum(of_block * found, axis=0, keepdims=True))
            picked_rows.append(values)
        return [jnp.concatenate([values[row] for values in picked_rows], axis=1) for row in range(3)]

    def gather_places(step):
        values = pick(step, pos_in)
        placed = jnp.concatenate(values + values, axis=0)
        for i in range(batch):
            peer = step * batch + i
            mine = slice(i * capacity, (i + 1) * capacity)
            out_pos[peer + 1, 0:3, 0:capacity] = placed[0:3, mine]
            out_pos[peer + 2, 0:3, capacity : 2 * capacity] = placed[0:3, mine]
            out_pos[peer, 3:6, 0:capacity] = placed[3:6, mine]

    def gather_speeds(step):
        speeds = jnp.concatenate(pick(step, vel_in), axis=0)
        for i in range(batch):
            out_vel[step * batch + i, 0:3, 0:capacity] = speeds[:, i * capacity : (i + 1) * capacity]

    def pos_copy(peer, there, many=1):
        return pltpu.make_async_remote_copy(
            src_ref=out_pos.at[pl.ds(peer, many), pl.ds(0, 6), :],
            dst_ref=in_pos.at[pl.ds(there, many), pl.ds(0, 6), :],
            send_sem=node_send_sem.at[0],
            recv_sem=node_recv_sem.at[0],
            device_id={"wall": neighbour(1)} if many > 1 else {"wall": peer - 1},
            device_id_type=MESH,
        )

    def vel_copy(peer, there, many=1):
        return pltpu.make_async_remote_copy(
            src_ref=out_vel.at[pl.ds(peer, many), pl.ds(0, 3), :],
            dst_ref=in_vel.at[pl.ds(there, many), pl.ds(0, 3), :],
            send_sem=node_send_sem.at[1],
            recv_sem=node_recv_sem.at[1],
            device_id={"wall": neighbour(1)} if many > 1 else {"wall": peer},
            device_id_type=MESH,
        )

    out_pos[...] = jnp.zeros(out_pos.shape, F32)
    def index_batch(step):
        rows = arrive_ref[pl.ds(step * batch, batch), :]
        slot_ids = lax.broadcasted_iota(jnp.int32, (1, capacity), 1)
        index_ref[1, step] = jnp.concatenate(
            [
                jnp.where(slot_ids < count_ref[0, step * batch + i], rows[i : i + 1, :], nodes)
                for i in range(batch)
            ],
            axis=1,
        )

    fetches["send"].wait()
    each_batch(mark_leaving)
    for name in ("arrive", "count"):
        fetches[name].wait()
    each_batch(index_batch)
    fetches["pos"].wait()
    for name in ("weight", "bonds", "mod", "vel"):
        fetches[name].start()
    for row in range(3):
        pos_in[row] = pos_raw[:, row, :]
    each_batch(gather_places)
    in_pos[me, 0:6, :] = out_pos[me + 1, 0:6, :]
    pl.semaphore_wait(barrier, peers - 1)

    def start_places(step, carry):
        pos_copy(lax.rem(me + step, count) + 1, me).start()
        return carry

    lax.fori_loop(1, peers, start_places, 0)

    for half in (0, 1):

        @pl.when(exists(half))
        def _():
            index_copy(half).start()

        @pl.when(jnp.logical_not(exists(half)))
        def _():
            index_ref[2 * half] = jnp.full(index_ref.shape[1:], nodes, jnp.int32)
            for slot in range(slots):
                ext_ref[slot, pl.ds(3 * LAYER * half, LAYER), :] = jnp.zeros((LAYER, 3 * width), BF16)

    for half in (0, 1):
        for row in range(3):
            put(0, half, row, pos_in[row, own(half), :].astype(BF16))
        send(0, half, 0, lanes_of(0, 3))

    lanes = lax.broadcasted_iota(jnp.int32, (LAYER, reach), 1)
    fetches["hor"].wait()
    padding = jnp.zeros((-nnz % 8, blocks), jnp.int32)
    horizon = jnp.transpose(jnp.concatenate([hor_ref[...], padding], axis=0))
    for half in range(2):
        local = horizon[half * LAYER : (half + 1) * LAYER] - (me * blocks - LAYER + half * LAYER)
        for j in range(nnz):
            hit = local[:, j : j + 1] == lanes
            onehot_ref[half, pl.ds(j * LAYER, LAYER), :] = jnp.where(hit, 1.0, 0.0).astype(BF16)

    fetches["vel"].wait()
    out_vel[...] = jnp.zeros(out_vel.shape, F32)
    for row in range(3):
        vel_in[row] = vel_raw[:, row, :]

    each_batch(gather_speeds)
    in_vel[me, 0:3, :] = out_vel[me, 0:3, :]

    def start_speeds(step, carry):
        vel_copy(lax.rem(me + step, count), me).start()
        return carry

    lax.fori_loop(1, peers, start_speeds, 0)

    for name in ("weight", "bonds", "mod"):
        fetches[name].wait()
    stiff = jnp.zeros((blocks, width), F32)
    ones = jnp.ones((16, width), BF16)
    for j in range(nnz):
        weight = jnp.transpose(weight_ref[j])
        wt_ref[j] = weight
        totals = jnp.dot(ones, weight, preferred_element_type=F32)[0:1, :]
        intact = raw_ref[j].astype(F32)
        intact_ref[j] = intact
        stiff = stiff + intact * totals
    stiff_ref[...] = stiff

    def gain(ref, value):
        ref[...] = value if batches == 1 else ref[...] + value

    def clear(refs):
        if batches > 1:
            for ref in refs:
                ref[...] = jnp.zeros(ref.shape, F32)

    def columns_of(which):
        if isinstance(which, int):
            return pl.ds((0, 2 * width, width)[which], 2 * width if which == 1 else width)
        return pl.ds(pl.multiple_of(lax.div(which, 2) * width, width), width)

    def land(marks, columns, step):
        return lax.dot_general(
            marks, node_ref[step, columns, :], (((1,), (1,)), ((), ())), preferred_element_type=F32
        )

    def mark_batch(step, which_ones):
        for which in which_ones:
            index = index_ref[which, step]
            inside = index & (width - 1)
            block = index >> shift
            if which == 1:
                inside = inside + jnp.where(block >= LAYER, width, 0)
                block = jnp.where(block < 2 * LAYER, block & (LAYER - 1), 2 * LAYER)
            first = LAYER if which == 0 else 0
            columns = columns_of(which)
            of_node = lax.broadcasted_iota(jnp.int32, (columns.size, lane_count), 0) == inside
            node_ref[step, columns, :] = jnp.where(of_node, 1.0, 0.0).astype(BF16)
            of_block = lax.broadcasted_iota(jnp.int32, (LAYER, lane_count), 0) + first == block
            marks = jnp.where(of_block, 1.0, 0.0).astype(BF16)
            rows = pl.ds(which * LAYER, LAYER)
            block_ref[step, rows, :] = marks
            gain(hit_ref.at[:, columns], land(marks, columns, step))

    clear([hit_ref, landed_ref, ghost_landed_ref])
    each_batch(lambda step: mark_batch(step, (1,)))
    for half in (0, 1):

        @pl.when(exists(half))
        def _():
            index_copy(1 - half).wait_recv()

    each_batch(lambda step: mark_batch(step, (0, 2)))

    for half in (0, 1):
        wait_halo(0, half, 0, lanes_of(0, 3))
        wait_sent(0, half, 0, lanes_of(0, 3))

    def places(step):
        bundles = [in_pos[step * batch + i, 0:6, :] for i in range(batch)]
        first = jnp.concatenate([bundle[:, 0:capacity] for bundle in bundles], axis=1)
        left = jnp.concatenate([bundle[0:3, capacity : 2 * capacity] for bundle in bundles], axis=1)
        return first[0:3], left, first[3:6]

    def ghost_rows(half):
        return pl.ds(pl.multiple_of(2 * half * LAYER, LAYER), LAYER)

    def land_ghost(step, half, values):
        rounded = values.astype(BF16)
        for row in range(3):
            ghost_spread_ref[pl.ds(row * LAYER, LAYER), :] = (
                block_ref[step, ghost_rows(half), :] * rounded[row : row + 1, :]
            )
        gain(ghost_landed_ref.at[half], land(ghost_spread_ref[...], columns_of(2 * half), step))

    def keep_ghost(half):
        hit = hit_ref[:, columns_of(2 * half)] > 0.5
        rows = pl.ds(pl.multiple_of(3 * LAYER * half, LAYER), LAYER)
        for row in range(3):
            landed = ghost_landed_ref[half, pl.ds(row * LAYER, LAYER), :]
            held_now = ext_ref[0, rows, lanes_of(row, 1)].astype(F32)
            ext_ref[0, rows, lanes_of(row, 1)] = jnp.where(hit, landed, held_now).astype(BF16)

    def spread(step, section, rounded):
        marks = block_ref[step, pl.ds(LAYER, LAYER), :]
        for row in range(3):
            spread_ref[pl.ds((3 * section + row) * LAYER, LAYER), :] = marks * rounded[row : row + 1, :]

    def land_section(step, section, pieces):
        for first, rows in pieces:
            rows_of = pl.ds((3 * section + first) * LAYER, rows * LAYER)
            gain(landed_ref.at[rows_of], land(spread_ref[rows_of, :], columns_of(1), step))

    def own_columns(half):
        return pl.ds(half * width, width)

    def own_hit(half):
        return hit_ref[:, pl.ds((2 + half) * width, width)] > 0.5

    def land_first(step):
        mine, left, right = places(step)
        spread(step, 0, mine.astype(BF16))
        land_ghost(step, slow, jnp.where(slow == 0, left, right))
        land_section(step, 0, ((0, 3),))

    def land_fast(step):
        _, left, right = places(step)
        land_ghost(step, fast, jnp.where(fast == 0, left, right))

    def land_rest(step):
        mine, _, _ = places(step)
        speeds = jnp.concatenate(
            [in_vel[step * batch + i, 0:3, :][:, 0:capacity] for i in range(batch)], axis=1
        )
        spread(step, 1, split(mine)[1])
        for part, rounded in enumerate(split(speeds)):
            spread(step, 2 + part, rounded)
        for section in (1, 2, 3):
            land_section(step, section, ((0, 3),))

    pos_copy(0, 0, peers - 1).wait_recv()

    @apart
    def _():
        each_batch(land_first)
        keep_ghost(slow)
        for half in (0, 1):
            hit = own_hit(half)
            for row in range(3):
                landed = landed_ref[pl.ds(row * LAYER, LAYER), own_columns(half)]
                put(0, half, row, jnp.where(hit, landed, get(0, half, row)).astype(BF16))

    group = 9 if nnz % 9 == 0 else nnz

    def pick_blocks(slot, first, rows, half, target):
        start = pl.multiple_of(half * LAYER, LAYER)
        source = ext_ref[slot, pl.ds(start, reach), lanes_of(first, rows)]
        for begin in range(0, nnz, group):
            part = pl.ds(begin * LAYER, group * LAYER)
            target[part, lanes_of(first, rows)] = jnp.dot(
                onehot_ref[half, part, :], source, preferred_element_type=F32
            ).astype(BF16)

    def weigh(half, picks):
        sums = [jnp.zeros((LAYER, width), F32) for _ in picks]
        for j in range(nnz):
            part = pl.ds(j * LAYER, LAYER)
            mask = intact_ref[j, own(half), :]
            stacked = jnp.concatenate([one(part) for one in picks], axis=0)
            product = jnp.dot(stacked, wt_ref[j], preferred_element_type=F32)
            for i in range(len(picks)):
                sums[i] = sums[i] + product[i * LAYER : (i + 1) * LAYER] * mask
        return sums

    def placed(half, row):
        return lambda part: picked_ref[half, part, lanes_of(row, 1)]

    def softened(half, row):
        return lambda part: picked_ref[half, part, lanes_of(row, 1)] * soft_picked_ref[part, :]

    def softening(part):
        return soft_picked_ref[part, :]

    def near_parts(parted):
        return ((0, 1), (1, 2)) if parted else ((0, 3),)

    def stretching(t, half, parted, waits):
        near, far = 2 * t, 2 * t + 1
        summed = []
        for part, (first, rows) in enumerate(near_parts(parted and waits)):
            if waits:
                wait_halo(near, half, part, lanes_of(first, rows))
            pick_blocks(near, first, rows, half, picked_ref.at[half])
            summed += weigh(half, [placed(half, first + row) for row in range(rows)])
        scaling = mod_ref[own(half), :]
        stiffness = stiff_ref[own(half), :]
        rounded = [get(near, half, row) for row in range(3)]
        stretch = [scaling * (summed[row] - stiffness * rounded[row]) for row in range(3)]
        dilatation = (stretch[0] + stretch[1] + stretch[2]) / 3.0
        soften = 1.0 / (1.0 + dilatation * dilatation)
        soft_low = soften.astype(BF16)
        put(far, half, 0, soft_low)
        send(far, half, 0, lanes_of(0, 1))
        for row in range(3):
            stretch_ref[row, own(half), :] = stretch[row]
        soften_ref[own(half), :] = soften

    def pairing(t, half, parted, last):
        near, far = 2 * t, 2 * t + 1
        scaling = mod_ref[own(half), :]
        soften = soften_ref[own(half), :]
        kick = 0.5 * TIME_STEP if last else jnp.where(t == 0, 0.5 * TIME_STEP, TIME_STEP)
        wait_halo(far, half, 0, lanes_of(0, 1))
        pick_blocks(far, 0, 1, half, soft_picked_ref)
        for part, (first, rows) in enumerate(near_parts(parted)):
            picks = [softened(half, first + row) for row in range(rows)]
            if part == 0:
                soft_sum, *paired = weigh(half, [softening] + picks)
            else:
                paired = weigh(half, picks)
            for row in range(first, first + rows):
                rounded = get(near, half, row)
                force = 0.5 * (
                    scaling * (paired[row - first] - rounded * soft_sum) + soften * stretch_ref[row, own(half), :]
                )
                speed = vel_ref[row, own(half), :] + kick * force
                if last:
                    vel_out[own(half), row, :] = speed
                else:
                    vel_ref[row, own(half), :] = speed
                    moved = pos_ref[row, own(half), :] + TIME_STEP * speed
                    pos_ref[row, own(half), :] = moved
                    put(near + 2, half, row, moved.astype(BF16))
            if not last:
                send(near + 2, half, part, lanes_of(first, rows))

    stretching(0, slow, True, False)

    @apart
    def _():
        each_batch(land_fast)
        keep_ghost(fast)

    stretching(0, fast, False, False)

    vel_copy(0, 0, peers - 1).wait_recv()
    each_batch(land_rest)
    for half in (0, 1):
        hit = own_hit(half)
        for row in range(3):
            parts = [
                landed_ref[pl.ds((3 * section + row) * LAYER, LAYER), own_columns(half)] for section in range(4)
            ]
            pos_ref[row, own(half), :] = jnp.where(hit, parts[0] + parts[1], pos_in[row, own(half), :])
            vel_ref[row, own(half), :] = jnp.where(hit, parts[2] + parts[3], vel_in[row, own(half), :])

    def substep(t, carry):
        pairing(t, fast, False, False)
        pairing(t, slow, True, False)
        stretching(t + 1, fast, False, True)
        stretching(t + 1, slow, True, True)
        return carry

    lax.fori_loop(0, SUBSTEPS, substep, 0)

    for row in range(3):
        pos_out[:, row, :] = pos_ref[row]
    pairing(SUBSTEPS, fast, False, True)
    pairing(SUBSTEPS, slow, False, True)

    pos_copy(0, 0, peers - 1).wait_send()
    vel_copy(0, 0, peers - 1).wait_send()
    for half in (0, 1):

        @pl.when(exists(half))
        def _():
            index_copy(half).wait_send()

    for slot in range(1, slots):
        for half, parted in ((fast, False), (slow, True)):
            parts = ((0, 1),) if slot % 2 else near_parts(parted)
            for part, (first, rows) in enumerate(parts):
                wait_sent(slot, half, part, lanes_of(first, rows))


def store_kernel(pos_in, vel_in, pos_out, vel_out, sems):
    copies = [
        pltpu.make_async_copy(pos_in, pos_out, sems.at[0]),
        pltpu.make_async_copy(vel_in, vel_out, sems.at[1]),
    ]
    for copy in copies:
        copy.start()
    for copy in copies:
        copy.wait()


def shards(
    displacement,
    velocity,
    send_list,
    arrive_list,
    recv_count,
    horizon_blocks,
    bond_intact,
    modulus,
    bond_weight,
):
    node_count = displacement.shape[1]
    blocks, nnz, width = bond_intact.shape
    peers, capacity = send_list.shape[1:]
    lane_count = math.gcd(PEER_BATCH, peers) * capacity
    batches = peers * capacity // lane_count
    bundle_width = 128 * pl.cdiv(2 * capacity, 128)
    slots = 2 * (SUBSTEPS + 1)
    vmem = pl.BlockSpec(memory_space=pltpu.VMEM)
    hbm = pl.BlockSpec(memory_space=pltpu.HBM)
    shape = jax.ShapeDtypeStruct((blocks, 3, width), F32)
    spare = VMEM_LIMIT - 2 * 4 * blocks * 4 * width
    final_position, final_speed = pl.pallas_call(
        functools.partial(force_kernel, blocks, width, nnz, peers),
        out_shape=(pltpu.VMEM(shape.shape, F32), pltpu.VMEM(shape.shape, F32)),
        in_specs=[hbm] * 9,
        out_specs=(vmem, vmem),
        scratch_shapes=[
            pltpu.VMEM((peers, capacity), jnp.int32),
            pltpu.VMEM((peers, capacity), jnp.int32),
            pltpu.SMEM((1, peers), jnp.int32),
            pltpu.VMEM((nnz, blocks), jnp.int32),
            pltpu.VMEM((blocks, width), F32),
            pltpu.VMEM((nnz, width, width), BF16),
            pltpu.VMEM((blocks, 3, width), F32),
            pltpu.VMEM((blocks, 3, width), F32),
            pltpu.VMEM((3, blocks, width), F32),
            pltpu.VMEM((3, blocks, width), F32),
            pltpu.VMEM((peers + 2, 8, bundle_width), F32),
            pltpu.VMEM((peers, 8, bundle_width), F32),
            pltpu.VMEM((peers, 8, bundle_width), F32),
            pltpu.VMEM((peers, 8, bundle_width), F32),
            pltpu.VMEM((batches, 2 * width, lane_count), BF16),
            pltpu.VMEM((batches, blocks, lane_count), F32),
            pltpu.VMEM((3, batches, 1, lane_count), jnp.int32),
            pltpu.VMEM((batches, 4 * width, lane_count), BF16),
            pltpu.VMEM((batches, 3 * LAYER, lane_count), BF16),
            pltpu.VMEM((LAYER, 4 * width), F32),
            pltpu.VMEM((12 * LAYER, lane_count), BF16),
            pltpu.VMEM((12 * LAYER, 2 * width), F32),
            pltpu.VMEM((3 * LAYER, lane_count), BF16),
            pltpu.VMEM((2, 3 * LAYER, width), F32),
            pltpu.VMEM((nnz, blocks, width), jnp.int32),
            pltpu.VMEM((nnz, blocks, width), F32),
            pltpu.VMEM((nnz, width, width), BF16),
            pltpu.VMEM((2, nnz * LAYER, 3 * LAYER), BF16),
            pltpu.VMEM((slots, 4 * LAYER, 3 * width), BF16),
            pltpu.VMEM((2, nnz * LAYER, 3 * width), BF16),
            pltpu.VMEM((nnz * LAYER, width), BF16),
            pltpu.VMEM((blocks, width), F32),
            pltpu.VMEM((3, blocks, width), F32),
            pltpu.VMEM((blocks, width), F32),
            pltpu.VMEM((3, blocks, width), F32),
            pltpu.VMEM((3, blocks, width), F32),
            pltpu.SemaphoreType.DMA((slots, 2, 2)),
            pltpu.SemaphoreType.DMA((slots, 2, 2)),
            pltpu.SemaphoreType.DMA((2,)),
            pltpu.SemaphoreType.DMA((2,)),
            pltpu.SemaphoreType.DMA((2,)),
            pltpu.SemaphoreType.DMA((2,)),
            pltpu.SemaphoreType.DMA((9,)),
        ],
        compiler_params=pltpu.CompilerParams(
            collective_id=0, has_side_effects=True, vmem_limit_bytes=spare
        ),
        name="forces",
    )(
        send_list,
        arrive_list,
        recv_count,
        jnp.transpose(horizon_blocks),
        jnp.transpose(bond_intact, (1, 0, 2)),
        modulus.reshape(blocks, width),
        bond_weight,
        jnp.transpose(displacement.reshape(3, blocks, width), (1, 0, 2)),
        jnp.transpose(velocity.reshape(3, blocks, width), (1, 0, 2)),
    )
    final_position, final_speed = pl.pallas_call(
        store_kernel,
        out_shape=(shape, shape),
        in_specs=[pl.BlockSpec(memory_space=pl.ANY)] * 2,
        out_specs=(hbm, hbm),
        scratch_shapes=[pltpu.SemaphoreType.DMA((2,))],
        compiler_params=pltpu.CompilerParams(vmem_limit_bytes=1048576),
        name="store",
    )(final_position, final_speed)
    return tuple(jnp.transpose(x, (1, 0, 2)).reshape(3, node_count) for x in (final_position, final_speed))


def solution(mesh):
    in_specs = (
        P(None, ("parts", "wall")),
        P(None, ("parts", "wall")),
        P(("parts", "wall"), None, None),
        P(("parts", "wall"), None, None),
        P(("parts", "wall"), None),
        P(("parts", "wall"), None),
        P(("parts", "wall"), None, None),
        P(("parts", "wall")),
        P(),
    )
    out_specs = (P(None, ("parts", "wall")), P(None, ("parts", "wall")))
    return jax.shard_map(shards, mesh=mesh, in_specs=in_specs, out_specs=out_specs, check_vma=False)
```

```python
import functools
import math

import jax
import jax.numpy as jnp
from jax import lax
from jax.experimental import pallas as pl
from jax.experimental.pallas import tpu as pltpu
from jax.sharding import PartitionSpec as P

SUBSTEPS = 2
LAYER = 64
PEER_BATCH = 16
TIME_STEP = 0.25
VMEM_LIMIT = 66977792
MESH = pl.DeviceIdType.MESH
F32 = jnp.float32
BF16 = jnp.bfloat16


def force_kernel(
    blocks,
    width,
    nnz,
    peers,
    send_hbm,
    arrive_hbm,
    count_hbm,
    hor_hbm,
    bonds_hbm,
    mod_hbm,
    weight_hbm,
    pos_hbm,
    vel_hbm,
    pos_out,
    vel_out,
    send_ref,
    arrive_ref,
    count_ref,
    hor_ref,
    mod_ref,
    weight_ref,
    pos_raw,
    vel_raw,
    pos_in,
    vel_in,
    out_pos,
    in_pos,
    out_vel,
    in_vel,
    leave_node_ref,
    leave_block_ref,
    index_ref,
    node_ref,
    block_ref,
    hit_ref,
    spread_ref,
    landed_ref,
    ghost_spread_ref,
    ghost_landed_ref,
    raw_ref,
    intact_ref,
    wt_ref,
    onehot_ref,
    ext_ref,
    picked_ref,
    soft_picked_ref,
    stiff_ref,
    stretch_ref,
    soften_ref,
    pos_ref,
    vel_ref,
    send_sem,
    recv_sem,
    index_send_sem,
    index_recv_sem,
    node_send_sem,
    node_recv_sem,
    fetch_sem,
):
    me = lax.axis_index("wall")
    count = lax.axis_size("wall")
    reach = 3 * LAYER
    slots = 2 * (SUBSTEPS + 1)
    slow = lax.rem(me, 2)
    fast = 1 - slow

    nodes = blocks * width
    capacity = send_ref.shape[1]
    shift = width.bit_length() - 1
    batch = math.gcd(PEER_BATCH, peers)
    batches = peers // batch
    lane_count = batch * capacity

    barrier = pltpu.get_barrier_semaphore()

    def greet(step, carry):
        pl.semaphore_signal(
            barrier, inc=1, device_id={"wall": lax.rem(me + step, count)}, device_id_type=MESH
        )
        return carry

    lax.fori_loop(1, peers, greet, 0)

    pairs = {
        "send": (send_hbm.at[0], send_ref),
        "pos": (pos_hbm, pos_raw),
        "arrive": (arrive_hbm.at[0], arrive_ref),
        "count": (count_hbm, count_ref),
        "hor": (hor_hbm, hor_ref),
        "weight": (weight_hbm, weight_ref),
        "bonds": (bonds_hbm, raw_ref),
        "mod": (mod_hbm, mod_ref),
        "vel": (vel_hbm, vel_raw),
    }
    fetches = {
        name: pltpu.make_async_copy(pair[0], pair[1], fetch_sem.at[i])
        for i, (name, pair) in enumerate(pairs.items())
    }
    for name in ("send", "pos", "arrive", "count", "hor"):
        fetches[name].start()

    def split(value):
        high = value.astype(BF16)
        low = (value - high.astype(F32)).astype(BF16)
        return high, low

    def neighbour(half):
        return lax.rem(me + count - 1 + 2 * half, count)

    def exists(half):
        there = me - 1 + 2 * half
        return jnp.logical_and(there >= 0, there < count)

    def own(half):
        return pl.ds(half * LAYER if isinstance(half, int) else pl.multiple_of(half * LAYER, LAYER), LAYER)

    def held(half):
        start = LAYER + half * LAYER
        return pl.ds(start if isinstance(half, int) else pl.multiple_of(start, LAYER), LAYER)

    def halo_copy(slot, half, part, lanes):
        start = 3 * LAYER * (1 - half)
        target = pl.ds(start if isinstance(half, int) else pl.multiple_of(start, LAYER), LAYER)
        return pltpu.make_async_remote_copy(
            src_ref=ext_ref.at[slot, held(half), lanes],
            dst_ref=ext_ref.at[slot, target, lanes],
            send_sem=send_sem.at[slot, half, part],
            recv_sem=recv_sem.at[slot, 1 - half, part],
            device_id={"wall": neighbour(half)},
            device_id_type=MESH,
        )

    def lanes_of(first, rows):
        return pl.ds(first * width, rows * width)

    def send(slot, half, part, lanes):
        @pl.when(exists(half))
        def _():
            halo_copy(slot, half, part, lanes).start()

    def wait_halo(slot, half, part, lanes):
        @pl.when(exists(half))
        def _():
            halo_copy(slot, 1 - half, part, lanes).wait_recv()

    def wait_sent(slot, half, part, lanes):
        @pl.when(exists(half))
        def _():
            halo_copy(slot, half, part, lanes).wait_send()

    def put(slot, half, column, value):
        ext_ref[slot, held(half), lanes_of(column, 1)] = value

    def get(slot, half, column):
        return ext_ref[slot, held(half), lanes_of(column, 1)].astype(F32)

    def index_copy(half):
        return pltpu.make_async_remote_copy(
            src_ref=index_ref.at[1],
            dst_ref=index_ref.at[2 - 2 * half],
            send_sem=index_send_sem.at[half],
            recv_sem=index_recv_sem.at[1 - half],
            device_id={"wall": neighbour(half)},
            device_id_type=MESH,
        )

    def each_batch(body):
        def step(index, carry):
            body(index)
            return carry

        if batches == 1:
            body(0)
        else:
            lax.fori_loop(0, batches, step, 0)

    def apart(body):
        def once(step, carry):
            body()
            return carry

        lax.fori_loop(0, 1 + lax.div(me, count), once, 0)

    def mark_leaving(step):
        rows = send_ref[pl.ds(step * batch, batch), :]
        index = jnp.concatenate([rows[i : i + 1, :] for i in range(batch)], axis=1)
        of_node = lax.broadcasted_iota(jnp.int32, (width, lane_count), 0) == (index & (width - 1))
        of_block = lax.broadcasted_iota(jnp.int32, (blocks, lane_count), 0) == (index >> shift)
        column = jnp.where(of_node, 1.0, 0.0).astype(BF16)
        leave_node_ref[step, 0:width, :] = column
        leave_node_ref[step, width : 2 * width, :] = column
        leave_block_ref[step] = jnp.where(of_block, 1.0, 0.0)

    def pick(step, source):
        tile = 256 if lane_count % 256 == 0 else lane_count
        splits = [jnp.concatenate(split(source[row]), axis=1) for row in range(3)]
        picked_rows = []
        for start in range(0, lane_count, tile):
            of_block = leave_block_ref[step, :, start : start + tile]
            values = []
            for row in range(3):
                found = jnp.dot(
                    splits[row], leave_node_ref[step, :, start : start + tile], preferred_element_type=F32
                )
                values.append(jnp.sum(of_block * found, axis=0, keepdims=True))
            picked_rows.append(values)
        return [jnp.concatenate([values[row] for values in picked_rows], axis=1) for row in range(3)]

    def gather_places(step):
        values = pick(step, pos_in)
        placed = jnp.concatenate(values + values, axis=0)
        for i in range(batch):
            peer = step * batch + i
            mine = slice(i * capacity, (i + 1) * capacity)
            out_pos[peer + 1, 0:3, 0:capacity] = placed[0:3, mine]
            out_pos[peer + 2, 0:3, capacity : 2 * capacity] = placed[0:3, mine]
            out_pos[peer, 3:6, 0:capacity] = placed[3:6, mine]

    def gather_speeds(step):
        speeds = jnp.concatenate(pick(step, vel_in), axis=0)
        for i in range(batch):
            out_vel[step * batch + i, 0:3, 0:capacity] = speeds[:, i * capacity : (i + 1) * capacity]

    def pos_copy(peer, there, many=1):
        return pltpu.make_async_remote_copy(
            src_ref=out_pos.at[pl.ds(peer, many), pl.ds(0, 6), :],
            dst_ref=in_pos.at[pl.ds(there, many), pl.ds(0, 6), :],
            send_sem=node_send_sem.at[0],
            recv_sem=node_recv_sem.at[0],
            device_id={"wall": neighbour(1)} if many > 1 else {"wall": peer - 1},
            device_id_type=MESH,
        )

    def vel_copy(peer, there, many=1):
        return pltpu.make_async_remote_copy(
            src_ref=out_vel.at[pl.ds(peer, many), pl.ds(0, 3), :],
            dst_ref=in_vel.at[pl.ds(there, many), pl.ds(0, 3), :],
            send_sem=node_send_sem.at[1],
            recv_sem=node_recv_sem.at[1],
            device_id={"wall": neighbour(1)} if many > 1 else {"wall": peer},
            device_id_type=MESH,
        )

    out_pos[...] = jnp.zeros(out_pos.shape, F32)
    def index_batch(step):
        rows = arrive_ref[pl.ds(step * batch, batch), :]
        slot_ids = lax.broadcasted_iota(jnp.int32, (1, capacity), 1)
        index_ref[1, step] = jnp.concatenate(
            [
                jnp.where(slot_ids < count_ref[0, step * batch + i], rows[i : i + 1, :], nodes)
                for i in range(batch)
            ],
            axis=1,
        )

    fetches["send"].wait()
    each_batch(mark_leaving)
    for name in ("arrive", "count"):
        fetches[name].wait()
    each_batch(index_batch)
    fetches["pos"].wait()
    for name in ("weight", "bonds", "mod", "vel"):
        fetches[name].start()
    for row in range(3):
        pos_in[row] = pos_raw[:, row, :]
    each_batch(gather_places)
    in_pos[me, 0:6, :] = out_pos[me + 1, 0:6, :]
    for half in (0, 1):
        for row in range(3):
            put(0, half, row, pos_in[row, own(half), :].astype(BF16))
    pl.semaphore_wait(barrier, peers - 1)
    for half in (0, 1):

        @pl.when(exists(half))
        def _():
            index_copy(half).start()

        @pl.when(jnp.logical_not(exists(half)))
        def _():
            index_ref[2 * half] = jnp.full(index_ref.shape[1:], nodes, jnp.int32)
            for slot in range(slots):
                ext_ref[slot, pl.ds(3 * LAYER * half, LAYER), :] = jnp.zeros((LAYER, 3 * width), BF16)

    for half in (0, 1):
        send(0, half, 0, lanes_of(0, 3))


    def start_places(step, carry):
        pos_copy(lax.rem(me + step, count) + 1, me).start()
        return carry

    lax.fori_loop(1, peers, start_places, 0)

    lanes = lax.broadcasted_iota(jnp.int32, (LAYER, reach), 1)
    fetches["hor"].wait()
    padding = jnp.zeros((-nnz % 8, blocks), jnp.int32)
    horizon = jnp.transpose(jnp.concatenate([hor_ref[...], padding], axis=0))
    for half in range(2):
        local = horizon[half * LAYER : (half + 1) * LAYER] - me * blocks
        local = jnp.where(local < 0, local + reach, local)
        for j in range(nnz):
            hit = local[:, j : j + 1] == lanes
            onehot_ref[half, pl.ds(j * LAYER, LAYER), :] = jnp.where(hit, 1.0, 0.0).astype(BF16)

    fetches["vel"].wait()
    out_vel[...] = jnp.zeros(out_vel.shape, F32)
    for row in range(3):
        vel_in[row] = vel_raw[:, row, :]

    each_batch(gather_speeds)
    in_vel[me, 0:3, :] = out_vel[me, 0:3, :]

    def start_speeds(step, carry):
        vel_copy(lax.rem(me + step, count), me).start()
        return carry

    lax.fori_loop(1, peers, start_speeds, 0)

    for name in ("weight", "bonds", "mod"):
        fetches[name].wait()
    stiff = jnp.zeros((blocks, width), F32)
    ones = jnp.ones((16, width), BF16)
    for j in range(nnz):
        weight = jnp.transpose(weight_ref[j])
        wt_ref[j] = weight
        totals = jnp.dot(ones, weight, preferred_element_type=F32)[0:1, :]
        intact = raw_ref[j].astype(F32)
        intact_ref[j] = intact
        stiff = stiff + intact * totals
    stiff_ref[...] = stiff

    def gain(ref, value):
        ref[...] = value if batches == 1 else ref[...] + value

    def clear(refs):
        if batches > 1:
            for ref in refs:
                ref[...] = jnp.zeros(ref.shape, F32)

    def columns_of(which):
        if isinstance(which, int):
            return pl.ds((0, 2 * width, width)[which], 2 * width if which == 1 else width)
        return pl.ds(pl.multiple_of(lax.div(which, 2) * width, width), width)

    def land(marks, columns, step):
        return lax.dot_general(
            marks, node_ref[step, columns, :], (((1,), (1,)), ((), ())), preferred_element_type=F32
        )

    def mark_batch(step, which_ones):
        for which in which_ones:
            index = index_ref[which, step]
            inside = index & (width - 1)
            block = index >> shift
            if which == 1:
                inside = inside + jnp.where(block >= LAYER, width, 0)
                block = jnp.where(block < 2 * LAYER, block & (LAYER - 1), 2 * LAYER)
            first = LAYER if which == 0 else 0
            columns = columns_of(which)
            of_node = lax.broadcasted_iota(jnp.int32, (columns.size, lane_count), 0) == inside
            node_ref[step, columns, :] = jnp.where(of_node, 1.0, 0.0).astype(BF16)
            of_block = lax.broadcasted_iota(jnp.int32, (LAYER, lane_count), 0) + first == block
            marks = jnp.where(of_block, 1.0, 0.0).astype(BF16)
            rows = pl.ds(which * LAYER, LAYER)
            block_ref[step, rows, :] = marks
            gain(hit_ref.at[:, columns], land(marks, columns, step))

    clear([hit_ref, landed_ref, ghost_landed_ref])
    each_batch(lambda step: mark_batch(step, (1,)))
    for half in (0, 1):

        @pl.when(exists(half))
        def _():
            index_copy(1 - half).wait_recv()

    each_batch(lambda step: mark_batch(step, (0, 2)))

    for half in (0, 1):
        wait_halo(0, half, 0, lanes_of(0, 3))
        wait_sent(0, half, 0, lanes_of(0, 3))

    def places(step):
        bundles = [in_pos[step * batch + i, 0:6, :] for i in range(batch)]
        first = jnp.concatenate([bundle[:, 0:capacity] for bundle in bundles], axis=1)
        left = jnp.concatenate([bundle[0:3, capacity : 2 * capacity] for bundle in bundles], axis=1)
        return first[0:3], left, first[3:6]

    def ghost_rows(half):
        return pl.ds(pl.multiple_of(2 * half * LAYER, LAYER), LAYER)

    def land_ghost(step, half, values):
        rounded = values.astype(BF16)
        for row in range(3):
            ghost_spread_ref[pl.ds(row * LAYER, LAYER), :] = (
                block_ref[step, ghost_rows(half), :] * rounded[row : row + 1, :]
            )
        gain(ghost_landed_ref.at[half], land(ghost_spread_ref[...], columns_of(2 * half), step))

    def keep_ghost(half):
        hit = hit_ref[:, columns_of(2 * half)] > 0.5
        rows = pl.ds(pl.multiple_of(3 * LAYER * half, LAYER), LAYER)
        for row in range(3):
            landed = ghost_landed_ref[half, pl.ds(row * LAYER, LAYER), :]
            held_now = ext_ref[0, rows, lanes_of(row, 1)].astype(F32)
            ext_ref[0, rows, lanes_of(row, 1)] = jnp.where(hit, landed, held_now).astype(BF16)

    def spread(step, section, rounded):
        marks = block_ref[step, pl.ds(LAYER, LAYER), :]
        for row in range(3):
            spread_ref[pl.ds((3 * section + row) * LAYER, LAYER), :] = marks * rounded[row : row + 1, :]

    def land_section(step, section, pieces):
        for first, rows in pieces:
            rows_of = pl.ds((3 * section + first) * LAYER, rows * LAYER)
            gain(landed_ref.at[rows_of], land(spread_ref[rows_of, :], columns_of(1), step))

    def own_columns(half):
        return pl.ds(half * width, width)

    def own_hit(half):
        return hit_ref[:, pl.ds((2 + half) * width, width)] > 0.5

    def land_first(step):
        mine, left, right = places(step)
        spread(step, 0, mine.astype(BF16))
        land_ghost(step, slow, jnp.where(slow == 0, left, right))
        land_section(step, 0, ((0, 3),))

    def land_fast(step):
        _, left, right = places(step)
        land_ghost(step, fast, jnp.where(fast == 0, left, right))

    def land_rest(step):
        mine, _, _ = places(step)
        speeds = jnp.concatenate(
            [in_vel[step * batch + i, 0:3, :][:, 0:capacity] for i in range(batch)], axis=1
        )
        spread(step, 1, split(mine)[1])
        for part, rounded in enumerate(split(speeds)):
            spread(step, 2 + part, rounded)
        for section in (1, 2, 3):
            land_section(step, section, ((0, 3),))

    pos_copy(0, 0, peers - 1).wait_recv()

    @apart
    def _():
        each_batch(land_first)
        keep_ghost(slow)
        for half in (0, 1):
            hit = own_hit(half)
            for row in range(3):
                landed = landed_ref[pl.ds(row * LAYER, LAYER), own_columns(half)]
                put(0, half, row, jnp.where(hit, landed, get(0, half, row)).astype(BF16))

    group = 9 if nnz % 9 == 0 else nnz

    def ghost_of(half):
        return pl.ds(pl.multiple_of(3 * LAYER * half, LAYER), LAYER)

    def pick_blocks(slot, first, rows, half, target):
        columns = lanes_of(first, rows)
        source = jnp.concatenate(
            [ext_ref[slot, pl.ds(LAYER, 2 * LAYER), columns], ext_ref[slot, ghost_of(half), columns]], axis=0
        )
        for begin in range(0, nnz, group):
            part = pl.ds(begin * LAYER, group * LAYER)
            target[part, columns] = jnp.dot(
                onehot_ref[half, part, :], source, preferred_element_type=F32
            ).astype(BF16)

    def pick_own(slot, half, target):
        source = ext_ref[slot, pl.ds(LAYER, 2 * LAYER), lanes_of(0, 1)]
        for begin in range(0, nnz, group):
            part = pl.ds(begin * LAYER, group * LAYER)
            target[part, lanes_of(0, 1)] = jnp.dot(
                onehot_ref[half, part, 0 : 2 * LAYER], source, preferred_element_type=F32
            ).astype(BF16)

    def pick_ghost(slot, half, target):
        source = ext_ref[slot, ghost_of(half), lanes_of(0, 1)]
        for begin in range(0, nnz, group):
            part = pl.ds(begin * LAYER, group * LAYER)
            target[part, lanes_of(0, 1)] = target[part, lanes_of(0, 1)] + jnp.dot(
                onehot_ref[half, part, 2 * LAYER : reach], source, preferred_element_type=F32
            ).astype(BF16)

    def weigh(half, picks):
        sums = [jnp.zeros((LAYER, width), F32) for _ in picks]
        for j in range(nnz):
            part = pl.ds(j * LAYER, LAYER)
            mask = intact_ref[j, own(half), :]
            stacked = jnp.concatenate([one(part) for one in picks], axis=0)
            product = jnp.dot(stacked, wt_ref[j], preferred_element_type=F32)
            for i in range(len(picks)):
                sums[i] = sums[i] + product[i * LAYER : (i + 1) * LAYER] * mask
        return sums

    def placed(half, row):
        return lambda part: picked_ref[half, part, lanes_of(row, 1)]

    def softened(half, row):
        return lambda part: picked_ref[half, part, lanes_of(row, 1)] * soft_picked_ref[part, :]

    def softening(part):
        return soft_picked_ref[part, :]

    def near_parts(parted):
        return ((0, 1), (1, 2)) if parted else ((0, 3),)

    def stretching(t, half, parted, waits):
        near, far = 2 * t, 2 * t + 1
        summed = []
        for part, (first, rows) in enumerate(near_parts(parted and waits)):
            single = waits and rows == 1
            if single:
                pick_own(near, half, picked_ref.at[half])
            if waits:
                wait_halo(near, half, part, lanes_of(first, rows))
            if single:
                pick_ghost(near, half, picked_ref.at[half])
            else:
                pick_blocks(near, first, rows, half, picked_ref.at[half])
            summed += weigh(half, [placed(half, first + row) for row in range(rows)])
        scaling = mod_ref[own(half), :]
        stiffness = stiff_ref[own(half), :]
        rounded = [get(near, half, row) for row in range(3)]
        stretch = [scaling * (summed[row] - stiffness * rounded[row]) for row in range(3)]
        dilatation = (stretch[0] + stretch[1] + stretch[2]) / 3.0
        soften = 1.0 / (1.0 + dilatation * dilatation)
        soft_low = soften.astype(BF16)
        put(far, half, 0, soft_low)
        send(far, half, 0, lanes_of(0, 1))
        for row in range(3):
            stretch_ref[row, own(half), :] = stretch[row]
        soften_ref[own(half), :] = soften

    def pairing(t, half, parted, last):
        near, far = 2 * t, 2 * t + 1
        scaling = mod_ref[own(half), :]
        soften = soften_ref[own(half), :]
        kick = 0.5 * TIME_STEP if last else jnp.where(t == 0, 0.5 * TIME_STEP, TIME_STEP)
        wait_halo(far, half, 0, lanes_of(0, 1))
        pick_blocks(far, 0, 1, half, soft_picked_ref)
        for part, (first, rows) in enumerate(near_parts(parted)):
            picks = [softened(half, first + row) for row in range(rows)]
            if part == 0:
                soft_sum, *paired = weigh(half, [softening] + picks)
            else:
                paired = weigh(half, picks)
            for row in range(first, first + rows):
                rounded = get(near, half, row)
                force = 0.5 * (
                    scaling * (paired[row - first] - rounded * soft_sum) + soften * stretch_ref[row, own(half), :]
                )
                speed = vel_ref[row, own(half), :] + kick * force
                if last:
                    vel_out[own(half), row, :] = speed
                else:
                    vel_ref[row, own(half), :] = speed
                    moved = pos_ref[row, own(half), :] + TIME_STEP * speed
                    pos_ref[row, own(half), :] = moved
                    put(near + 2, half, row, moved.astype(BF16))
            if not last:
                send(near + 2, half, part, lanes_of(first, rows))

    stretching(0, slow, True, False)

    @apart
    def _():
        each_batch(land_fast)
        keep_ghost(fast)

    stretching(0, fast, False, False)

    vel_copy(0, 0, peers - 1).wait_recv()
    each_batch(land_rest)
    for half in (0, 1):
        hit = own_hit(half)
        for row in range(3):
            parts = [
                landed_ref[pl.ds((3 * section + row) * LAYER, LAYER), own_columns(half)] for section in range(4)
            ]
            pos_ref[row, own(half), :] = jnp.where(hit, parts[0] + parts[1], pos_in[row, own(half), :])
            vel_ref[row, own(half), :] = jnp.where(hit, parts[2] + parts[3], vel_in[row, own(half), :])

    def substep(t, carry):
        pairing(t, fast, False, False)
        pairing(t, slow, True, False)
        stretching(t + 1, fast, False, True)
        stretching(t + 1, slow, True, True)
        return carry

    lax.fori_loop(0, SUBSTEPS, substep, 0)

    for row in range(3):
        pos_out[:, row, :] = pos_ref[row]
    pairing(SUBSTEPS, fast, False, True)
    pairing(SUBSTEPS, slow, False, True)

    pos_copy(0, 0, peers - 1).wait_send()
    vel_copy(0, 0, peers - 1).wait_send()
    for half in (0, 1):

        @pl.when(exists(half))
        def _():
            index_copy(half).wait_send()

    for slot in range(1, slots):
        for half, parted in ((fast, False), (slow, True)):
            parts = ((0, 1),) if slot % 2 else near_parts(parted)
            for part, (first, rows) in enumerate(parts):
                wait_sent(slot, half, part, lanes_of(first, rows))


def store_kernel(pos_in, vel_in, pos_out, vel_out, sems):
    copies = [
        pltpu.make_async_copy(pos_in, pos_out, sems.at[0]),
        pltpu.make_async_copy(vel_in, vel_out, sems.at[1]),
    ]
    for copy in copies:
        copy.start()
    for copy in copies:
        copy.wait()


def shards(
    displacement,
    velocity,
    send_list,
    arrive_list,
    recv_count,
    horizon_blocks,
    bond_intact,
    modulus,
    bond_weight,
):
    node_count = displacement.shape[1]
    blocks, nnz, width = bond_intact.shape
    peers, capacity = send_list.shape[1:]
    lane_count = math.gcd(PEER_BATCH, peers) * capacity
    batches = peers * capacity // lane_count
    bundle_width = 128 * pl.cdiv(2 * capacity, 128)
    slots = 2 * (SUBSTEPS + 1)
    vmem = pl.BlockSpec(memory_space=pltpu.VMEM)
    hbm = pl.BlockSpec(memory_space=pltpu.HBM)
    shape = jax.ShapeDtypeStruct((blocks, 3, width), F32)
    spare = VMEM_LIMIT - 2 * 4 * blocks * 4 * width
    final_position, final_speed = pl.pallas_call(
        functools.partial(force_kernel, blocks, width, nnz, peers),
        out_shape=(pltpu.VMEM(shape.shape, F32), pltpu.VMEM(shape.shape, F32)),
        in_specs=[hbm] * 9,
        out_specs=(vmem, vmem),
        scratch_shapes=[
            pltpu.VMEM((peers, capacity), jnp.int32),
            pltpu.VMEM((peers, capacity), jnp.int32),
            pltpu.SMEM((1, peers), jnp.int32),
            pltpu.VMEM((nnz, blocks), jnp.int32),
            pltpu.VMEM((blocks, width), F32),
            pltpu.VMEM((nnz, width, width), BF16),
            pltpu.VMEM((blocks, 3, width), F32),
            pltpu.VMEM((blocks, 3, width), F32),
            pltpu.VMEM((3, blocks, width), F32),
            pltpu.VMEM((3, blocks, width), F32),
            pltpu.VMEM((peers + 2, 8, bundle_width), F32),
            pltpu.VMEM((peers, 8, bundle_width), F32),
            pltpu.VMEM((peers, 8, bundle_width), F32),
            pltpu.VMEM((peers, 8, bundle_width), F32),
            pltpu.VMEM((batches, 2 * width, lane_count), BF16),
            pltpu.VMEM((batches, blocks, lane_count), F32),
            pltpu.VMEM((3, batches, 1, lane_count), jnp.int32),
            pltpu.VMEM((batches, 4 * width, lane_count), BF16),
            pltpu.VMEM((batches, 3 * LAYER, lane_count), BF16),
            pltpu.VMEM((LAYER, 4 * width), F32),
            pltpu.VMEM((12 * LAYER, lane_count), BF16),
            pltpu.VMEM((12 * LAYER, 2 * width), F32),
            pltpu.VMEM((3 * LAYER, lane_count), BF16),
            pltpu.VMEM((2, 3 * LAYER, width), F32),
            pltpu.VMEM((nnz, blocks, width), jnp.int32),
            pltpu.VMEM((nnz, blocks, width), F32),
            pltpu.VMEM((nnz, width, width), BF16),
            pltpu.VMEM((2, nnz * LAYER, 3 * LAYER), BF16),
            pltpu.VMEM((slots, 4 * LAYER, 3 * width), BF16),
            pltpu.VMEM((2, nnz * LAYER, 3 * width), BF16),
            pltpu.VMEM((nnz * LAYER, width), BF16),
            pltpu.VMEM((blocks, width), F32),
            pltpu.VMEM((3, blocks, width), F32),
            pltpu.VMEM((blocks, width), F32),
            pltpu.VMEM((3, blocks, width), F32),
            pltpu.VMEM((3, blocks, width), F32),
            pltpu.SemaphoreType.DMA((slots, 2, 2)),
            pltpu.SemaphoreType.DMA((slots, 2, 2)),
            pltpu.SemaphoreType.DMA((2,)),
            pltpu.SemaphoreType.DMA((2,)),
            pltpu.SemaphoreType.DMA((2,)),
            pltpu.SemaphoreType.DMA((2,)),
            pltpu.SemaphoreType.DMA((9,)),
        ],
        compiler_params=pltpu.CompilerParams(
            collective_id=0, has_side_effects=True, vmem_limit_bytes=spare
        ),
        name="forces",
    )(
        send_list,
        arrive_list,
        recv_count,
        jnp.transpose(horizon_blocks),
        jnp.transpose(bond_intact, (1, 0, 2)),
        modulus.reshape(blocks, width),
        bond_weight,
        jnp.transpose(displacement.reshape(3, blocks, width), (1, 0, 2)),
        jnp.transpose(velocity.reshape(3, blocks, width), (1, 0, 2)),
    )
    final_position, final_speed = pl.pallas_call(
        store_kernel,
        out_shape=(shape, shape),
        in_specs=[pl.BlockSpec(memory_space=pl.ANY)] * 2,
        out_specs=(hbm, hbm),
        scratch_shapes=[pltpu.SemaphoreType.DMA((2,))],
        compiler_params=pltpu.CompilerParams(vmem_limit_bytes=1048576),
        name="store",
    )(final_position, final_speed)
    return tuple(jnp.transpose(x, (1, 0, 2)).reshape(3, node_count) for x in (final_position, final_speed))


def solution(mesh):
    in_specs = (
        P(None, ("parts", "wall")),
        P(None, ("parts", "wall")),
        P(("parts", "wall"), None, None),
        P(("parts", "wall"), None, None),
        P(("parts", "wall"), None),
        P(("parts", "wall"), None),
        P(("parts", "wall"), None, None),
        P(("parts", "wall")),
        P(),
    )
    out_specs = (P(None, ("parts", "wall")), P(None, ("parts", "wall")))
    return jax.shard_map(shards, mesh=mesh, in_specs=in_specs, out_specs=out_specs, check_vma=False)
```

```python
import functools
import math

import jax
import jax.numpy as jnp
from jax import lax
from jax.experimental import pallas as pl
from jax.experimental.pallas import tpu as pltpu
from jax.sharding import PartitionSpec as P

SUBSTEPS = 2
LAYER = 64
PEER_BATCH = 16
TIME_STEP = 0.25
VMEM_LIMIT = 66977792
MESH = pl.DeviceIdType.MESH
F32 = jnp.float32
BF16 = jnp.bfloat16


def force_kernel(
    blocks,
    width,
    nnz,
    peers,
    send_hbm,
    arrive_hbm,
    count_hbm,
    hor_hbm,
    bonds_hbm,
    mod_hbm,
    weight_hbm,
    pos_hbm,
    vel_hbm,
    pos_out,
    vel_out,
    send_ref,
    arrive_ref,
    count_ref,
    hor_ref,
    mod_ref,
    weight_ref,
    pos_raw,
    vel_raw,
    pos_in,
    vel_in,
    out_pos,
    in_pos,
    out_vel,
    in_vel,
    leave_node_ref,
    leave_block_ref,
    index_ref,
    node_ref,
    block_ref,
    hit_ref,
    spread_ref,
    landed_ref,
    ghost_spread_ref,
    ghost_landed_ref,
    raw_ref,
    intact_ref,
    wt_ref,
    onehot_ref,
    ext_ref,
    picked_ref,
    soft_picked_ref,
    stiff_ref,
    stretch_ref,
    soften_ref,
    pos_ref,
    vel_ref,
    send_sem,
    recv_sem,
    index_send_sem,
    index_recv_sem,
    node_send_sem,
    node_recv_sem,
    fetch_sem,
):
    me = lax.axis_index("wall")
    count = lax.axis_size("wall")
    reach = 3 * LAYER
    slots = 2 * (SUBSTEPS + 1)
    slow = lax.rem(me, 2)
    fast = 1 - slow

    nodes = blocks * width
    capacity = send_ref.shape[1]
    shift = width.bit_length() - 1
    batch = math.gcd(PEER_BATCH, peers)
    batches = peers // batch
    lane_count = batch * capacity

    barrier = pltpu.get_barrier_semaphore()

    def greet(step, carry):
        pl.semaphore_signal(
            barrier, inc=1, device_id={"wall": lax.rem(me + step, count)}, device_id_type=MESH
        )
        return carry

    lax.fori_loop(1, peers, greet, 0)

    pairs = {
        "send": (send_hbm.at[0], send_ref),
        "pos": (pos_hbm, pos_raw),
        "arrive": (arrive_hbm.at[0], arrive_ref),
        "count": (count_hbm, count_ref),
        "hor": (hor_hbm, hor_ref),
        "weight": (weight_hbm, weight_ref),
        "bonds": (bonds_hbm, raw_ref),
        "mod": (mod_hbm, mod_ref),
        "vel": (vel_hbm, vel_raw),
    }
    fetches = {
        name: pltpu.make_async_copy(pair[0], pair[1], fetch_sem.at[i])
        for i, (name, pair) in enumerate(pairs.items())
    }
    for name in ("send", "pos", "arrive", "count", "hor"):
        fetches[name].start()

    def split(value):
        high = value.astype(BF16)
        low = (value - high.astype(F32)).astype(BF16)
        return high, low

    def neighbour(half):
        return lax.rem(me + count - 1 + 2 * half, count)

    def exists(half):
        there = me - 1 + 2 * half
        return jnp.logical_and(there >= 0, there < count)

    def own(half):
        return pl.ds(half * LAYER if isinstance(half, int) else pl.multiple_of(half * LAYER, LAYER), LAYER)

    def held(half):
        start = LAYER + half * LAYER
        return pl.ds(start if isinstance(half, int) else pl.multiple_of(start, LAYER), LAYER)

    def halo_copy(slot, half, part, lanes):
        start = 3 * LAYER * (1 - half)
        target = pl.ds(start if isinstance(half, int) else pl.multiple_of(start, LAYER), LAYER)
        return pltpu.make_async_remote_copy(
            src_ref=ext_ref.at[slot, held(half), lanes],
            dst_ref=ext_ref.at[slot, target, lanes],
            send_sem=send_sem.at[slot, half, part],
            recv_sem=recv_sem.at[slot, 1 - half, part],
            device_id={"wall": neighbour(half)},
            device_id_type=MESH,
        )

    def lanes_of(first, rows):
        return pl.ds(first * width, rows * width)

    def send(slot, half, part, lanes):
        @pl.when(exists(half))
        def _():
            halo_copy(slot, half, part, lanes).start()

    def wait_halo(slot, half, part, lanes):
        @pl.when(exists(half))
        def _():
            halo_copy(slot, 1 - half, part, lanes).wait_recv()

    def wait_sent(slot, half, part, lanes):
        @pl.when(exists(half))
        def _():
            halo_copy(slot, half, part, lanes).wait_send()

    def put(slot, half, column, value):
        ext_ref[slot, held(half), lanes_of(column, 1)] = value

    def get(slot, half, column):
        return ext_ref[slot, held(half), lanes_of(column, 1)].astype(F32)

    def index_copy(half):
        return pltpu.make_async_remote_copy(
            src_ref=index_ref.at[1],
            dst_ref=index_ref.at[2 - 2 * half],
            send_sem=index_send_sem.at[half],
            recv_sem=index_recv_sem.at[1 - half],
            device_id={"wall": neighbour(half)},
            device_id_type=MESH,
        )

    def each_batch(body):
        def step(index, carry):
            body(index)
            return carry

        if batches == 1:
            body(0)
        else:
            lax.fori_loop(0, batches, step, 0)

    def apart(body):
        def once(step, carry):
            body()
            return carry

        lax.fori_loop(0, 1 + lax.div(me, count), once, 0)

    def mark_leaving(step):
        rows = send_ref[pl.ds(step * batch, batch), :]
        index = jnp.concatenate([rows[i : i + 1, :] for i in range(batch)], axis=1)
        of_node = lax.broadcasted_iota(jnp.int32, (width, lane_count), 0) == (index & (width - 1))
        of_block = lax.broadcasted_iota(jnp.int32, (blocks, lane_count), 0) == (index >> shift)
        column = jnp.where(of_node, 1.0, 0.0).astype(BF16)
        leave_node_ref[step, 0:width, :] = column
        leave_node_ref[step, width : 2 * width, :] = column
        leave_block_ref[step] = jnp.where(of_block, 1.0, 0.0)

    def pick(step, source):
        tile = 256 if lane_count % 256 == 0 else lane_count
        splits = [jnp.concatenate(split(source[row]), axis=1) for row in range(3)]
        picked_rows = []
        for start in range(0, lane_count, tile):
            of_block = leave_block_ref[step, :, start : start + tile]
            values = []
            for row in range(3):
                found = jnp.dot(
                    splits[row], leave_node_ref[step, :, start : start + tile], preferred_element_type=F32
                )
                values.append(jnp.sum(of_block * found, axis=0, keepdims=True))
            picked_rows.append(values)
        return [jnp.concatenate([values[row] for values in picked_rows], axis=1) for row in range(3)]

    def gather_places(step):
        values = pick(step, pos_in)
        placed = jnp.concatenate(values + values, axis=0)
        for i in range(batch):
            peer = step * batch + i
            mine = slice(i * capacity, (i + 1) * capacity)
            out_pos[peer + 1, 0:3, 0:capacity] = placed[0:3, mine]
            out_pos[peer + 2, 0:3, capacity : 2 * capacity] = placed[0:3, mine]
            out_pos[peer, 3:6, 0:capacity] = placed[3:6, mine]

    def gather_speeds(step):
        speeds = jnp.concatenate(pick(step, vel_in), axis=0)
        for i in range(batch):
            out_vel[step * batch + i, 0:3, 0:capacity] = speeds[:, i * capacity : (i + 1) * capacity]

    def pos_copy(peer, there, many=1):
        return pltpu.make_async_remote_copy(
            src_ref=out_pos.at[pl.ds(peer, many), pl.ds(0, 6), :],
            dst_ref=in_pos.at[pl.ds(there, many), pl.ds(0, 6), :],
            send_sem=node_send_sem.at[0],
            recv_sem=node_recv_sem.at[0],
            device_id={"wall": neighbour(1)} if many > 1 else {"wall": peer - 1},
            device_id_type=MESH,
        )

    def vel_copy(peer, there, many=1):
        return pltpu.make_async_remote_copy(
            src_ref=out_vel.at[pl.ds(peer, many), pl.ds(0, 3), :],
            dst_ref=in_vel.at[pl.ds(there, many), pl.ds(0, 3), :],
            send_sem=node_send_sem.at[1],
            recv_sem=node_recv_sem.at[1],
            device_id={"wall": neighbour(1)} if many > 1 else {"wall": peer},
            device_id_type=MESH,
        )

    out_pos[...] = jnp.zeros(out_pos.shape, F32)
    def index_batch(step):
        rows = arrive_ref[pl.ds(step * batch, batch), :]
        slot_ids = lax.broadcasted_iota(jnp.int32, (1, capacity), 1)
        index_ref[1, step] = jnp.concatenate(
            [
                jnp.where(slot_ids < count_ref[0, step * batch + i], rows[i : i + 1, :], nodes)
                for i in range(batch)
            ],
            axis=1,
        )

    fetches["send"].wait()
    each_batch(mark_leaving)
    for name in ("arrive", "count"):
        fetches[name].wait()
    each_batch(index_batch)
    fetches["pos"].wait()
    for name in ("weight", "bonds", "mod", "vel"):
        fetches[name].start()
    for row in range(3):
        pos_in[row] = pos_raw[:, row, :]
    each_batch(gather_places)
    in_pos[me, 0:6, :] = out_pos[me + 1, 0:6, :]
    for half in (0, 1):
        for row in range(3):
            put(0, half, row, pos_in[row, own(half), :].astype(BF16))
    pl.semaphore_wait(barrier, peers - 1)
    for half in (0, 1):

        @pl.when(exists(half))
        def _():
            index_copy(half).start()

        @pl.when(jnp.logical_not(exists(half)))
        def _():
            index_ref[2 * half] = jnp.full(index_ref.shape[1:], nodes, jnp.int32)
            for slot in range(slots):
                ext_ref[slot, pl.ds(3 * LAYER * half, LAYER), :] = jnp.zeros((LAYER, 3 * width), BF16)

    for half in (0, 1):
        send(0, half, 0, lanes_of(0, 3))


    def start_places(step, carry):
        pos_copy(lax.rem(me + step, count) + 1, me).start()
        return carry

    lax.fori_loop(1, peers, start_places, 0)

    lanes = lax.broadcasted_iota(jnp.int32, (LAYER, reach), 1)
    fetches["hor"].wait()
    padding = jnp.zeros((-nnz % 8, blocks), jnp.int32)
    horizon = jnp.transpose(jnp.concatenate([hor_ref[...], padding], axis=0))
    for half in range(2):
        local = horizon[half * LAYER : (half + 1) * LAYER] - me * blocks
        local = jnp.where(local < 0, local + reach, local)
        for j in range(nnz):
            hit = local[:, j : j + 1] == lanes
            onehot_ref[half, pl.ds(j * LAYER, LAYER), :] = jnp.where(hit, 1.0, 0.0).astype(BF16)

    fetches["vel"].wait()
    out_vel[...] = jnp.zeros(out_vel.shape, F32)
    for row in range(3):
        vel_in[row] = vel_raw[:, row, :]

    each_batch(gather_speeds)
    in_vel[me, 0:3, :] = out_vel[me, 0:3, :]

    def start_speeds(step, carry):
        vel_copy(lax.rem(me + step, count), me).start()
        return carry

    lax.fori_loop(1, peers, start_speeds, 0)

    for name in ("weight", "bonds", "mod"):
        fetches[name].wait()
    stiff = jnp.zeros((blocks, width), F32)
    ones = jnp.ones((16, width), BF16)
    for j in range(nnz):
        weight = jnp.transpose(weight_ref[j])
        wt_ref[j] = weight
        totals = jnp.dot(ones, weight, preferred_element_type=F32)[0:1, :]
        intact = raw_ref[j].astype(F32)
        intact_ref[j] = intact
        stiff = stiff + intact * totals
    stiff_ref[...] = stiff

    def gain(ref, value):
        ref[...] = value if batches == 1 else ref[...] + value

    def clear(refs):
        if batches > 1:
            for ref in refs:
                ref[...] = jnp.zeros(ref.shape, F32)

    def columns_of(which):
        if isinstance(which, int):
            return pl.ds((0, 2 * width, width)[which], 2 * width if which == 1 else width)
        return pl.ds(pl.multiple_of(lax.div(which, 2) * width, width), width)

    def land(marks, columns, step):
        return lax.dot_general(
            marks, node_ref[step, columns, :], (((1,), (1,)), ((), ())), preferred_element_type=F32
        )

    def mark_batch(step, which_ones):
        for which in which_ones:
            index = index_ref[which, step]
            inside = index & (width - 1)
            block = index >> shift
            if which == 1:
                inside = inside + jnp.where(block >= LAYER, width, 0)
                block = jnp.where(block < 2 * LAYER, block & (LAYER - 1), 2 * LAYER)
            first = LAYER if which == 0 else 0
            columns = columns_of(which)
            of_node = lax.broadcasted_iota(jnp.int32, (columns.size, lane_count), 0) == inside
            node_ref[step, columns, :] = jnp.where(of_node, 1.0, 0.0).astype(BF16)
            of_block = lax.broadcasted_iota(jnp.int32, (LAYER, lane_count), 0) + first == block
            marks = jnp.where(of_block, 1.0, 0.0).astype(BF16)
            rows = pl.ds(which * LAYER, LAYER)
            block_ref[step, rows, :] = marks
            gain(hit_ref.at[:, columns], land(marks, columns, step))

    clear([hit_ref, landed_ref, ghost_landed_ref])
    each_batch(lambda step: mark_batch(step, (1,)))
    for half in (0, 1):

        @pl.when(exists(half))
        def _():
            index_copy(1 - half).wait_recv()

    each_batch(lambda step: mark_batch(step, (0, 2)))

    for half in (0, 1):
        wait_halo(0, half, 0, lanes_of(0, 3))
        wait_sent(0, half, 0, lanes_of(0, 3))

    def places(step):
        bundles = [in_pos[step * batch + i, 0:6, :] for i in range(batch)]
        first = jnp.concatenate([bundle[:, 0:capacity] for bundle in bundles], axis=1)
        left = jnp.concatenate([bundle[0:3, capacity : 2 * capacity] for bundle in bundles], axis=1)
        return first[0:3], left, first[3:6]

    def ghost_rows(half):
        return pl.ds(pl.multiple_of(2 * half * LAYER, LAYER), LAYER)

    def land_ghost(step, half, values):
        rounded = values.astype(BF16)
        for row in range(3):
            ghost_spread_ref[pl.ds(row * LAYER, LAYER), :] = (
                block_ref[step, ghost_rows(half), :] * rounded[row : row + 1, :]
            )
        gain(ghost_landed_ref.at[half], land(ghost_spread_ref[...], columns_of(2 * half), step))

    def keep_ghost(half):
        hit = hit_ref[:, columns_of(2 * half)] > 0.5
        rows = pl.ds(pl.multiple_of(3 * LAYER * half, LAYER), LAYER)
        for row in range(3):
            landed = ghost_landed_ref[half, pl.ds(row * LAYER, LAYER), :]
            held_now = ext_ref[0, rows, lanes_of(row, 1)].astype(F32)
            ext_ref[0, rows, lanes_of(row, 1)] = jnp.where(hit, landed, held_now).astype(BF16)

    def spread(step, section, rounded):
        marks = block_ref[step, pl.ds(LAYER, LAYER), :]
        for row in range(3):
            spread_ref[pl.ds((3 * section + row) * LAYER, LAYER), :] = marks * rounded[row : row + 1, :]

    def land_section(step, section, pieces):
        for first, rows in pieces:
            rows_of = pl.ds((3 * section + first) * LAYER, rows * LAYER)
            gain(landed_ref.at[rows_of], land(spread_ref[rows_of, :], columns_of(1), step))

    def own_columns(half):
        return pl.ds(half * width, width)

    def own_hit(half):
        return hit_ref[:, pl.ds((2 + half) * width, width)] > 0.5

    def land_first(step):
        mine, left, right = places(step)
        spread(step, 0, mine.astype(BF16))
        land_ghost(step, slow, jnp.where(slow == 0, left, right))
        land_section(step, 0, ((0, 3),))

    def land_fast(step):
        _, left, right = places(step)
        land_ghost(step, fast, jnp.where(fast == 0, left, right))

    def land_rest(step):
        mine, _, _ = places(step)
        speeds = jnp.concatenate(
            [in_vel[step * batch + i, 0:3, :][:, 0:capacity] for i in range(batch)], axis=1
        )
        spread(step, 1, split(mine)[1])
        for part, rounded in enumerate(split(speeds)):
            spread(step, 2 + part, rounded)
        for section in (1, 2, 3):
            land_section(step, section, ((0, 3),))

    pos_copy(0, 0, peers - 1).wait_recv()

    @apart
    def _():
        each_batch(land_first)
        keep_ghost(slow)
        for half in (0, 1):
            hit = own_hit(half)
            for row in range(3):
                landed = landed_ref[pl.ds(row * LAYER, LAYER), own_columns(half)]
                put(0, half, row, jnp.where(hit, landed, get(0, half, row)).astype(BF16))

    group = 3 if nnz % 3 == 0 else nnz

    def ghost_of(half):
        return pl.ds(pl.multiple_of(3 * LAYER * half, LAYER), LAYER)

    def pick_blocks(slot, first, rows, half, target):
        columns = lanes_of(first, rows)
        source = jnp.concatenate(
            [ext_ref[slot, pl.ds(LAYER, 2 * LAYER), columns], ext_ref[slot, ghost_of(half), columns]], axis=0
        )
        for begin in range(0, nnz, group):
            part = pl.ds(begin * LAYER, group * LAYER)
            target[part, columns] = jnp.dot(
                onehot_ref[half, part, :], source, preferred_element_type=F32
            ).astype(BF16)

    def pick_own(slot, half, target):
        source = ext_ref[slot, pl.ds(LAYER, 2 * LAYER), lanes_of(0, 1)]
        for begin in range(0, nnz, group):
            part = pl.ds(begin * LAYER, group * LAYER)
            target[part, lanes_of(0, 1)] = jnp.dot(
                onehot_ref[half, part, 0 : 2 * LAYER], source, preferred_element_type=F32
            ).astype(BF16)

    def pick_ghost(slot, half, target):
        source = ext_ref[slot, ghost_of(half), lanes_of(0, 1)]
        for begin in range(0, nnz, group):
            part = pl.ds(begin * LAYER, group * LAYER)
            target[part, lanes_of(0, 1)] = target[part, lanes_of(0, 1)] + jnp.dot(
                onehot_ref[half, part, 2 * LAYER : reach], source, preferred_element_type=F32
            ).astype(BF16)

    def weigh(half, picks):
        sums = [jnp.zeros((LAYER, width), F32) for _ in picks]
        for j in range(nnz):
            part = pl.ds(j * LAYER, LAYER)
            mask = intact_ref[j, own(half), :]
            stacked = jnp.concatenate([one(part) for one in picks], axis=0)
            product = jnp.dot(stacked, wt_ref[j], preferred_element_type=F32)
            for i in range(len(picks)):
                sums[i] = sums[i] + product[i * LAYER : (i + 1) * LAYER] * mask
        return sums

    def placed(half, row):
        return lambda part: picked_ref[half, part, lanes_of(row, 1)]

    def softened(half, row):
        return lambda part: picked_ref[half, part, lanes_of(row, 1)] * soft_picked_ref[part, :]

    def softening(part):
        return soft_picked_ref[part, :]

    def near_parts(parted):
        return ((0, 1), (1, 2)) if parted else ((0, 3),)

    def stretching(t, half, parted, waits):
        near, far = 2 * t, 2 * t + 1
        summed = []
        for part, (first, rows) in enumerate(near_parts(parted and waits)):
            single = waits and rows == 1
            if single:
                pick_own(near, half, picked_ref.at[half])
            if waits:
                wait_halo(near, half, part, lanes_of(first, rows))
            if single:
                pick_ghost(near, half, picked_ref.at[half])
            else:
                pick_blocks(near, first, rows, half, picked_ref.at[half])
            summed += weigh(half, [placed(half, first + row) for row in range(rows)])
        scaling = mod_ref[own(half), :]
        stiffness = stiff_ref[own(half), :]
        rounded = [get(near, half, row) for row in range(3)]
        stretch = [scaling * (summed[row] - stiffness * rounded[row]) for row in range(3)]
        dilatation = (stretch[0] + stretch[1] + stretch[2]) / 3.0
        soften = 1.0 / (1.0 + dilatation * dilatation)
        soft_low = soften.astype(BF16)
        put(far, half, 0, soft_low)
        send(far, half, 0, lanes_of(0, 1))
        for row in range(3):
            stretch_ref[row, own(half), :] = stretch[row]
        soften_ref[own(half), :] = soften

    def pairing(t, half, parted, last):
        near, far = 2 * t, 2 * t + 1
        scaling = mod_ref[own(half), :]
        soften = soften_ref[own(half), :]
        kick = 0.5 * TIME_STEP if last else jnp.where(t == 0, 0.5 * TIME_STEP, TIME_STEP)
        wait_halo(far, half, 0, lanes_of(0, 1))
        pick_blocks(far, 0, 1, half, soft_picked_ref)
        for part, (first, rows) in enumerate(near_parts(parted)):
            picks = [softened(half, first + row) for row in range(rows)]
            if part == 0:
                soft_sum, *paired = weigh(half, [softening] + picks)
            else:
                paired = weigh(half, picks)
            for row in range(first, first + rows):
                rounded = get(near, half, row)
                force = 0.5 * (
                    scaling * (paired[row - first] - rounded * soft_sum) + soften * stretch_ref[row, own(half), :]
                )
                speed = vel_ref[row, own(half), :] + kick * force
                if last:
                    vel_out[own(half), row, :] = speed
                else:
                    vel_ref[row, own(half), :] = speed
                    moved = pos_ref[row, own(half), :] + TIME_STEP * speed
                    pos_ref[row, own(half), :] = moved
                    put(near + 2, half, row, moved.astype(BF16))
            if not last:
                send(near + 2, half, part, lanes_of(first, rows))

    stretching(0, slow, True, False)

    @apart
    def _():
        each_batch(land_fast)
        keep_ghost(fast)

    stretching(0, fast, False, False)

    vel_copy(0, 0, peers - 1).wait_recv()
    each_batch(land_rest)
    for half in (0, 1):
        hit = own_hit(half)
        for row in range(3):
            parts = [
                landed_ref[pl.ds((3 * section + row) * LAYER, LAYER), own_columns(half)] for section in range(4)
            ]
            pos_ref[row, own(half), :] = jnp.where(hit, parts[0] + parts[1], pos_in[row, own(half), :])
            vel_ref[row, own(half), :] = jnp.where(hit, parts[2] + parts[3], vel_in[row, own(half), :])

    def substep(t, carry):
        pairing(t, fast, False, False)
        pairing(t, slow, True, False)
        stretching(t + 1, fast, False, True)
        stretching(t + 1, slow, True, True)
        return carry

    lax.fori_loop(0, SUBSTEPS, substep, 0)

    for row in range(3):
        pos_out[:, row, :] = pos_ref[row]
    pairing(SUBSTEPS, fast, False, True)
    pairing(SUBSTEPS, slow, False, True)

    pos_copy(0, 0, peers - 1).wait_send()
    vel_copy(0, 0, peers - 1).wait_send()
    for half in (0, 1):

        @pl.when(exists(half))
        def _():
            index_copy(half).wait_send()

    for slot in range(1, slots):
        for half, parted in ((fast, False), (slow, True)):
            parts = ((0, 1),) if slot % 2 else near_parts(parted)
            for part, (first, rows) in enumerate(parts):
                wait_sent(slot, half, part, lanes_of(first, rows))


def store_kernel(pos_in, vel_in, pos_out, vel_out, sems):
    copies = [
        pltpu.make_async_copy(pos_in, pos_out, sems.at[0]),
        pltpu.make_async_copy(vel_in, vel_out, sems.at[1]),
    ]
    for copy in copies:
        copy.start()
    for copy in copies:
        copy.wait()


def shards(
    displacement,
    velocity,
    send_list,
    arrive_list,
    recv_count,
    horizon_blocks,
    bond_intact,
    modulus,
    bond_weight,
):
    node_count = displacement.shape[1]
    blocks, nnz, width = bond_intact.shape
    peers, capacity = send_list.shape[1:]
    lane_count = math.gcd(PEER_BATCH, peers) * capacity
    batches = peers * capacity // lane_count
    bundle_width = 128 * pl.cdiv(2 * capacity, 128)
    slots = 2 * (SUBSTEPS + 1)
    vmem = pl.BlockSpec(memory_space=pltpu.VMEM)
    hbm = pl.BlockSpec(memory_space=pltpu.HBM)
    shape = jax.ShapeDtypeStruct((blocks, 3, width), F32)
    spare = VMEM_LIMIT - 2 * 4 * blocks * 4 * width
    final_position, final_speed = pl.pallas_call(
        functools.partial(force_kernel, blocks, width, nnz, peers),
        out_shape=(pltpu.VMEM(shape.shape, F32), pltpu.VMEM(shape.shape, F32)),
        in_specs=[hbm] * 9,
        out_specs=(vmem, vmem),
        scratch_shapes=[
            pltpu.VMEM((peers, capacity), jnp.int32),
            pltpu.VMEM((peers, capacity), jnp.int32),
            pltpu.SMEM((1, peers), jnp.int32),
            pltpu.VMEM((nnz, blocks), jnp.int32),
            pltpu.VMEM((blocks, width), F32),
            pltpu.VMEM((nnz, width, width), BF16),
            pltpu.VMEM((blocks, 3, width), F32),
            pltpu.VMEM((blocks, 3, width), F32),
            pltpu.VMEM((3, blocks, width), F32),
            pltpu.VMEM((3, blocks, width), F32),
            pltpu.VMEM((peers + 2, 8, bundle_width), F32),
            pltpu.VMEM((peers, 8, bundle_width), F32),
            pltpu.VMEM((peers, 8, bundle_width), F32),
            pltpu.VMEM((peers, 8, bundle_width), F32),
            pltpu.VMEM((batches, 2 * width, lane_count), BF16),
            pltpu.VMEM((batches, blocks, lane_count), F32),
            pltpu.VMEM((3, batches, 1, lane_count), jnp.int32),
            pltpu.VMEM((batches, 4 * width, lane_count), BF16),
            pltpu.VMEM((batches, 3 * LAYER, lane_count), BF16),
            pltpu.VMEM((LAYER, 4 * width), F32),
            pltpu.VMEM((12 * LAYER, lane_count), BF16),
            pltpu.VMEM((12 * LAYER, 2 * width), F32),
            pltpu.VMEM((3 * LAYER, lane_count), BF16),
            pltpu.VMEM((2, 3 * LAYER, width), F32),
            pltpu.VMEM((nnz, blocks, width), jnp.int32),
            pltpu.VMEM((nnz, blocks, width), F32),
            pltpu.VMEM((nnz, width, width), BF16),
            pltpu.VMEM((2, nnz * LAYER, 3 * LAYER), BF16),
            pltpu.VMEM((slots, 4 * LAYER, 3 * width), BF16),
            pltpu.VMEM((2, nnz * LAYER, 3 * width), BF16),
            pltpu.VMEM((nnz * LAYER, width), BF16),
            pltpu.VMEM((blocks, width), F32),
            pltpu.VMEM((3, blocks, width), F32),
            pltpu.VMEM((blocks, width), F32),
            pltpu.VMEM((3, blocks, width), F32),
            pltpu.VMEM((3, blocks, width), F32),
            pltpu.SemaphoreType.DMA((slots, 2, 2)),
            pltpu.SemaphoreType.DMA((slots, 2, 2)),
            pltpu.SemaphoreType.DMA((2,)),
            pltpu.SemaphoreType.DMA((2,)),
            pltpu.SemaphoreType.DMA((2,)),
            pltpu.SemaphoreType.DMA((2,)),
            pltpu.SemaphoreType.DMA((9,)),
        ],
        compiler_params=pltpu.CompilerParams(
            collective_id=0, has_side_effects=True, vmem_limit_bytes=spare
        ),
        name="forces",
    )(
        send_list,
        arrive_list,
        recv_count,
        jnp.transpose(horizon_blocks),
        jnp.transpose(bond_intact, (1, 0, 2)),
        modulus.reshape(blocks, width),
        bond_weight,
        jnp.transpose(displacement.reshape(3, blocks, width), (1, 0, 2)),
        jnp.transpose(velocity.reshape(3, blocks, width), (1, 0, 2)),
    )
    final_position, final_speed = pl.pallas_call(
        store_kernel,
        out_shape=(shape, shape),
        in_specs=[pl.BlockSpec(memory_space=pl.ANY)] * 2,
        out_specs=(hbm, hbm),
        scratch_shapes=[pltpu.SemaphoreType.DMA((2,))],
        compiler_params=pltpu.CompilerParams(vmem_limit_bytes=1048576),
        name="store",
    )(final_position, final_speed)
    return tuple(jnp.transpose(x, (1, 0, 2)).reshape(3, node_count) for x in (final_position, final_speed))


def solution(mesh):
    in_specs = (
        P(None, ("parts", "wall")),
        P(None, ("parts", "wall")),
        P(("parts", "wall"), None, None),
        P(("parts", "wall"), None, None),
        P(("parts", "wall"), None),
        P(("parts", "wall"), None),
        P(("parts", "wall"), None, None),
        P(("parts", "wall")),
        P(),
    )
    out_specs = (P(None, ("parts", "wall")), P(None, ("parts", "wall")))
    return jax.shard_map(shards, mesh=mesh, in_specs=in_specs, out_specs=out_specs, check_vma=False)
```
